32 devices in a mesh: grp: 2 (over y), ctx: 16 (over z, x, core).
Axes of the slice: x: 2, y: 2, z: 4, core: 2. Of those that a mesh axis runs over, the one named last changes fastest.
Arguments:
- query_main: bfloat16 [64, 128, 576], P(('grp', 'ctx')), parts along dimension 0, may hold values from -3 to 3
- key_codes: bfloat16 [4096, 576], P(('grp', 'ctx')), parts along dimension 0, may hold values from -4 to 4
- key_scales: int32 [4096, 4], P(('grp', 'ctx')), parts along dimension 0, may hold values from -2 to 2
- index_keys: bfloat16 [4096, 128], P(('grp', 'ctx')), parts along dimension 0, may hold values from -5 to 5
- index_query: bfloat16 [64, 64, 128], P(('grp', 'ctx')), parts along dimension 0, may hold values from -7 to 7
- index_weight: float32 [64, 64], P(('grp', 'ctx')), parts along dimension 0, may hold values from -4 to 4
- query_pos: int32 [64], P(('grp', 'ctx')), parts along dimension 0, may hold values from 1024 to 2047
Outputs:
- grad_index_query: float32 [64, 64, 128], P(('grp', 'ctx')), parts along dimension 0
- grad_index_weight: float32 [64, 64], P(('grp', 'ctx')), parts along dimension 0
- grad_index_keys: float32 [4096, 128], P(('grp', 'ctx')), parts along dimension 0
The draws below stay inside these ranges and needn't reach their ends.
There are 2 independent parts, one for each index of `grp`. The reference program is written for one: setup_inputs(seed, part) draws one part's arguments, and reference() takes and returns one part's arrays. A program takes and returns all parts, laid end to end along the dimension named above; each array names one. Nothing has to cross between parts.
All inputs are finite; a program needn't handle non-finite values.
Results may differ from the reference program's by a relative error of at most 0.005.
Values may be sent and summed in bfloat16 or wider, within the bound.
No kernel may reach another device: no remote copies, remote signals or barrier semaphores. Data moves between devices by JAX's collectives and lax.ppermute only.
A program may use at most 192 MiB of HBM per device.

```python
import jax
import jax.numpy as jnp
from jax import lax

H = 128
LAT = 576
ROPE = 64
IH = 64
ID = 128
Q_DEV = 2
GROUPS = 4
Q = 32
S = 2048


def plant(result, stream_key, low, largest):
    extent = result.shape
    spot = [jax.random.randint(jax.random.fold_in(stream_key, axis), (), 0, extent[axis]) for axis in range(len(extent))]
    result = result.at[tuple(spot)].set(low)
    longest = extent.index(max(extent))
    spot[longest] = (spot[longest] + 1) % extent[longest]
    return result.at[tuple(spot)].set(largest)


def steps_of(rng, extent, split, least, top_value):
    level, own = 1.0, jax.random.fold_in(rng, 6)
    for axis_at, shards_of in split:
        draws = jnp.exp(jax.random.uniform(jax.random.fold_in(own, axis_at), (shards_of,), jnp.float32, least / len(split), top_value / len(split)))
        level = level * jnp.repeat(draws, extent[axis_at] // shards_of).reshape([-1 if axis == axis_at else 1 for axis in range(len(extent))])
    return level


def noise(key, shape, deviation, limit, split=(), kind=jnp.bfloat16):
    factor_of = steps_of(key, shape, split, -0.22, 0.18) if split else 1.0
    drawn = jax.random.normal(key, shape, jnp.float32) * deviation * factor_of
    return jnp.minimum(jnp.maximum(drawn, -limit), limit).astype(kind)


def setup_inputs(seed: int = 0, part: int = 0) -> dict:
    key_of = jax.random.split(jax.random.key(seed), 8)
    part_keys = jax.random.split(jax.random.fold_in(key_of[7], part), 8)
    return {
        "query_main": noise(part_keys[0], (Q, H, LAT), 0.5, 3.0, ((0, 16),)),
        "key_codes": noise(part_keys[1], (S, LAT), 1.0, 4.0, ((0, 16),)),
        "key_scales": plant(jax.random.randint(part_keys[2], (S, GROUPS), -2, 3), jax.random.fold_in(part_keys[2], 1), -2, 2).astype(jnp.int32),
        "index_keys": noise(part_keys[3], (S, ID), 1.0, 5.0, ((0, 16),)),
        "index_query": noise(part_keys[4], (Q, IH, ID), 1.5, 7.0, ((0, 16),)),
        "index_weight": noise(part_keys[5], (Q, IH), 1.0, 4.0, ((0, 16),), jnp.float32),
        "query_pos": plant(jax.random.randint(part_keys[6], (Q,), S // 2, S), jax.random.fold_in(part_keys[6], 1), S // 2, S - 1).astype(jnp.int32),
    }


main_scale = 192.0 ** -0.5


def dot_rows(left, right):
    return lax.dot_general(left, right, (((1,), (1,)), ((), ())), preferred_element_type=jnp.float32)


def dequantize(key_codes, factors):
    key_count = key_codes.shape[0]
    group_width = (key_codes.shape[1] - ROPE) // GROUPS
    scaled = key_codes[:, :GROUPS * group_width].astype(jnp.float32).reshape(key_count, GROUPS, group_width) * factors[:, :, None]
    rotary = key_codes[:, GROUPS * group_width:].astype(jnp.float32)
    return jnp.concatenate([scaled.reshape(key_count, -1), rotary], axis=1).astype(jnp.bfloat16)


def reference(query_main, key_codes, key_scales, index_keys, index_query, index_weight, query_pos):
    factors = jnp.exp2(key_scales.astype(jnp.float32))
    latent = dequantize(key_codes, factors)
    index_scale = float(IH * ID) ** -0.5
    key_pos = jnp.arange(S, dtype=jnp.int32)

    def one_block(key_grad, inputs):
        query_block, iquery_block, weight_block, pos_block = inputs
        row_count = query_block.shape[0]
        main_score = dot_rows(query_block.reshape(row_count * H, -1), latent).reshape(row_count, H, S) * main_scale
        visible = key_pos[None, :] <= pos_block[:, None]
        main_exp = jnp.where(visible[:, None, :], jnp.exp(main_score), 0.0)
        main_prob = main_exp / jnp.sum(main_exp, axis=2, keepdims=True)
        target = jnp.sum(main_prob, axis=1) / H
        query_flat = iquery_block.reshape(row_count * IH, ID)
        head_dots = dot_rows(query_flat, index_keys).reshape(row_count, IH, S)
        index_score = index_scale * jnp.sum(weight_block[:, :, None] * jnp.maximum(head_dots, 0.0), axis=1)
        index_exp = jnp.where(visible, jnp.exp(index_score), 0.0)
        index_prob = index_exp / jnp.sum(index_exp, axis=1, keepdims=True)
        gradient = S * (index_prob - target)
        grad_weight = index_scale * jnp.sum(gradient[:, None, :] * jnp.maximum(head_dots, 0.0), axis=2)
        grad_dots = jnp.where(head_dots > 0, index_scale * gradient[:, None, :] * weight_block[:, :, None], 0.0)
        grad_dots = grad_dots.astype(jnp.bfloat16).reshape(row_count * IH, S)
        grad_query = jnp.dot(grad_dots, index_keys, preferred_element_type=jnp.float32).reshape(row_count, IH, ID)
        key_grad = key_grad + lax.dot_general(grad_dots, query_flat, (((0,), (0,)), ((), ())), preferred_element_type=jnp.float32)
        return key_grad, (grad_query, grad_weight)

    blocks = Q // Q_DEV
    inputs = (query_main.reshape(blocks, Q_DEV, H, LAT), index_query.reshape(blocks, Q_DEV, IH, ID),
              index_weight.reshape(blocks, Q_DEV, IH), query_pos.reshape(blocks, Q_DEV))
    key_grad, outputs = lax.scan(one_block, jnp.zeros((S, ID), jnp.float32), inputs)
    grad_query, grad_weight = outputs
    return grad_query.reshape(Q, IH, ID), grad_weight.reshape(Q, IH), key_grad
```

```python
import jax
import jax.numpy as jnp
from jax import lax
from jax.sharding import PartitionSpec as P

ROPE = 64


main_scale = 192.0 ** (-0.5)


def dot_rows(left, right):
    return lax.dot_general(
        left, right, (((1,), (1,)), ((), ())), preferred_element_type=jnp.float32
    )


def dequantize(key_codes, key_scales):
    key_count = key_codes.shape[0]
    groups = key_scales.shape[1]
    group_width = (key_codes.shape[1] - ROPE) // groups
    factors = jnp.exp2(key_scales.astype(jnp.float32))
    scaled = key_codes[:, : groups * group_width].astype(jnp.float32)
    scaled = scaled.reshape(key_count, groups, group_width) * factors[:, :, None]
    rotary = key_codes[:, groups * group_width :].astype(jnp.float32)
    return jnp.concatenate([scaled.reshape(key_count, -1), rotary], axis=1).astype(jnp.bfloat16)


def swap(array, mask, count):
    return lax.ppermute(array, "ctx", [(i, i ^ mask) for i in range(count)])


def swap_gather(block, stride, parts, count):
    held = {0: block}
    bit = parts // 2
    while bit:
        held.update({k ^ bit: swap(own, stride * bit, count) for k, own in list(held.items())})
        bit //= 2
    return [held[k] for k in range(parts)]


def body(query_main, key_codes, key_scales, index_keys, index_query, index_weight, query_pos):
    own_rows, head_count, latent_width = query_main.shape
    index_heads, index_width = index_query.shape[1:]
    own_keys = key_codes.shape[0]
    count = lax.axis_size("ctx")
    row_parts = 4 if count % 4 == 0 else 1
    key_parts = count // row_parts
    me = lax.axis_index("ctx")
    key_total = own_keys * count
    index_scale = float(index_heads * index_width) ** (-0.5)
    rows = own_rows * row_parts
    keys = own_keys * key_parts

    latent = dequantize(key_codes, key_scales)
    key_pack = jnp.concatenate([latent, index_keys], axis=1)
    side = jnp.concatenate([index_weight, query_pos.astype(jnp.float32)[:, None]], axis=1)
    key_blocks = swap_gather(key_pack, row_parts, key_parts, count)
    query_blocks = swap_gather(query_main, 1, row_parts, count)
    iquery_blocks = swap_gather(index_query, 1, row_parts, count)
    side_blocks = swap_gather(side, 1, row_parts, count)

    key_all = jnp.concatenate(key_blocks, axis=0)
    latent_all = key_all[:, :latent_width]
    ikeys = key_all[:, latent_width:]
    main_flat = jnp.concatenate(query_blocks, axis=0).reshape(rows * head_count, latent_width)
    query_flat = jnp.concatenate(iquery_blocks, axis=0).reshape(rows * index_heads, index_width)
    side_all = jnp.concatenate(side_blocks, axis=0)
    weight = side_all[:, :index_heads]
    pos = side_all[:, index_heads].astype(jnp.int32)
    owners = jnp.stack([me ^ (row_parts * k) for k in range(key_parts)])
    key_pos = (owners[:, None] * own_keys + lax.iota(jnp.int32, own_keys)[None, :]).reshape(-1)
    visible = key_pos[None, :] <= pos[:, None]

    main_score = dot_rows(main_flat, latent_all).reshape(rows, head_count, keys) * main_scale
    main_exp = jnp.where(visible[:, None, :], jnp.exp(main_score), 0.0)
    head_dots = dot_rows(query_flat, ikeys).reshape(rows, index_heads, keys)
    positive = jnp.maximum(head_dots, 0.0)
    index_score = index_scale * jnp.sum(weight[:, :, None] * positive, axis=1)
    index_exp = jnp.where(visible, jnp.exp(index_score), 0.0)
    sums = jnp.concatenate(
        [jnp.sum(main_exp, axis=2), jnp.sum(index_exp, axis=1, keepdims=True)], axis=1
    )
    sums = sums.reshape(row_parts, own_rows, -1)
    bit = row_parts // 2
    while bit:
        got = swap(sums, bit, count)
        sums = sums + jnp.stack([got[r ^ bit] for r in range(row_parts)])
        bit //= 2
    sums = sums.reshape(rows, -1)
    main_total, index_total = sums[:, :head_count], sums[:, head_count:]

    target = jnp.sum(main_exp / main_total[:, :, None], axis=1) / head_count
    gradient = key_total * (index_exp / index_total - target)
    grad_weight = index_scale * jnp.sum(gradient[:, None, :] * positive, axis=2)
    grad_dots = jnp.where(
        head_dots > 0, index_scale * gradient[:, None, :] * weight[:, :, None], 0.0
    )
    grad_dots = grad_dots.astype(jnp.bfloat16).reshape(rows * index_heads, keys)
    key_part = lax.dot_general(
        grad_dots, query_flat, (((0,), (0,)), ((), ())), preferred_element_type=jnp.float32
    )
    key_part = key_part.reshape(key_parts, own_keys, index_width)
    got_keys = [
        swap(key_part[k].astype(jnp.bfloat16), row_parts * k, count) for k in range(1, key_parts)
    ]
    grad_query = jnp.dot(grad_dots, ikeys, preferred_element_type=jnp.float32)
    lines = own_rows * index_heads
    grad_rows = jnp.concatenate(
        [
            grad_query.reshape(row_parts, lines, index_width),
            grad_weight.reshape(row_parts, -1, index_width),
        ],
        axis=1,
    )
    bit = row_parts // 2
    while bit:
        grad_rows = grad_rows[:bit] + swap(grad_rows[bit:], bit, count)
        bit //= 2
    grad_rows = grad_rows[0]
    key_grad = key_part[0]
    for got in got_keys:
        key_grad = key_grad + got.astype(jnp.float32)
    return (
        grad_rows[:lines].reshape(own_rows, index_heads, index_width),
        grad_rows[lines:].reshape(own_rows, index_heads),
        key_grad,
    )


def solution(mesh):
    placed = (
        P(("grp", "ctx"), None, None),
        P(("grp", "ctx"), None),
        P(("grp", "ctx"), None),
        P(("grp", "ctx"), None),
        P(("grp", "ctx"), None, None),
        P(("grp", "ctx"), None),
        P(("grp", "ctx")),
    )
    return jax.shard_map(
        body,
        mesh=mesh,
        in_specs=placed,
        out_specs=(P(("grp", "ctx"), None, None), P(("grp", "ctx"), None), P(("grp", "ctx"), None)),
        check_vma=False,
    )
```

```python
import jax
import jax.numpy as jnp
from jax import lax
from jax.experimental import pallas as pl
from jax.experimental.pallas import tpu as pltpu
from jax.sharding import PartitionSpec as P

ROPE = 64


main_scale = 192.0 ** (-0.5)


def dot_rows(left, right):
    return lax.dot_general(
        left, right, (((1,), (1,)), ((), ())), preferred_element_type=jnp.float32
    )


def pack_kernel(codes_ref, scales_ref, keys_ref, out_ref):
    groups = scales_ref.shape[0]
    latent_width = codes_ref.shape[0]
    group_width = (latent_width - ROPE) // groups
    factors = jnp.exp2(scales_ref[...].astype(jnp.float32))
    for g in range(groups):
        lines = slice(g * group_width, (g + 1) * group_width)
        scaled = codes_ref[lines, :].astype(jnp.float32) * factors[g : g + 1, :]
        out_ref[lines, :] = scaled.astype(jnp.bfloat16)
    out_ref[groups * group_width : latent_width, :] = codes_ref[groups * group_width :, :]
    out_ref[latent_width:, :] = keys_ref[...]


def pack_keys(codes, scales, index_keys):
    lines = codes.shape[0] + index_keys.shape[0]
    return pl.pallas_call(
        pack_kernel,
        out_shape=jax.ShapeDtypeStruct((lines, codes.shape[1]), jnp.bfloat16),
        name="pack_keys",
    )(codes, scales, index_keys)


def swap(array, mask, count):
    return lax.ppermute(array, "ctx", [(i, i ^ mask) for i in range(count)])


def swap_gather(block, stride, parts, count):
    held = {0: block}
    bit = parts // 2
    while bit:
        held.update({k ^ bit: swap(own, stride * bit, count) for k, own in list(held.items())})
        bit //= 2
    return [held[k] for k in range(parts)]


def body(query_main, key_codes, key_scales, index_keys, index_query, index_weight, query_pos):
    own_rows, head_count, latent_width = query_main.shape
    index_heads, index_width = index_query.shape[1:]
    own_keys = key_codes.shape[0]
    count = lax.axis_size("ctx")
    row_parts = 4 if count % 4 == 0 else 1
    key_parts = count // row_parts
    me = lax.axis_index("ctx")
    key_total = own_keys * count
    index_scale = float(index_heads * index_width) ** (-0.5)
    rows = own_rows * row_parts
    keys = own_keys * key_parts

    key_pack = pack_keys(key_codes.T, key_scales.T, index_keys)
    key_pack, query_main, index_query, index_weight, query_pos = lax.optimization_barrier(
        (key_pack, query_main, index_query, index_weight, query_pos)
    )
    key_blocks = swap_gather(key_pack, row_parts, key_parts, count)
    side = jnp.concatenate([index_weight, query_pos.astype(jnp.float32)[:, None]], axis=1)
    query_blocks = swap_gather(query_main, 1, row_parts, count)
    iquery_blocks = swap_gather(index_query, 1, row_parts, count)
    side_blocks = swap_gather(side, 1, row_parts, count)

    latent_all = jnp.concatenate([b[:latent_width] for b in key_blocks], axis=1)
    ikeys = jnp.concatenate([b[latent_width:] for b in key_blocks], axis=0)
    main_flat = jnp.concatenate(query_blocks, axis=0).reshape(rows * head_count, latent_width)
    query_flat = jnp.concatenate(iquery_blocks, axis=0).reshape(rows * index_heads, index_width)
    side_all = jnp.concatenate(side_blocks, axis=0)
    weight = side_all[:, :index_heads]
    pos = side_all[:, index_heads].astype(jnp.int32)
    owners = jnp.stack([me ^ (row_parts * k) for k in range(key_parts)])
    key_pos = (owners[:, None] * own_keys + lax.iota(jnp.int32, own_keys)[None, :]).reshape(-1)
    visible = key_pos[None, :] <= pos[:, None]

    main_score = jnp.dot(main_flat, latent_all, preferred_element_type=jnp.float32).reshape(rows, head_count, keys) * main_scale
    main_exp = jnp.where(visible[:, None, :], jnp.exp(main_score), 0.0)
    head_dots = dot_rows(query_flat, ikeys).reshape(rows, index_heads, keys)
    positive = jnp.maximum(head_dots, 0.0)
    index_score = index_scale * jnp.sum(weight[:, :, None] * positive, axis=1)
    index_exp = jnp.where(visible, jnp.exp(index_score), 0.0)
    sums = jnp.concatenate(
        [jnp.sum(main_exp, axis=2), jnp.sum(index_exp, axis=1, keepdims=True)], axis=1
    )
    sums = sums.reshape(row_parts, own_rows, -1)
    bit = row_parts // 2
    while bit:
        got = swap(sums, bit, count)
        sums = sums + jnp.stack([got[r ^ bit] for r in range(row_parts)])
        bit //= 2
    sums = sums.reshape(rows, -1)
    main_total, index_total = sums[:, :head_count], sums[:, head_count:]

    target = jnp.sum(main_exp / main_total[:, :, None], axis=1) / head_count
    gradient = key_total * (index_exp / index_total - target)
    grad_weight = index_scale * jnp.sum(gradient[:, None, :] * positive, axis=2)
    grad_dots = jnp.where(
        head_dots > 0, index_scale * gradient[:, None, :] * weight[:, :, None], 0.0
    )
    grad_dots = grad_dots.astype(jnp.bfloat16).reshape(rows * index_heads, keys)
    key_part = lax.dot_general(
        grad_dots, query_flat, (((0,), (0,)), ((), ())), preferred_element_type=jnp.float32
    )
    key_part = key_part.reshape(key_parts, own_keys, index_width)
    halves = key_part[key_parts // 2 :].astype(jnp.bfloat16)
    key_sum = key_part[: key_parts // 2]
    bit = key_parts // 2
    while bit:
        key_sum = key_sum + swap(halves, row_parts * bit, count).astype(jnp.float32)
        bit //= 2
        if bit:
            halves = key_sum[bit:].astype(jnp.bfloat16)
            key_sum = key_sum[:bit]
    key_grad = key_sum[0]
    grad_query = jnp.dot(grad_dots, ikeys, preferred_element_type=jnp.float32)
    lines = own_rows * index_heads
    grad_rows = jnp.concatenate(
        [
            grad_query.reshape(row_parts, lines, index_width),
            grad_weight.reshape(row_parts, -1, index_width),
        ],
        axis=1,
    )
    bit = row_parts // 2
    while bit:
        grad_rows = grad_rows[:bit] + swap(grad_rows[bit:], bit, count)
        bit //= 2
    grad_rows = grad_rows[0]
    return (
        grad_rows[:lines].reshape(own_rows, index_heads, index_width),
        grad_rows[lines:].reshape(own_rows, index_heads),
        key_grad,
    )


def solution(mesh):
    placed = (
        P(("grp", "ctx"), None, None),
        P(("grp", "ctx"), None),
        P(("grp", "ctx"), None),
        P(("grp", "ctx"), None),
        P(("grp", "ctx"), None, None),
        P(("grp", "ctx"), None),
        P(("grp", "ctx")),
    )
    return jax.shard_map(
        body,
        mesh=mesh,
        in_specs=placed,
        out_specs=(P(("grp", "ctx"), None, None), P(("grp", "ctx"), None), P(("grp", "ctx"), None)),
        check_vma=False,
    )
```

```python
import functools

import jax
import jax.numpy as jnp
from jax import lax
from jax.experimental import pallas as pl
from jax.experimental.pallas import tpu as pltpu
from jax.sharding import PartitionSpec as P


ROPE = 64
LANES = 128

f32, bf16 = jnp.float32, jnp.bfloat16
main_scale = 192.0 ** (-0.5)


def kernel_call(kernel, shapes, operands, scratch=(), flops=0):
    nbytes = sum(x.size * x.dtype.itemsize for x in (*operands, *shapes))
    return pl.pallas_call(
        kernel,
        out_shape=tuple(shapes),
        scratch_shapes=list(scratch),
        compiler_params=pltpu.CompilerParams(vmem_limit_bytes=24 << 20),
        cost_estimate=pl.CostEstimate(flops=flops, bytes_accessed=nbytes, transcendentals=0),
    )(*operands)


def contract(left, right, dims):
    return lax.dot_general(left, right, ((dims[:1], dims[1:]), ((), ())), preferred_element_type=f32)


def swap(array, mask, count):
    return lax.ppermute(array, "ctx", [(i, i ^ mask) for i in range(count)])


def swap_gather(block, stride, parts, count):
    held = {0: block}
    bit = parts // 2
    while bit:
        for k, own in list(held.items()):
            held[k ^ bit] = swap(own, stride * bit, count)
        bit //= 2
    return [held[k] for k in range(parts)]


def pack_kernel(
    codes_hbm, scales_hbm, keys_hbm, weight_hbm, pos_hbm, out_ref, side_ref, codes_ref, scales_ref,
    weight_ref, pos_ref, sems
):
    groups, own_keys = scales_hbm.shape
    latent_width = codes_hbm.shape[0]
    group_width = (latent_width - ROPE) // groups
    keys_copy = pltpu.make_async_copy(
        keys_hbm, out_ref.at[pl.ds(latent_width, own_keys), :], sems.at[0]
    )
    scales_copy = pltpu.make_async_copy(scales_hbm, scales_ref, sems.at[1])
    weight_copy = pltpu.make_async_copy(weight_hbm, weight_ref, sems.at[2])
    codes_copy = pltpu.make_async_copy(codes_hbm, codes_ref, sems.at[3])
    pos_copy = pltpu.make_async_copy(pos_hbm, pos_ref, sems.at[4])
    for copy in (scales_copy, codes_copy, weight_copy, pos_copy, keys_copy):
        copy.start()
    scales_copy.wait()
    factors = jnp.exp2(scales_ref[...].astype(f32))
    codes_copy.wait()
    for g in range(groups):
        lines = slice(g * group_width, (g + 1) * group_width)
        scaled = codes_ref[lines, :].astype(f32) * factors[g : g + 1, :]
        out_ref[lines, :] = scaled.astype(bf16)
    out_ref[groups * group_width : latent_width, :] = codes_ref[groups * group_width :, :]
    weight_copy.wait()
    pos_copy.wait()
    own_rows, index_heads = weight_ref.shape
    lane = lax.broadcasted_iota(jnp.int32, (1, LANES), 1)
    for i in range(own_rows):
        at = jnp.full((1, LANES), pos_ref[i], jnp.int32).astype(f32)
        side_ref[i : i + 1, :] = jnp.where(lane == index_heads, at, 0.0)
        side_ref[i : i + 1, :index_heads] = weight_ref[i : i + 1, :]
    keys_copy.wait()


def score_kernel(offsets, row_parts, *refs):
    parts = len(offsets)
    sides, queries, iqueries = (refs[n * row_parts : (n + 1) * row_parts] for n in range(3))
    blocks = refs[3 * row_parts : 3 * row_parts + parts]
    exp_ref, index_ref, sums_ref = refs[3 * row_parts + parts :]
    own_rows, latent_width, head_count = queries[0].shape
    index_heads, index_width = iqueries[0].shape[1:]
    own_keys = blocks[0].shape[1]
    index_scale = float(index_heads * index_width) ** (-0.5)
    me = lax.axis_index("ctx")
    iota = lax.broadcasted_iota(jnp.int32, (1, own_keys), 1)
    key_pos = [((me ^ (row_parts * k)) * own_keys + iota).astype(f32) for k in offsets]
    key_pos = jnp.concatenate(key_pos, axis=1)
    latent = jnp.concatenate([b[:latent_width, :] for b in blocks], axis=1)
    ikeys = jnp.concatenate([b[latent_width:, :] for b in blocks], axis=0)
    sums_ref[...] = jnp.zeros_like(sums_ref)
    for r in range(row_parts):
        for i in range(own_rows):
            t = r * own_rows + i
            pos = sides[r][i : i + 1, index_heads : index_heads + 1]
            visible = key_pos <= pos
            weight = jnp.transpose(jnp.broadcast_to(sides[r][i : i + 1, :], (LANES, LANES)))
            weight = weight[:index_heads, :1]
            dots = contract(iqueries[r][i], ikeys, (1, 1))
            score = jnp.sum(weight * jnp.maximum(dots, 0.0), axis=0, keepdims=True)
            index_exp = jnp.where(visible, jnp.exp(index_scale * score), 0.0)
            index_ref[t : t + 1, :] = index_exp
            score = contract(jnp.transpose(queries[r][i]), latent, (1, 0)) * main_scale
            main_exp = jnp.where(visible, jnp.exp(score), 0.0)
            exp_ref[t] = main_exp
            total = main_exp[:, :own_keys]
            index_total = index_exp[:, :own_keys]
            for k in range(1, parts):
                lines = slice(k * own_keys, (k + 1) * own_keys)
                total = total + main_exp[:, lines]
                index_total = index_total + index_exp[:, lines]
            total = jnp.sum(jnp.transpose(total), axis=0, keepdims=True)
            sums_ref[r, i : i + 1, :] = total
            index_total = jnp.sum(index_total, axis=1, keepdims=True)
            sums_ref[r, own_rows + i : own_rows + i + 1, :] = jnp.broadcast_to(
                index_total, (1, head_count)
            )


def grad_kernel(key_total, row_parts, sizes, *refs):
    near_ref, far_ref = refs[:2]
    sides, iqueries = refs[2 : 2 + row_parts], refs[2 + row_parts : 2 + 2 * row_parts]
    refs = refs[2 + 2 * row_parts :]
    exps, indexes = refs[: len(sizes)], refs[len(sizes) : 2 * len(sizes)]
    refs = refs[2 * len(sizes) :]
    blocks = refs[: sum(sizes)]
    even_ref, odd_ref, keep_ref, send_ref, dots_ref, flat_ref = refs[sum(sizes) :]
    own_rows, index_heads, index_width = iqueries[0].shape
    head_count, own_keys = exps[0].shape[1], blocks[0].shape[1]
    latent_width = blocks[0].shape[0] - index_width
    index_scale = float(index_heads * index_width) ** (-0.5)
    ikeys = jnp.concatenate([b[latent_width:, :] for b in blocks], axis=0)
    lane = lax.broadcasted_iota(jnp.int32, (index_heads, LANES), 1)
    lines = own_rows * index_heads
    columns = jnp.zeros((index_heads, LANES), f32)
    for r in range(row_parts):
        for i in range(own_rows):
            t = r * own_rows + i
            total = near_ref[r, i : i + 1, :] + far_ref[r ^ 1, i : i + 1, :]
            share = jnp.transpose(jnp.broadcast_to(1.0 / total, (LANES, head_count)))
            share = share[:, :1]
            index_total = (
                near_ref[r, own_rows + i : own_rows + i + 1, :1]
                + far_ref[r ^ 1, own_rows + i : own_rows + i + 1, :1]
            )
            target = jnp.concatenate(
                [jnp.sum(e[t] * share, axis=0, keepdims=True) for e in exps], axis=1
            )
            index_exp = jnp.concatenate([x[t : t + 1, :] for x in indexes], axis=1)
            gradient = key_total * (index_exp / index_total - target / head_count)
            weight = jnp.transpose(jnp.broadcast_to(sides[r][i : i + 1, :], (LANES, LANES)))
            weight = weight[:index_heads, :1]
            query = iqueries[r][i]
            dots = contract(query, ikeys, (1, 1))
            column = index_scale * jnp.sum(
                gradient * jnp.maximum(dots, 0.0), axis=1, keepdims=True
            )
            columns = jnp.where(lane == t, column, columns)
            grad_dots = jnp.where(dots > 0, index_scale * gradient * weight, 0.0).astype(bf16)
            dots_ref[t * index_heads : (t + 1) * index_heads, :] = grad_dots
            flat_ref[t * index_heads : (t + 1) * index_heads, :] = query
    grad_dots = dots_ref[...]
    key_grad = contract(grad_dots, flat_ref[...], (0, 0))
    for k in range(len(blocks)):
        value = key_grad[k * own_keys : (k + 1) * own_keys, :]
        if k % 2:
            odd_ref[k // 2] = value.astype(bf16)
        else:
            even_ref[k // 2] = value
    grad_query = contract(grad_dots, ikeys, (1, 0))
    weights = jnp.transpose(jnp.concatenate([columns, jnp.zeros_like(columns)], axis=0)[:LANES])
    for r in range(row_parts):
        out, at = (keep_ref, r) if r < row_parts // 2 else (send_ref, r - row_parts // 2)
        out[at, :lines, :] = grad_query[r * lines : (r + 1) * lines, :]
        out[at, lines : lines + own_rows, :] = weights[r * own_rows : (r + 1) * own_rows, :]


def finish_kernel(key_ref, key_got_ref, row_ref, row_got_ref, query_ref, weight_ref, key_out_ref):
    lines = query_ref.shape[0]
    own_rows, index_heads = weight_ref.shape
    key_out_ref[...] = key_ref[...] + key_got_ref[...].astype(f32)
    query_ref[...] = row_ref[:lines, :] + row_got_ref[:lines, :]
    tail = slice(lines, lines + own_rows)
    weight_ref[...] = (row_ref[tail, :] + row_got_ref[tail, :])[:, :index_heads]


def body(query_main, key_codes, key_scales, index_keys, index_query, index_weight, query_pos):
    own_rows, head_count, latent_width = query_main.shape
    index_heads, index_width = index_query.shape[1:]
    own_keys = key_codes.shape[0]
    count = lax.axis_size("ctx")
    row_parts = 4
    key_parts = count // row_parts
    key_total = own_keys * count
    rows = own_rows * row_parts
    lines = own_rows * index_heads
    tall = lines + 8
    struct = jax.ShapeDtypeStruct

    key_pack, side = pl.pallas_call(
        pack_kernel,
        out_shape=(
            struct((latent_width + own_keys, own_keys), bf16),
            struct((own_rows, LANES), f32),
        ),
        in_specs=[pl.BlockSpec(memory_space=pltpu.HBM)] * 5,
        scratch_shapes=[
            pltpu.VMEM((latent_width, own_keys), bf16),
            pltpu.VMEM((key_scales.shape[1], own_keys), jnp.int32),
            pltpu.VMEM((own_rows, index_heads), f32),
            pltpu.SMEM((own_rows,), jnp.int32),
            pltpu.SemaphoreType.DMA((5,)),
        ],
        compiler_params=pltpu.CompilerParams(vmem_limit_bytes=8 << 20),
        name="pack",
    )(
        *(
            pltpu.with_memory_space_constraint(x, pltpu.HBM)
            for x in (key_codes.T, key_scales.T, index_keys, index_weight, query_pos)
        )
    )
    query_main = jnp.transpose(query_main, (0, 2, 1))
    blocks = swap_gather(key_pack, row_parts, key_parts, count)
    queries = swap_gather(query_main, 1, row_parts, count)
    iqueries = swap_gather(index_query, 1, row_parts, count)
    sides = swap_gather(side, 1, row_parts, count)

    step = 4
    if key_parts <= step:
        pieces = [list(range(key_parts - 1)), [key_parts - 1]]
    else:
        pieces = [list(range(k, k + step)) for k in range(0, key_parts, step)]
    exps, indexes, sums = [], [], None
    for piece in pieces:
        wide = len(piece) * own_keys
        main_exp, index_exp, part = kernel_call(
            functools.partial(score_kernel, tuple(piece), row_parts),
            (
                struct((rows, head_count, wide), f32),
                struct((rows, wide), f32),
                struct((row_parts, 8, head_count), f32),
            ),
            (*sides, *queries, *iqueries, *(blocks[k] for k in piece)),
            flops=2 * rows * head_count * latent_width * wide,
        )
        exps.append(main_exp)
        indexes.append(index_exp)
        sums = part if sums is None else sums + part

    bit = row_parts // 2
    while bit > 1:
        got = swap(sums, bit, count)
        sums = sums + jnp.stack([got[r ^ bit] for r in range(row_parts)])
        bit //= 2
    got = swap(sums, 1, count)

    if key_parts <= step:
        groups = [(pieces, exps, indexes)]
    else:
        groups = [([p], [e], [x]) for p, e, x in zip(pieces, exps, indexes)]
    even, odd, keep, send = [], [], None, None
    for members, group_exps, group_indexes in groups:
        ids = [k for piece in members for k in piece]
        half = len(ids) // 2
        out = kernel_call(
            functools.partial(grad_kernel, key_total, row_parts, tuple(len(p) for p in members)),
            (
                struct((half, own_keys, index_width), f32),
                struct((half, own_keys, index_width), bf16),
                struct((row_parts // 2, tall, index_width), f32),
                struct((row_parts // 2, tall, index_width), f32),
            ),
            (sums, got, *sides, *iqueries, *group_exps, *group_indexes, *(blocks[k] for k in ids)),
            scratch=(
                pltpu.VMEM((rows * index_heads, len(ids) * own_keys), bf16),
                pltpu.VMEM((rows * index_heads, index_width), bf16),
            ),
            flops=6 * rows * index_heads * index_width * len(ids) * own_keys,
        )
        even.append(out[0])
        odd.append(out[1])
        keep = out[2] if keep is None else keep + out[2]
        send = out[3] if send is None else send + out[3]
    key_sum = even[0] if len(even) == 1 else jnp.concatenate(even)
    key_send = odd[0] if len(odd) == 1 else jnp.concatenate(odd)

    key_got = swap(key_send, row_parts, count)
    row_got = swap(send, row_parts // 2, count)
    bit = 2
    while bit < key_parts:
        key_sum = key_sum + key_got.astype(f32)
        key_got = swap(key_sum[1::2].astype(bf16), row_parts * bit, count)
        key_sum = key_sum[0::2]
        bit *= 2
    row_sum = keep + row_got
    row_got = swap(row_sum[1], 1, count)
    grad_query, grad_weight, key_grad = kernel_call(
        finish_kernel,
        (
            struct((lines, index_width), f32),
            struct((own_rows, index_heads), f32),
            struct((own_keys, index_width), f32),
        ),
        (key_sum[0], key_got[0], row_sum[0], row_got),
    )
    return grad_query.reshape(own_rows, index_heads, index_width), grad_weight, key_grad


def solution(mesh):
    placed = (
        P(("grp", "ctx"), None, None),
        P(("grp", "ctx"), None),
        P(("grp", "ctx"), None),
        P(("grp", "ctx"), None),
        P(("grp", "ctx"), None, None),
        P(("grp", "ctx"), None),
        P(("grp", "ctx")),
    )

    return jax.shard_map(
        body,
        mesh=mesh,
        in_specs=placed,
        out_specs=(P(("grp", "ctx"), None, None), P(("grp", "ctx"), None), P(("grp", "ctx"), None)),
        check_vma=False,
    )
```

```python
import functools

import jax
import jax.numpy as jnp
from jax import lax
from jax.experimental import pallas as pl
from jax.experimental.pallas import tpu as pltpu
from jax.sharding import PartitionSpec as P


ROPE = 64
LANES = 128

f32, bf16 = jnp.float32, jnp.bfloat16
main_scale = 192.0 ** (-0.5)


def kernel_call(kernel, shapes, operands, scratch=(), flops=0):
    nbytes = sum(x.size * x.dtype.itemsize for x in (*operands, *shapes))
    return pl.pallas_call(
        kernel,
        out_shape=tuple(shapes),
        scratch_shapes=list(scratch),
        compiler_params=pltpu.CompilerParams(vmem_limit_bytes=24 << 20),
        cost_estimate=pl.CostEstimate(flops=flops, bytes_accessed=nbytes, transcendentals=0),
    )(*operands)


def contract(left, right, dims):
    return lax.dot_general(left, right, ((dims[:1], dims[1:]), ((), ())), preferred_element_type=f32)


def swap(array, mask, count):
    return lax.ppermute(array, "ctx", [(i, i ^ mask) for i in range(count)])


def swap_gather(block, stride, parts, count):
    held = {0: block}
    bit = parts // 2
    while bit:
        for k, own in list(held.items()):
            held[k ^ bit] = swap(own, stride * bit, count)
        bit //= 2
    return [held[k] for k in range(parts)]


def pack_kernel(
    codes_hbm, scales_hbm, keys_hbm, weight_hbm, pos_hbm, out_ref, side_ref, codes_ref, scales_ref,
    weight_ref, pos_ref, sems
):
    groups, own_keys = scales_hbm.shape
    latent_width = codes_hbm.shape[0]
    group_width = (latent_width - ROPE) // groups
    keys_copy = pltpu.make_async_copy(
        keys_hbm, out_ref.at[pl.ds(latent_width, own_keys), :], sems.at[0]
    )
    scales_copy = pltpu.make_async_copy(scales_hbm, scales_ref, sems.at[1])
    weight_copy = pltpu.make_async_copy(weight_hbm, weight_ref, sems.at[2])
    codes_copy = pltpu.make_async_copy(codes_hbm, codes_ref, sems.at[3])
    pos_copy = pltpu.make_async_copy(pos_hbm, pos_ref, sems.at[4])
    for copy in (scales_copy, codes_copy, weight_copy, pos_copy, keys_copy):
        copy.start()
    scales_copy.wait()
    factors = jnp.exp2(scales_ref[...].astype(f32))
    codes_copy.wait()
    for g in range(groups):
        lines = slice(g * group_width, (g + 1) * group_width)
        scaled = codes_ref[lines, :].astype(f32) * factors[g : g + 1, :]
        out_ref[lines, :] = scaled.astype(bf16)
    out_ref[groups * group_width : latent_width, :] = codes_ref[groups * group_width :, :]
    weight_copy.wait()
    pos_copy.wait()
    own_rows, index_heads = weight_ref.shape
    lane = lax.broadcasted_iota(jnp.int32, (1, LANES), 1)
    for i in range(own_rows):
        at = jnp.full((1, LANES), pos_ref[i], jnp.int32).astype(f32)
        side_ref[i : i + 1, :] = jnp.where(lane == index_heads, at, 0.0)
        side_ref[i : i + 1, :index_heads] = weight_ref[i : i + 1, :]
    keys_copy.wait()


def score_kernel(offsets, row_parts, first, *refs):
    parts = len(offsets)
    if first:
        sides, queries, iqueries = (refs[n * row_parts : (n + 1) * row_parts] for n in range(3))
        blocks = refs[3 * row_parts : 3 * row_parts + parts]
        exp_ref, index_ref, sums_ref, main_ref, flat_ref, column_ref, pos_ref, side_ref = refs[
            3 * row_parts + parts :
        ]
        own_rows, index_heads = iqueries[0].shape[:2]
        head_count = queries[0].shape[2]
        for r in range(row_parts):
            side_ref[r * own_rows : (r + 1) * own_rows, :] = sides[r][...]
            for i in range(own_rows):
                t = r * own_rows + i
                main_ref[t * head_count : (t + 1) * head_count, :] = jnp.transpose(queries[r][i])
                flat_ref[t * index_heads : (t + 1) * index_heads, :] = iqueries[r][i]
        side = side_ref[...]
        columns = jnp.transpose(side)
        column_ref[...] = columns[:index_heads, :]
        pos_ref[...] = jnp.broadcast_to(side[:, index_heads : index_heads + 1], pos_ref.shape)
    else:
        main_ref, flat_ref, column_ref, pos_ref = refs[:4]
        blocks = refs[4 : 4 + parts]
        exp_ref, index_ref, sums_ref = refs[4 + parts :]
    rows = pos_ref.shape[0]
    own_rows = rows // row_parts
    index_heads = column_ref.shape[0]
    index_width = flat_ref.shape[1]
    latent_width = main_ref.shape[1]
    head_count = main_ref.shape[0] // rows
    own_keys = blocks[0].shape[1]
    index_scale = float(index_heads * index_width) ** (-0.5)
    me = lax.axis_index("ctx")
    iota = lax.broadcasted_iota(jnp.int32, (1, own_keys), 1)
    key_pos = [((me ^ (row_parts * k)) * own_keys + iota).astype(f32) for k in offsets]
    key_pos = jnp.concatenate(key_pos, axis=1)
    latent = jnp.concatenate([b[:latent_width, :] for b in blocks], axis=1)
    ikeys = jnp.concatenate([b[latent_width:, :] for b in blocks], axis=0)
    dots = contract(flat_ref[...], ikeys, (1, 1))
    scores = contract(main_ref[...], latent, (1, 0))
    sums_ref[...] = jnp.zeros_like(sums_ref)
    for t in range(rows):
        r, i = divmod(t, own_rows)
        visible = key_pos <= pos_ref[t : t + 1, :1]
        heads = jnp.maximum(dots[t * index_heads : (t + 1) * index_heads, :], 0.0)
        score = jnp.sum(column_ref[:, t : t + 1] * heads, axis=0, keepdims=True)
        index_exp = jnp.where(visible, jnp.exp(index_scale * score), 0.0)
        index_ref[t : t + 1, :] = index_exp
        score = scores[t * head_count : (t + 1) * head_count, :] * main_scale
        main_exp = jnp.where(visible, jnp.exp(score), 0.0)
        exp_ref[t] = main_exp
        total = main_exp[:, :own_keys]
        for k in range(1, parts):
            total = total + main_exp[:, k * own_keys : (k + 1) * own_keys]
        sums_ref[r, i : i + 1, :] = jnp.sum(jnp.transpose(total), axis=0, keepdims=True)
        index_total = jnp.sum(index_exp, axis=1, keepdims=True)
        sums_ref[r, own_rows + i : own_rows + i + 1, :] = jnp.broadcast_to(
            index_total, (1, head_count)
        )


def grad_kernel(key_total, row_parts, places, last, *refs):
    count = 1 + max(n for n, _ in places)
    near_ref, far_ref, flat_ref, column_ref = refs[:4]
    exps, indexes = refs[4 : 4 + count], refs[4 + count : 4 + 2 * count]
    refs = refs[4 + 2 * count :]
    blocks, refs = refs[: len(places)], refs[len(places) :]
    if last:
        early_dots, early_columns = refs[:2]
        early_blocks, refs = refs[2 : 2 + len(places)], refs[2 + len(places) :]
        key_ref, keep_ref, send_ref, dots_ref, total_ref = refs
    else:
        key_ref, dots_ref, columns_ref, total_ref = refs
    rows, own_rows = total_ref.shape[0], total_ref.shape[0] // row_parts
    index_heads, index_width = column_ref.shape[0], flat_ref.shape[1]
    head_count, own_keys = exps[0].shape[1], blocks[0].shape[1]
    latent_width = blocks[0].shape[0] - index_width
    index_scale = float(index_heads * index_width) ** (-0.5)
    ikeys = jnp.concatenate([b[latent_width:, :] for b in blocks], axis=0)
    flat = flat_ref[...]
    dots = contract(flat, ikeys, (1, 1))
    for r in range(row_parts):
        lines = slice(0, own_rows)
        total_ref[r * own_rows : (r + 1) * own_rows, :] = near_ref[r, lines, :] + far_ref[r ^ 1, lines, :]
    shares = jnp.transpose(1.0 / total_ref[...])
    lane = lax.broadcasted_iota(jnp.int32, (index_heads, LANES), 1)
    columns = early_columns[...] if last else jnp.zeros((index_heads, LANES), f32)
    for t in range(rows):
        r, i = divmod(t, own_rows)
        share = shares[:, t : t + 1]
        at = own_rows + i
        index_total = near_ref[r, at : at + 1, :1] + far_ref[r ^ 1, at : at + 1, :1]
        target = jnp.concatenate(
            [
                jnp.sum(exps[n][t, :, p : p + own_keys] * share, axis=0, keepdims=True)
                for n, p in places
            ],
            axis=1,
        )
        index_exp = jnp.concatenate(
            [indexes[n][t : t + 1, p : p + own_keys] for n, p in places], axis=1
        )
        gradient = key_total * (index_exp / index_total - target / head_count)
        heads = dots[t * index_heads : (t + 1) * index_heads, :]
        column = index_scale * jnp.sum(gradient * jnp.maximum(heads, 0.0), axis=1, keepdims=True)
        columns = jnp.where(lane == t, columns + column, columns)
        weight = column_ref[:, t : t + 1]
        grad_dots = jnp.where(heads > 0, index_scale * gradient * weight, 0.0).astype(bf16)
        dots_ref[t * index_heads : (t + 1) * index_heads, :] = grad_dots
    grad_dots = dots_ref[...]
    key_grad = contract(grad_dots, flat, (0, 0))
    for k in range(len(blocks)):
        key_ref[k] = key_grad[k * own_keys : (k + 1) * own_keys, :].astype(key_ref.dtype)
    if not last:
        columns_ref[...] = columns
        return
    early_keys = jnp.concatenate([b[latent_width:, :] for b in early_blocks], axis=0)
    grad_query = contract(grad_dots, ikeys, (1, 0)) + contract(early_dots[...], early_keys, (1, 0))
    weights = jnp.transpose(jnp.concatenate([columns, jnp.zeros_like(columns)], axis=0)[:LANES])
    lines = own_rows * index_heads
    for r in range(row_parts):
        out, at = (keep_ref, r) if r < row_parts // 2 else (send_ref, r - row_parts // 2)
        out[at, :lines, :] = grad_query[r * lines : (r + 1) * lines, :]
        out[at, lines : lines + own_rows, :] = weights[r * own_rows : (r + 1) * own_rows, :]


def finish_kernel(key_ref, key_got_ref, row_ref, row_got_ref, query_ref, weight_ref, key_out_ref):
    lines = query_ref.shape[0]
    own_rows, index_heads = weight_ref.shape
    key_out_ref[...] = key_ref[...] + key_got_ref[...].astype(f32)
    query_ref[...] = row_ref[:lines, :] + row_got_ref[:lines, :]
    tail = slice(lines, lines + own_rows)
    weight_ref[...] = (row_ref[tail, :] + row_got_ref[tail, :])[:, :index_heads]


def body(query_main, key_codes, key_scales, index_keys, index_query, index_weight, query_pos):
    own_rows, head_count, latent_width = query_main.shape
    index_heads, index_width = index_query.shape[1:]
    own_keys = key_codes.shape[0]
    count = lax.axis_size("ctx")
    row_parts = 4
    key_parts = count // row_parts
    key_total = own_keys * count
    rows = own_rows * row_parts
    lines = own_rows * index_heads
    tall = lines + 8
    struct = jax.ShapeDtypeStruct

    key_pack, side = pl.pallas_call(
        pack_kernel,
        out_shape=(
            struct((latent_width + own_keys, own_keys), bf16),
            struct((own_rows, LANES), f32),
        ),
        in_specs=[pl.BlockSpec(memory_space=pltpu.HBM)] * 5,
        scratch_shapes=[
            pltpu.VMEM((latent_width, own_keys), bf16),
            pltpu.VMEM((key_scales.shape[1], own_keys), jnp.int32),
            pltpu.VMEM((own_rows, index_heads), f32),
            pltpu.SMEM((own_rows,), jnp.int32),
            pltpu.SemaphoreType.DMA((5,)),
        ],
        compiler_params=pltpu.CompilerParams(vmem_limit_bytes=8 << 20),
        name="pack",
    )(
        *(
            pltpu.with_memory_space_constraint(x, pltpu.HBM)
            for x in (key_codes.T, key_scales.T, index_keys, index_weight, query_pos)
        )
    )
    query_main = jnp.transpose(query_main, (0, 2, 1))
    blocks = swap_gather(key_pack, row_parts, key_parts, count)
    queries = swap_gather(query_main, 1, row_parts, count)
    iqueries = swap_gather(index_query, 1, row_parts, count)
    sides = swap_gather(side, 1, row_parts, count)

    step = 4
    if key_parts <= step:
        pieces = [list(range(key_parts - 1)), [key_parts - 1]]
    else:
        pieces = [list(range(k, k + step)) for k in range(0, key_parts, step)]
    exps, indexes, sums, laid = [], [], None, None
    for n, piece in enumerate(pieces):
        wide = len(piece) * own_keys
        shapes = (
            struct((rows, head_count, wide), f32),
            struct((rows, wide), f32),
            struct((row_parts, 8, head_count), f32),
        )
        if n == 0:
            shapes += (
                struct((rows * head_count, latent_width), bf16),
                struct((rows * index_heads, index_width), bf16),
                struct((index_heads, rows), f32),
                struct((rows, LANES), f32),
            )
        out = kernel_call(
            functools.partial(score_kernel, tuple(piece), row_parts, n == 0),
            shapes,
            (*(laid or (*sides, *queries, *iqueries)), *(blocks[k] for k in piece)),
            scratch=(pltpu.VMEM((rows, LANES), f32),) if n == 0 else (),
            flops=2 * rows * head_count * latent_width * wide,
        )
        laid = laid or out[3:]
        exps.append(out[0])
        indexes.append(out[1])
        sums = out[2] if sums is None else sums + out[2]

    bit = row_parts // 2
    while bit > 1:
        got = swap(sums, bit, count)
        sums = sums + jnp.stack([got[r ^ bit] for r in range(row_parts)])
        bit //= 2
    got = swap(sums, 1, count)

    place = {k: (n, p * own_keys) for n, piece in enumerate(pieces) for p, k in enumerate(piece)}
    groups = [list(range(key_parts))] if key_parts <= step else pieces
    even, odd, keep, send = [], [], None, None
    for ids in groups:
        half = len(ids) // 2
        early = None
        for part in (1, 0):
            mine = ids[part::2]
            used = sorted({place[k][0] for k in mine})
            places = tuple((used.index(place[k][0]), place[k][1]) for k in mine)
            operands = (
                sums,
                got,
                *laid[1:3],
                *(exps[n] for n in used),
                *(indexes[n] for n in used),
                *(blocks[k] for k in mine),
            )
            shapes = (struct((half, own_keys, index_width), bf16 if part else f32),)
            more = struct((rows * index_heads, half * own_keys), bf16)
            scratch = (pltpu.VMEM((rows, head_count), f32),)
            if part:
                shapes += (more, struct((index_heads, LANES), f32))
            else:
                operands += (*early, *(blocks[k] for k in ids[1::2]))
                shapes += (struct((row_parts // 2, tall, index_width), f32),) * 2
                scratch = (pltpu.VMEM(more.shape, bf16), *scratch)
            out = kernel_call(
                functools.partial(grad_kernel, key_total, row_parts, places, not part),
                shapes,
                operands,
                scratch=scratch,
                flops=6 * rows * index_heads * index_width * half * own_keys,
            )
            if part:
                odd.append(out[0])
                early = out[1:]
            else:
                even.append(out[0])
                keep = out[1] if keep is None else keep + out[1]
                send = out[2] if send is None else send + out[2]
    key_sum = even[0] if len(even) == 1 else jnp.concatenate(even)
    key_send = odd[0] if len(odd) == 1 else jnp.concatenate(odd)

    key_got = swap(key_send, row_parts, count)
    row_got = swap(send, row_parts // 2, count)
    bit = 2
    while bit < key_parts:
        key_sum = key_sum + key_got.astype(f32)
        key_got = swap(key_sum[1::2].astype(bf16), row_parts * bit, count)
        key_sum = key_sum[0::2]
        bit *= 2
    row_sum = keep + row_got
    row_got = swap(row_sum[1], 1, count)
    grad_query, grad_weight, key_grad = kernel_call(
        finish_kernel,
        (
            struct((lines, index_width), f32),
            struct((own_rows, index_heads), f32),
            struct((own_keys, index_width), f32),
        ),
        (key_sum[0], key_got[0], row_sum[0], row_got),
    )
    return grad_query.reshape(own_rows, index_heads, index_width), grad_weight, key_grad


def solution(mesh):
    placed = (
        P(("grp", "ctx"), None, None),
        P(("grp", "ctx"), None),
        P(("grp", "ctx"), None),
        P(("grp", "ctx"), None),
        P(("grp", "ctx"), None, None),
        P(("grp", "ctx"), None),
        P(("grp", "ctx")),
    )

    return jax.shard_map(
        body,
        mesh=mesh,
        in_specs=placed,
        out_specs=(P(("grp", "ctx"), None, None), P(("grp", "ctx"), None), P(("grp", "ctx"), None)),
        check_vma=False,
    )
```

```python
import functools

import jax
import jax.numpy as jnp
from jax import lax
from jax.experimental import pallas as pl
from jax.experimental.pallas import tpu as pltpu
from jax.sharding import PartitionSpec as P


ROPE = 64
LANES = 128

f32, bf16 = jnp.float32, jnp.bfloat16
main_scale = 192.0 ** (-0.5)


def kernel_call(kernel, shapes, operands, scratch=(), flops=0):
    nbytes = sum(x.size * x.dtype.itemsize for x in (*operands, *shapes))
    return pl.pallas_call(
        kernel,
        out_shape=tuple(shapes),
        scratch_shapes=list(scratch),
        compiler_params=pltpu.CompilerParams(vmem_limit_bytes=24 << 20),
        cost_estimate=pl.CostEstimate(flops=flops, bytes_accessed=nbytes, transcendentals=0),
    )(*operands)


def contract(left, right, dims):
    return lax.dot_general(left, right, ((dims[:1], dims[1:]), ((), ())), preferred_element_type=f32)


def swap(array, mask, count):
    return lax.ppermute(array, "ctx", [(i, i ^ mask) for i in range(count)])


def swap_gather(block, stride, parts, count):
    held = {0: block}
    bit = parts // 2
    while bit:
        for k, own in list(held.items()):
            held[k ^ bit] = swap(own, stride * bit, count)
        bit //= 2
    return [held[k] for k in range(parts)]


def pack_kernel(
    scales_hbm, keys_hbm, weight_hbm, pos_hbm, main_hbm, query_hbm, codes_hbm, out_ref, side_ref,
    main_ref, query_ref, codes_ref, scales_ref, weight_ref, pos_ref, sems
):
    groups, own_keys = scales_hbm.shape
    key_count = keys_hbm.shape[0]
    pairs = (
        (scales_hbm, scales_ref),
        (weight_hbm, weight_ref),
        (pos_hbm, pos_ref),
        (keys_hbm, out_ref.at[pl.ds(0, key_count), :]),
        (query_hbm, query_ref),
        (main_hbm, main_ref),
        (codes_hbm, codes_ref),
    )
    copies = [pltpu.make_async_copy(a, b, sems.at[n]) for n, (a, b) in enumerate(pairs)]
    for copy in copies:
        copy.start()
    for copy in copies[:3]:
        copy.wait()
    factors = jnp.exp2(scales_ref[...].astype(f32))
    spare = out_ref.shape[0] - key_count - groups
    factors = jnp.concatenate([factors, jnp.zeros((spare, own_keys), f32)], axis=0)
    out_ref[key_count:, :] = factors.astype(bf16)
    own_rows, index_heads = weight_ref.shape
    lane = lax.broadcasted_iota(jnp.int32, (1, LANES), 1)
    for i in range(own_rows):
        at = jnp.full((1, LANES), pos_ref[i], jnp.int32).astype(f32)
        side_ref[i : i + 1, :] = jnp.where(lane == index_heads, at, 0.0)
        side_ref[i : i + 1, :index_heads] = weight_ref[i : i + 1, :]
    for copy in copies[3:]:
        copy.wait()


def latent_of(codes_ref, keys_ref, groups):
    latent_width, own_keys = codes_ref.shape
    group_width = (latent_width - ROPE) // groups
    factors = keys_ref[own_keys:, :].astype(f32)
    latent = [
        (codes_ref[g * group_width : (g + 1) * group_width, :].astype(f32) * factors[g : g + 1, :]).astype(bf16)
        for g in range(groups)
    ]
    return jnp.concatenate([*latent, codes_ref[groups * group_width :, :]], axis=0)


def score_kernel(offsets, row_parts, groups, first, *refs):
    parts = len(offsets)
    if first:
        sides, queries, iqueries = (refs[n * row_parts : (n + 1) * row_parts] for n in range(3))
        refs = refs[3 * row_parts :]
        codes, blocks, refs = refs[:parts], refs[parts : 2 * parts], refs[2 * parts :]
        exp_ref, index_ref, sums_ref, main_ref, flat_ref, column_ref, pos_ref, side_ref = refs
        own_rows, index_heads = iqueries[0].shape[:2]
        head_count = queries[0].shape[2]
        for r in range(row_parts):
            side_ref[r * own_rows : (r + 1) * own_rows, :] = sides[r][...]
            for i in range(own_rows):
                t = r * own_rows + i
                main_ref[t * head_count : (t + 1) * head_count, :] = jnp.transpose(queries[r][i])
                flat_ref[t * index_heads : (t + 1) * index_heads, :] = iqueries[r][i]
        side = side_ref[...]
        columns = jnp.transpose(side)
        column_ref[...] = columns[:index_heads, :]
        pos_ref[...] = jnp.broadcast_to(side[:, index_heads : index_heads + 1], pos_ref.shape)
    else:
        main_ref, flat_ref, column_ref, pos_ref = refs[:4]
        codes, blocks = refs[4 : 4 + parts], refs[4 + parts : 4 + 2 * parts]
        exp_ref, index_ref, sums_ref = refs[4 + 2 * parts :]
    rows = pos_ref.shape[0]
    own_rows = rows // row_parts
    index_heads = column_ref.shape[0]
    index_width = flat_ref.shape[1]
    head_count = main_ref.shape[0] // rows
    own_keys = blocks[0].shape[1]
    index_scale = float(index_heads * index_width) ** (-0.5)
    me = lax.axis_index("ctx")
    iota = lax.broadcasted_iota(jnp.int32, (1, own_keys), 1)
    key_pos = [((me ^ (row_parts * k)) * own_keys + iota).astype(f32) for k in offsets]
    key_pos = jnp.concatenate(key_pos, axis=1)
    latent = jnp.concatenate([latent_of(c, b, groups) for c, b in zip(codes, blocks)], axis=1)
    ikeys = jnp.concatenate([b[:own_keys, :] for b in blocks], axis=0)
    dots = contract(flat_ref[...], ikeys, (1, 1))
    scores = contract(main_ref[...], latent, (1, 0))
    sums_ref[...] = jnp.zeros_like(sums_ref)
    for t in range(rows):
        r, i = divmod(t, own_rows)
        visible = key_pos <= pos_ref[t : t + 1, :1]
        heads = jnp.maximum(dots[t * index_heads : (t + 1) * index_heads, :], 0.0)
        score = jnp.sum(column_ref[:, t : t + 1] * heads, axis=0, keepdims=True)
        index_exp = jnp.where(visible, jnp.exp(index_scale * score), 0.0)
        index_ref[t : t + 1, :] = index_exp
        score = scores[t * head_count : (t + 1) * head_count, :] * main_scale
        main_exp = jnp.where(visible, jnp.exp(score), 0.0)
        exp_ref[t] = main_exp
        total = main_exp[:, :own_keys]
        for k in range(1, parts):
            total = total + main_exp[:, k * own_keys : (k + 1) * own_keys]
        sums_ref[r, i : i + 1, :] = jnp.sum(jnp.transpose(total), axis=0, keepdims=True)
        index_total = jnp.sum(index_exp, axis=1, keepdims=True)
        sums_ref[r, own_rows + i : own_rows + i + 1, :] = jnp.broadcast_to(
            index_total, (1, head_count)
        )


def grad_kernel(key_total, row_parts, places, last, *refs):
    count = 1 + max(n for n, _ in places)
    near_ref, far_ref, flat_ref, column_ref = refs[:4]
    exps, indexes = refs[4 : 4 + count], refs[4 + count : 4 + 2 * count]
    refs = refs[4 + 2 * count :]
    blocks, refs = refs[: len(places)], refs[len(places) :]
    if last:
        early_dots, early_columns = refs[:2]
        early_blocks, refs = refs[2 : 2 + len(places)], refs[2 + len(places) :]
        key_ref, keep_ref, send_ref, dots_ref, total_ref = refs
    else:
        key_ref, dots_ref, columns_ref, total_ref = refs
    rows, own_rows = total_ref.shape[0], total_ref.shape[0] // row_parts
    index_heads, index_width = column_ref.shape[0], flat_ref.shape[1]
    head_count, own_keys = exps[0].shape[1], key_ref.shape[1]
    index_scale = float(index_heads * index_width) ** (-0.5)
    ikeys = jnp.concatenate([b[:own_keys, :] for b in blocks], axis=0)
    flat = flat_ref[...]
    dots = contract(flat, ikeys, (1, 1))
    for r in range(row_parts):
        lines = slice(0, own_rows)
        total_ref[r * own_rows : (r + 1) * own_rows, :] = near_ref[r, lines, :] + far_ref[r ^ 1, lines, :]
    shares = jnp.transpose(1.0 / total_ref[...])
    lane = lax.broadcasted_iota(jnp.int32, (index_heads, LANES), 1)
    columns = early_columns[...] if last else jnp.zeros((index_heads, LANES), f32)
    for t in range(rows):
        r, i = divmod(t, own_rows)
        share = shares[:, t : t + 1]
        at = own_rows + i
        index_total = near_ref[r, at : at + 1, :1] + far_ref[r ^ 1, at : at + 1, :1]
        target = jnp.concatenate(
            [
                jnp.sum(exps[n][t, :, p : p + own_keys] * share, axis=0, keepdims=True)
                for n, p in places
            ],
            axis=1,
        )
        index_exp = jnp.concatenate(
            [indexes[n][t : t + 1, p : p + own_keys] for n, p in places], axis=1
        )
        gradient = key_total * (index_exp / index_total - target / head_count)
        heads = dots[t * index_heads : (t + 1) * index_heads, :]
        column = index_scale * jnp.sum(gradient * jnp.maximum(heads, 0.0), axis=1, keepdims=True)
        columns = jnp.where(lane == t, columns + column, columns)
        weight = column_ref[:, t : t + 1]
        grad_dots = jnp.where(heads > 0, index_scale * gradient * weight, 0.0).astype(bf16)
        dots_ref[t * index_heads : (t + 1) * index_heads, :] = grad_dots
    grad_dots = dots_ref[...]
    key_grad = contract(grad_dots, flat, (0, 0))
    for k in range(len(blocks)):
        key_ref[k] = key_grad[k * own_keys : (k + 1) * own_keys, :].astype(key_ref.dtype)
    if not last:
        columns_ref[...] = columns
        return
    early_keys = jnp.concatenate([b[:own_keys, :] for b in early_blocks], axis=0)
    grad_query = contract(grad_dots, ikeys, (1, 0)) + contract(early_dots[...], early_keys, (1, 0))
    weights = jnp.transpose(jnp.concatenate([columns, jnp.zeros_like(columns)], axis=0)[:LANES])
    lines = own_rows * index_heads
    for r in range(row_parts):
        out, at = (keep_ref, r) if r < row_parts // 2 else (send_ref, r - row_parts // 2)
        out[at, :lines, :] = grad_query[r * lines : (r + 1) * lines, :]
        out[at, lines : lines + own_rows, :] = weights[r * own_rows : (r + 1) * own_rows, :]


def finish_kernel(key_ref, key_got_ref, row_ref, row_got_ref, query_ref, weight_ref, key_out_ref):
    lines = query_ref.shape[0]
    own_rows, index_heads = weight_ref.shape
    key_out_ref[...] = key_ref[...] + key_got_ref[...].astype(f32)
    query_ref[...] = row_ref[:lines, :] + row_got_ref[:lines, :]
    tail = slice(lines, lines + own_rows)
    weight_ref[...] = (row_ref[tail, :] + row_got_ref[tail, :])[:, :index_heads]


def body(query_main, key_codes, key_scales, index_keys, index_query, index_weight, query_pos):
    own_rows, head_count, latent_width = query_main.shape
    index_heads, index_width = index_query.shape[1:]
    own_keys = key_codes.shape[0]
    count = lax.axis_size("ctx")
    row_parts = 4
    key_parts = count // row_parts
    key_total = own_keys * count
    rows = own_rows * row_parts
    lines = own_rows * index_heads
    tall = lines + 8
    struct = jax.ShapeDtypeStruct

    codes = key_codes.T
    groups = key_scales.shape[1]
    sources = (
        key_scales.T,
        index_keys,
        index_weight,
        query_pos,
        jnp.transpose(query_main, (0, 2, 1)),
        index_query,
        codes,
    )
    key_pack, side, main_own, index_own, codes_own = pl.pallas_call(
        pack_kernel,
        out_shape=(
            struct((own_keys + 16, own_keys), bf16),
            struct((own_rows, LANES), f32),
            struct(sources[4].shape, bf16),
            struct(index_query.shape, bf16),
            struct(codes.shape, bf16),
        ),
        in_specs=[pl.BlockSpec(memory_space=pltpu.HBM)] * len(sources),
        scratch_shapes=[
            pltpu.VMEM((groups, own_keys), jnp.int32),
            pltpu.VMEM((own_rows, index_heads), f32),
            pltpu.SMEM((own_rows,), jnp.int32),
            pltpu.SemaphoreType.DMA((len(sources),)),
        ],
        compiler_params=pltpu.CompilerParams(vmem_limit_bytes=8 << 20),
        name="pack",
    )(*(pltpu.with_memory_space_constraint(x, pltpu.HBM) for x in sources))
    codes = swap_gather(codes, row_parts, key_parts, count)
    codes[0] = codes_own
    blocks = swap_gather(key_pack, row_parts, key_parts, count)
    queries = swap_gather(main_own, 1, row_parts, count)
    iqueries = swap_gather(index_own, 1, row_parts, count)
    sides = swap_gather(side, 1, row_parts, count)

    step = 4
    if key_parts <= step:
        pieces = [list(range(key_parts - 1)), [key_parts - 1]]
    else:
        pieces = [list(range(k, k + step)) for k in range(0, key_parts, step)]
    exps, indexes, sums, laid = [], [], None, None
    for n, piece in enumerate(pieces):
        wide = len(piece) * own_keys
        shapes = (
            struct((rows, head_count, wide), f32),
            struct((rows, wide), f32),
            struct((row_parts, 8, head_count), f32),
        )
        if n == 0:
            shapes += (
                struct((rows * head_count, latent_width), bf16),
                struct((rows * index_heads, index_width), bf16),
                struct((index_heads, rows), f32),
                struct((rows, LANES), f32),
            )
        out = kernel_call(
            functools.partial(score_kernel, tuple(piece), row_parts, groups, n == 0),
            shapes,
            (
                *(laid or (*sides, *queries, *iqueries)),
                *(codes[k] for k in piece),
                *(blocks[k] for k in piece),
            ),
            scratch=(pltpu.VMEM((rows, LANES), f32),) if n == 0 else (),
            flops=2 * rows * head_count * latent_width * wide,
        )
        laid = laid or out[3:]
        exps.append(out[0])
        indexes.append(out[1])
        sums = out[2] if sums is None else sums + out[2]

    bit = row_parts // 2
    while bit > 1:
        got = swap(sums, bit, count)
        sums = sums + jnp.stack([got[r ^ bit] for r in range(row_parts)])
        bit //= 2
    got = swap(sums, 1, count)

    place = {k: (n, p * own_keys) for n, piece in enumerate(pieces) for p, k in enumerate(piece)}
    teams = [list(range(key_parts))] if key_parts <= step else pieces
    even, odd, keep, send = [], [], None, None
    for ids in teams:
        half = len(ids) // 2
        early = None
        for part in (1, 0):
            mine = ids[part::2]
            used = sorted({place[k][0] for k in mine})
            places = tuple((used.index(place[k][0]), place[k][1]) for k in mine)
            operands = (
                sums,
                got,
                *laid[1:3],
                *(exps[n] for n in used),
                *(indexes[n] for n in used),
                *(blocks[k] for k in mine),
            )
            shapes = (struct((half, own_keys, index_width), bf16 if part else f32),)
            more = struct((rows * index_heads, half * own_keys), bf16)
            scratch = (pltpu.VMEM((rows, head_count), f32),)
            if part:
                shapes += (more, struct((index_heads, LANES), f32))
            else:
                operands += (*early, *(blocks[k] for k in ids[1::2]))
                shapes += (struct((row_parts // 2, tall, index_width), f32),) * 2
                scratch = (pltpu.VMEM(more.shape, bf16), *scratch)
            out = kernel_call(
                functools.partial(grad_kernel, key_total, row_parts, places, not part),
                shapes,
                operands,
                scratch=scratch,
                flops=6 * rows * index_heads * index_width * half * own_keys,
            )
            if part:
                odd.append(out[0])
                early = out[1:]
            else:
                even.append(out[0])
                keep = out[1] if keep is None else keep + out[1]
                send = out[2] if send is None else send + out[2]
    key_sum = even[0] if len(even) == 1 else jnp.concatenate(even)
    key_send = odd[0] if len(odd) == 1 else jnp.concatenate(odd)

    key_got = swap(key_send, row_parts, count)
    row_got = swap(send, row_parts // 2, count)
    bit = 2
    while bit < key_parts:
        key_sum = key_sum + key_got.astype(f32)
        key_got = swap(key_sum[1::2].astype(bf16), row_parts * bit, count)
        key_sum = key_sum[0::2]
        bit *= 2
    row_sum = keep + row_got
    row_got = swap(row_sum[1], 1, count)
    grad_query, grad_weight, key_grad = kernel_call(
        finish_kernel,
        (
            struct((lines, index_width), f32),
            struct((own_rows, index_heads), f32),
            struct((own_keys, index_width), f32),
        ),
        (key_sum[0], key_got[0], row_sum[0], row_got),
    )
    return grad_query.reshape(own_rows, index_heads, index_width), grad_weight, key_grad


def solution(mesh):
    placed = (
        P(("grp", "ctx"), None, None),
        P(("grp", "ctx"), None),
        P(("grp", "ctx"), None),
        P(("grp", "ctx"), None),
        P(("grp", "ctx"), None, None),
        P(("grp", "ctx"), None),
        P(("grp", "ctx")),
    )

    return jax.shard_map(
        body,
        mesh=mesh,
        in_specs=placed,
        out_specs=(P(("grp", "ctx"), None, None), P(("grp", "ctx"), None), P(("grp", "ctx"), None)),
        check_vma=False,
    )
```

```python
import functools

import jax
import jax.numpy as jnp
from jax import lax
from jax.experimental import pallas as pl
from jax.experimental.pallas import tpu as pltpu
from jax.sharding import PartitionSpec as P


ROPE = 64
LANES = 128

f32, bf16 = jnp.float32, jnp.bfloat16
main_scale = 192.0 ** (-0.5)


def kernel_call(kernel, shapes, operands, scratch=(), flops=0):
    nbytes = sum(x.size * x.dtype.itemsize for x in (*operands, *shapes))
    return pl.pallas_call(
        kernel,
        out_shape=tuple(shapes),
        scratch_shapes=list(scratch),
        compiler_params=pltpu.CompilerParams(vmem_limit_bytes=24 << 20),
        cost_estimate=pl.CostEstimate(flops=flops, bytes_accessed=nbytes, transcendentals=0),
    )(*operands)


def contract(left, right, dims):
    return lax.dot_general(left, right, ((dims[:1], dims[1:]), ((), ())), preferred_element_type=f32)


def swap(array, mask, count):
    return lax.ppermute(array, "ctx", [(i, i ^ mask) for i in range(count)])


def swap_gather(block, stride, parts, count):
    held = {0: block}
    bit = parts // 2
    while bit:
        for k, own in list(held.items()):
            held[k ^ bit] = swap(own, stride * bit, count)
        bit //= 2
    return [held[k] for k in range(parts)]


def pack_kernel(
    scales_hbm, keys_hbm, weight_hbm, pos_hbm, main_hbm, query_hbm, codes_hbm, out_ref, query_ref,
    main_ref, codes_ref, scales_ref, weight_ref, pos_ref, sems
):
    groups, own_keys = scales_hbm.shape
    key_count = keys_hbm.shape[0]
    lines = query_hbm.shape[0]
    pairs = (
        (scales_hbm, scales_ref),
        (weight_hbm, weight_ref),
        (pos_hbm, pos_ref),
        (keys_hbm, out_ref.at[pl.ds(0, key_count), :]),
        (query_hbm, query_ref.at[pl.ds(0, lines), :]),
        (main_hbm, main_ref),
        (codes_hbm, codes_ref),
    )
    copies = [pltpu.make_async_copy(a, b, sems.at[n]) for n, (a, b) in enumerate(pairs)]
    for copy in copies:
        copy.start()
    for copy in copies[:3]:
        copy.wait()
    factors = jnp.exp2(scales_ref[...].astype(f32))
    spare = out_ref.shape[0] - key_count - groups
    factors = jnp.concatenate([factors, jnp.zeros((spare, own_keys), f32)], axis=0)
    out_ref[key_count:, :] = factors.astype(bf16)
    own_rows, index_heads = weight_ref.shape
    rest = jnp.concatenate([weight_ref[...], jnp.zeros((own_rows, LANES - index_heads), f32)], axis=1)
    lane = lax.broadcasted_iota(jnp.int32, (1, LANES), 1)
    tail = []
    for part in range(3):
        piece = rest.astype(bf16).astype(f32)
        rest = rest - piece
        for i in range(own_rows):
            pos = jnp.full((1, LANES), pos_ref[i], jnp.int32)
            at = ((pos // LANES) * LANES, pos % LANES, jnp.zeros_like(pos))[part].astype(f32)
            tail.append(jnp.where(lane == index_heads, at, piece[i : i + 1, :]))
    tail.append(jnp.zeros((query_ref.shape[0] - lines - len(tail), LANES), f32))
    query_ref[lines:, :] = jnp.concatenate(tail, axis=0).astype(bf16)
    for copy in copies[3:]:
        copy.wait()


def latent_of(codes_ref, keys_ref, groups):
    latent_width, own_keys = codes_ref.shape
    group_width = (latent_width - ROPE) // groups
    factors = keys_ref[own_keys:, :].astype(f32)
    latent = [
        (codes_ref[g * group_width : (g + 1) * group_width, :].astype(f32) * factors[g : g + 1, :]).astype(bf16)
        for g in range(groups)
    ]
    return jnp.concatenate([*latent, codes_ref[groups * group_width :, :]], axis=0)


def score_kernel(offsets, row_parts, groups, first, *refs):
    parts = len(offsets)
    if first:
        queries, iqueries = refs[:row_parts], refs[row_parts : 2 * row_parts]
        refs = refs[2 * row_parts :]
        codes, blocks, refs = refs[:parts], refs[parts : 2 * parts], refs[2 * parts :]
        exp_ref, index_ref, sums_ref, main_ref, flat_ref, column_ref, pos_ref, side_ref = refs
        own_rows, head_count = queries[0].shape[0], queries[0].shape[2]
        lines = flat_ref.shape[0] // row_parts
        index_heads = lines // own_rows
        for r in range(row_parts):
            tail = iqueries[r][lines:, :].astype(f32)
            side = tail[:own_rows] + tail[own_rows : 2 * own_rows]
            side = side + tail[2 * own_rows : 3 * own_rows]
            side_ref[r * own_rows : (r + 1) * own_rows, :] = side
            flat_ref[r * lines : (r + 1) * lines, :] = iqueries[r][:lines, :]
            for i in range(own_rows):
                t = r * own_rows + i
                main_ref[t * head_count : (t + 1) * head_count, :] = jnp.transpose(queries[r][i])
        side = side_ref[...]
        columns = jnp.transpose(side)
        column_ref[...] = columns[:index_heads, :]
        pos_ref[...] = jnp.broadcast_to(side[:, index_heads : index_heads + 1], pos_ref.shape)
    else:
        main_ref, flat_ref, column_ref, pos_ref = refs[:4]
        codes, blocks = refs[4 : 4 + parts], refs[4 + parts : 4 + 2 * parts]
        exp_ref, index_ref, sums_ref = refs[4 + 2 * parts :]
    rows = pos_ref.shape[0]
    own_rows = rows // row_parts
    index_heads = column_ref.shape[0]
    index_width = flat_ref.shape[1]
    head_count = main_ref.shape[0] // rows
    own_keys = blocks[0].shape[1]
    index_scale = float(index_heads * index_width) ** (-0.5)
    me = lax.axis_index("ctx")
    iota = lax.broadcasted_iota(jnp.int32, (1, own_keys), 1)
    key_pos = [((me ^ (row_parts * k)) * own_keys + iota).astype(f32) for k in offsets]
    key_pos = jnp.concatenate(key_pos, axis=1)
    latent = jnp.concatenate([latent_of(c, b, groups) for c, b in zip(codes, blocks)], axis=1)
    ikeys = jnp.concatenate([b[:own_keys, :] for b in blocks], axis=0)
    dots = contract(flat_ref[...], ikeys, (1, 1))
    scores = contract(main_ref[...], latent, (1, 0))
    sums_ref[...] = jnp.zeros_like(sums_ref)
    for t in range(rows):
        r, i = divmod(t, own_rows)
        visible = key_pos <= pos_ref[t : t + 1, :1]
        heads = jnp.maximum(dots[t * index_heads : (t + 1) * index_heads, :], 0.0)
        score = jnp.sum(column_ref[:, t : t + 1] * heads, axis=0, keepdims=True)
        index_exp = jnp.where(visible, jnp.exp(index_scale * score), 0.0)
        index_ref[t : t + 1, :] = index_exp
        score = scores[t * head_count : (t + 1) * head_count, :] * main_scale
        main_exp = jnp.where(visible, jnp.exp(score), 0.0)
        exp_ref[t] = main_exp
        total = main_exp[:, :own_keys]
        for k in range(1, parts):
            total = total + main_exp[:, k * own_keys : (k + 1) * own_keys]
        sums_ref[r, i : i + 1, :] = jnp.sum(jnp.transpose(total), axis=0, keepdims=True)
        index_total = jnp.sum(index_exp, axis=1, keepdims=True)
        sums_ref[r, own_rows + i : own_rows + i + 1, :] = jnp.broadcast_to(
            index_total, (1, head_count)
        )


def grad_kernel(key_total, row_parts, places, last, *refs):
    count = 1 + max(n for n, _ in places)
    near_ref, far_ref, flat_ref, column_ref = refs[:4]
    exps, indexes = refs[4 : 4 + count], refs[4 + count : 4 + 2 * count]
    refs = refs[4 + 2 * count :]
    blocks, refs = refs[: len(places)], refs[len(places) :]
    if last:
        early_dots, early_columns = refs[:2]
        early_blocks, refs = refs[2 : 2 + len(places)], refs[2 + len(places) :]
        key_ref, keep_ref, send_ref, dots_ref, total_ref = refs
    else:
        key_ref, dots_ref, columns_ref, total_ref = refs
    rows, own_rows = total_ref.shape[0], total_ref.shape[0] // row_parts
    index_heads, index_width = column_ref.shape[0], flat_ref.shape[1]
    head_count, own_keys = exps[0].shape[1], key_ref.shape[1]
    index_scale = float(index_heads * index_width) ** (-0.5)
    ikeys = jnp.concatenate([b[:own_keys, :] for b in blocks], axis=0)
    flat = flat_ref[...]
    dots = contract(flat, ikeys, (1, 1))
    for r in range(row_parts):
        lines = slice(0, own_rows)
        total_ref[r * own_rows : (r + 1) * own_rows, :] = near_ref[r, lines, :] + far_ref[r ^ 1, lines, :]
    shares = jnp.transpose(1.0 / total_ref[...])
    lane = lax.broadcasted_iota(jnp.int32, (index_heads, LANES), 1)
    columns = early_columns[...] if last else jnp.zeros((index_heads, LANES), f32)
    for t in range(rows):
        r, i = divmod(t, own_rows)
        share = shares[:, t : t + 1]
        at = own_rows + i
        index_total = near_ref[r, at : at + 1, :1] + far_ref[r ^ 1, at : at + 1, :1]
        target = jnp.concatenate(
            [
                jnp.sum(exps[n][t, :, p : p + own_keys] * share, axis=0, keepdims=True)
                for n, p in places
            ],
            axis=1,
        )
        index_exp = jnp.concatenate(
            [indexes[n][t : t + 1, p : p + own_keys] for n, p in places], axis=1
        )
        gradient = key_total * (index_exp / index_total - target / head_count)
        heads = dots[t * index_heads : (t + 1) * index_heads, :]
        column = index_scale * jnp.sum(gradient * jnp.maximum(heads, 0.0), axis=1, keepdims=True)
        columns = jnp.where(lane == t, columns + column, columns)
        weight = column_ref[:, t : t + 1]
        grad_dots = jnp.where(heads > 0, index_scale * gradient * weight, 0.0).astype(bf16)
        dots_ref[t * index_heads : (t + 1) * index_heads, :] = grad_dots
    grad_dots = dots_ref[...]
    key_grad = contract(grad_dots, flat, (0, 0))
    for k in range(len(blocks)):
        key_ref[k] = key_grad[k * own_keys : (k + 1) * own_keys, :].astype(key_ref.dtype)
    if not last:
        columns_ref[...] = columns
        return
    early_keys = jnp.concatenate([b[:own_keys, :] for b in early_blocks], axis=0)
    grad_query = contract(grad_dots, ikeys, (1, 0)) + contract(early_dots[...], early_keys, (1, 0))
    weights = jnp.transpose(jnp.concatenate([columns, jnp.zeros_like(columns)], axis=0)[:LANES])
    lines = own_rows * index_heads
    for r in range(row_parts):
        out, at = (keep_ref, r) if r < row_parts // 2 else (send_ref, r - row_parts // 2)
        out[at, :lines, :] = grad_query[r * lines : (r + 1) * lines, :]
        out[at, lines : lines + own_rows, :] = weights[r * own_rows : (r + 1) * own_rows, :]


def finish_kernel(key_ref, key_got_ref, row_ref, row_got_ref, query_ref, weight_ref, key_out_ref):
    lines = query_ref.shape[0]
    own_rows, index_heads = weight_ref.shape
    key_out_ref[...] = key_ref[...] + key_got_ref[...].astype(f32)
    query_ref[...] = row_ref[:lines, :] + row_got_ref[:lines, :]
    tail = slice(lines, lines + own_rows)
    weight_ref[...] = (row_ref[tail, :] + row_got_ref[tail, :])[:, :index_heads]


def body(query_main, key_codes, key_scales, index_keys, index_query, index_weight, query_pos):
    own_rows, head_count, latent_width = query_main.shape
    index_heads, index_width = index_query.shape[1:]
    own_keys = key_codes.shape[0]
    count = lax.axis_size("ctx")
    row_parts = 4
    key_parts = count // row_parts
    key_total = own_keys * count
    rows = own_rows * row_parts
    lines = own_rows * index_heads
    tall = lines + 8
    struct = jax.ShapeDtypeStruct

    codes = key_codes.T
    groups = key_scales.shape[1]
    main_raw = jnp.transpose(query_main, (0, 2, 1))
    sources = (
        key_scales.T,
        index_keys,
        index_weight,
        query_pos,
        main_raw,
        index_query.reshape(lines, index_width),
        codes,
    )
    key_pack, index_own, main_own, codes_own = pl.pallas_call(
        pack_kernel,
        out_shape=(
            struct((own_keys + 16, own_keys), bf16),
            struct((lines + 16, index_width), bf16),
            struct(main_raw.shape, bf16),
            struct(codes.shape, bf16),
        ),
        in_specs=[pl.BlockSpec(memory_space=pltpu.HBM)] * len(sources),
        scratch_shapes=[
            pltpu.VMEM((groups, own_keys), jnp.int32),
            pltpu.VMEM((own_rows, index_heads), f32),
            pltpu.SMEM((own_rows,), jnp.int32),
            pltpu.SemaphoreType.DMA((len(sources),)),
        ],
        compiler_params=pltpu.CompilerParams(vmem_limit_bytes=8 << 20),
        name="pack",
    )(*(pltpu.with_memory_space_constraint(x, pltpu.HBM) for x in sources))
    codes = swap_gather(codes, row_parts, key_parts, count)
    codes[0] = codes_own
    blocks = swap_gather(key_pack, row_parts, key_parts, count)
    queries = swap_gather(main_raw, 1, row_parts, count)
    queries[0] = main_own
    iqueries = swap_gather(index_own, 1, row_parts, count)

    step = 4
    if key_parts <= step:
        pieces = [list(range(key_parts - 1)), [key_parts - 1]]
    else:
        pieces = [list(range(k, k + step)) for k in range(0, key_parts, step)]
    exps, indexes, sums, laid = [], [], None, None
    for n, piece in enumerate(pieces):
        wide = len(piece) * own_keys
        shapes = (
            struct((rows, head_count, wide), f32),
            struct((rows, wide), f32),
            struct((row_parts, 2 * own_rows, head_count), f32),
        )
        if n == 0:
            shapes += (
                struct((rows * head_count, latent_width), bf16),
                struct((rows * index_heads, index_width), bf16),
                struct((index_heads, rows), f32),
                struct((rows, LANES), f32),
            )
        out = kernel_call(
            functools.partial(score_kernel, tuple(piece), row_parts, groups, n == 0),
            shapes,
            (
                *(laid or (*queries, *iqueries)),
                *(codes[k] for k in piece),
                *(blocks[k] for k in piece),
            ),
            scratch=(pltpu.VMEM((rows, LANES), f32),) if n == 0 else (),
            flops=2 * rows * head_count * latent_width * wide,
        )
        laid = laid or out[3:]
        exps.append(out[0])
        indexes.append(out[1])
        sums = out[2] if sums is None else sums + out[2]

    bit = row_parts // 2
    while bit > 1:
        got = swap(sums, bit, count)
        sums = sums + jnp.stack([got[r ^ bit] for r in range(row_parts)])
        bit //= 2
    got = swap(sums, 1, count)

    place = {k: (n, p * own_keys) for n, piece in enumerate(pieces) for p, k in enumerate(piece)}
    teams = [list(range(key_parts))] if key_parts <= step else pieces
    even, odd, keep, send = [], [], None, None
    for ids in teams:
        half = len(ids) // 2
        early = None
        for part in (1, 0):
            mine = ids[part::2]
            used = sorted({place[k][0] for k in mine})
            places = tuple((used.index(place[k][0]), place[k][1]) for k in mine)
            operands = (
                sums,
                got,
                *laid[1:3],
                *(exps[n] for n in used),
                *(indexes[n] for n in used),
                *(blocks[k] for k in mine),
            )
            shapes = (struct((half, own_keys, index_width), bf16 if part else f32),)
            more = struct((rows * index_heads, half * own_keys), bf16)
            scratch = (pltpu.VMEM((rows, head_count), f32),)
            if part:
                shapes += (more, struct((index_heads, LANES), f32))
            else:
                operands += (*early, *(blocks[k] for k in ids[1::2]))
                shapes += (struct((row_parts // 2, tall, index_width), f32),) * 2
                scratch = (pltpu.VMEM(more.shape, bf16), *scratch)
            out = kernel_call(
                functools.partial(grad_kernel, key_total, row_parts, places, not part),
                shapes,
                operands,
                scratch=scratch,
                flops=6 * rows * index_heads * index_width * half * own_keys,
            )
            if part:
                odd.append(out[0])
                early = out[1:]
            else:
                even.append(out[0])
                keep = out[1] if keep is None else keep + out[1]
                send = out[2] if send is None else send + out[2]
    key_sum = even[0] if len(even) == 1 else jnp.concatenate(even)
    key_send = odd[0] if len(odd) == 1 else jnp.concatenate(odd)

    key_got = swap(key_send, row_parts, count)
    row_got = swap(send, row_parts // 2, count)
    bit = 2
    while bit < key_parts:
        key_sum = key_sum + key_got.astype(f32)
        key_got = swap(key_sum[1::2].astype(bf16), row_parts * bit, count)
        key_sum = key_sum[0::2]
        bit *= 2
    row_sum = keep + row_got
    row_got = swap(row_sum[1], 1, count)
    grad_query, grad_weight, key_grad = kernel_call(
        finish_kernel,
        (
            struct((lines, index_width), f32),
            struct((own_rows, index_heads), f32),
            struct((own_keys, index_width), f32),
        ),
        (key_sum[0], key_got[0], row_sum[0], row_got),
    )
    return grad_query.reshape(own_rows, index_heads, index_width), grad_weight, key_grad


def solution(mesh):
    placed = (
        P(("grp", "ctx"), None, None),
        P(("grp", "ctx"), None),
        P(("grp", "ctx"), None),
        P(("grp", "ctx"), None),
        P(("grp", "ctx"), None, None),
        P(("grp", "ctx"), None),
        P(("grp", "ctx")),
    )

    return jax.shard_map(
        body,
        mesh=mesh,
        in_specs=placed,
        out_specs=(P(("grp", "ctx"), None, None), P(("grp", "ctx"), None), P(("grp", "ctx"), None)),
        check_vma=False,
    )
```

```python
import functools

import jax
import jax.numpy as jnp
from jax import lax
from jax.experimental import pallas as pl
from jax.experimental.pallas import tpu as pltpu
from jax.sharding import PartitionSpec as P


ROPE = 64
LANES = 128

f32, bf16 = jnp.float32, jnp.bfloat16
main_scale = 192.0 ** (-0.5)


def kernel_call(kernel, shapes, operands, scratch=(), flops=0):
    nbytes = sum(x.size * x.dtype.itemsize for x in (*operands, *shapes))
    return pl.pallas_call(
        kernel,
        out_shape=tuple(shapes),
        scratch_shapes=list(scratch),
        compiler_params=pltpu.CompilerParams(vmem_limit_bytes=24 << 20),
        cost_estimate=pl.CostEstimate(flops=flops, bytes_accessed=nbytes, transcendentals=0),
    )(*operands)


def contract(left, right, dims):
    return lax.dot_general(left, right, ((dims[:1], dims[1:]), ((), ())), preferred_element_type=f32)


def swap(array, mask, count):
    return lax.ppermute(array, "ctx", [(i, i ^ mask) for i in range(count)])


def swap_gather(block, stride, parts, count):
    held = {0: block}
    bit = parts // 2
    while bit:
        for k, own in list(held.items()):
            held[k ^ bit] = swap(own, stride * bit, count)
        bit //= 2
    return [held[k] for k in range(parts)]


def pack_kernel(
    scales_hbm, keys_hbm, weight_hbm, pos_hbm, main_hbm, query_hbm, codes_hbm, out_ref, query_ref,
    main_ref, codes_ref, scales_ref, weight_ref, pos_ref, sems
):
    groups, own_keys = scales_hbm.shape
    key_count = keys_hbm.shape[0]
    lines = query_hbm.shape[0]
    pairs = (
        (scales_hbm, scales_ref),
        (weight_hbm, weight_ref),
        (pos_hbm, pos_ref),
        (keys_hbm, out_ref.at[pl.ds(0, key_count), :]),
        (query_hbm, query_ref.at[pl.ds(0, lines), :]),
        (main_hbm, main_ref),
        (codes_hbm, codes_ref),
    )
    copies = [pltpu.make_async_copy(a, b, sems.at[n]) for n, (a, b) in enumerate(pairs)]
    for copy in copies:
        copy.start()
    for copy in copies[:3]:
        copy.wait()
    factors = jnp.exp2(scales_ref[...].astype(f32))
    spare = out_ref.shape[0] - key_count - groups
    factors = jnp.concatenate([factors, jnp.zeros((spare, own_keys), f32)], axis=0)
    out_ref[key_count:, :] = factors.astype(bf16)
    own_rows, index_heads = weight_ref.shape
    rest = jnp.concatenate([weight_ref[...], jnp.zeros((own_rows, LANES - index_heads), f32)], axis=1)
    lane = lax.broadcasted_iota(jnp.int32, (1, LANES), 1)
    tail = []
    for part in range(3):
        piece = rest.astype(bf16).astype(f32)
        rest = rest - piece
        for i in range(own_rows):
            pos = jnp.full((1, LANES), pos_ref[i], jnp.int32)
            at = ((pos // LANES) * LANES, pos % LANES, jnp.zeros_like(pos))[part].astype(f32)
            tail.append(jnp.where(lane == index_heads, at, piece[i : i + 1, :]))
    tail.append(jnp.zeros((query_ref.shape[0] - lines - len(tail), LANES), f32))
    query_ref[lines:, :] = jnp.concatenate(tail, axis=0).astype(bf16)
    for copy in copies[3:]:
        copy.wait()


def latent_of(codes_ref, keys_ref, groups):
    latent_width, own_keys = codes_ref.shape
    group_width = (latent_width - ROPE) // groups
    factors = keys_ref[own_keys:, :].astype(f32)
    latent = [
        (codes_ref[g * group_width : (g + 1) * group_width, :].astype(f32) * factors[g : g + 1, :]).astype(bf16)
        for g in range(groups)
    ]
    return jnp.concatenate([*latent, codes_ref[groups * group_width :, :]], axis=0)


def score_kernel(offsets, row_parts, groups, first, *refs):
    parts = len(offsets)
    if first:
        queries, iqueries = refs[:row_parts], refs[row_parts : 2 * row_parts]
        refs = refs[2 * row_parts :]
        codes, blocks, refs = refs[:parts], refs[parts : 2 * parts], refs[2 * parts :]
        exp_ref, index_ref, sums_ref, main_ref, flat_ref, column_ref, pos_ref, side_ref = refs
        own_rows, head_count = queries[0].shape[0], queries[0].shape[2]
        lines = flat_ref.shape[0] // row_parts
        index_heads = lines // own_rows
        for r in range(row_parts):
            tail = iqueries[r][lines:, :].astype(f32)
            side = tail[:own_rows] + tail[own_rows : 2 * own_rows]
            side = side + tail[2 * own_rows : 3 * own_rows]
            side_ref[r * own_rows : (r + 1) * own_rows, :] = side
            flat_ref[r * lines : (r + 1) * lines, :] = iqueries[r][:lines, :]
            for i in range(own_rows):
                t = r * own_rows + i
                main_ref[t * head_count : (t + 1) * head_count, :] = jnp.transpose(queries[r][i])
        side = side_ref[...]
        columns = jnp.transpose(side)
        column_ref[...] = columns[:index_heads, :]
        pos_ref[...] = jnp.broadcast_to(side[:, index_heads : index_heads + 1], pos_ref.shape)
    else:
        main_ref, flat_ref, column_ref, pos_ref = refs[:4]
        codes, blocks = refs[4 : 4 + parts], refs[4 + parts : 4 + 2 * parts]
        exp_ref, index_ref, sums_ref = refs[4 + 2 * parts :]
    rows = pos_ref.shape[0]
    own_rows = rows // row_parts
    index_heads = column_ref.shape[0]
    index_width = flat_ref.shape[1]
    head_count = main_ref.shape[0] // rows
    own_keys = blocks[0].shape[1]
    index_scale = float(index_heads * index_width) ** (-0.5)
    me = lax.axis_index("ctx")
    iota = lax.broadcasted_iota(jnp.int32, (1, own_keys), 1)
    key_pos = [((me ^ (row_parts * k)) * own_keys + iota).astype(f32) for k in offsets]
    key_pos = jnp.concatenate(key_pos, axis=1)
    latent = jnp.concatenate([latent_of(c, b, groups) for c, b in zip(codes, blocks)], axis=1)
    ikeys = jnp.concatenate([b[:own_keys, :] for b in blocks], axis=0)
    dots = contract(flat_ref[...], ikeys, (1, 1))
    scores = contract(main_ref[...], latent, (1, 0))
    sums_ref[...] = jnp.zeros_like(sums_ref)
    for t in range(rows):
        r, i = divmod(t, own_rows)
        visible = key_pos <= pos_ref[t : t + 1, :1]
        heads = jnp.maximum(dots[t * index_heads : (t + 1) * index_heads, :], 0.0)
        score = jnp.sum(column_ref[:, t : t + 1] * heads, axis=0, keepdims=True)
        index_exp = jnp.where(visible, jnp.exp(index_scale * score), 0.0)
        index_ref[t : t + 1, :] = index_exp
        score = scores[t * head_count : (t + 1) * head_count, :] * main_scale
        main_exp = jnp.where(visible, jnp.exp(score), 0.0)
        exp_ref[t] = main_exp
        total = main_exp[:, :own_keys]
        for k in range(1, parts):
            total = total + main_exp[:, k * own_keys : (k + 1) * own_keys]
        sums_ref[r, i : i + 1, :] = jnp.sum(jnp.transpose(total), axis=0, keepdims=True)
        index_total = jnp.sum(index_exp, axis=1, keepdims=True)
        sums_ref[r, own_rows + i : own_rows + i + 1, :] = jnp.broadcast_to(
            index_total, (1, head_count)
        )


def grad_kernel(key_total, row_parts, places, early_count, *refs):
    count = 1 + max(n for n, _ in places)
    near_ref, far_ref, flat_ref, column_ref = refs[:4]
    exps, indexes = refs[4 : 4 + count], refs[4 + count : 4 + 2 * count]
    refs = refs[4 + 2 * count :]
    blocks, refs = refs[: len(places)], refs[len(places) :]
    last = early_count > 0
    if last:
        early_dots, early_columns = refs[:2]
        early_blocks, refs = refs[2 : 2 + early_count], refs[2 + early_count :]
        key_refs, refs = refs[: len(places)], refs[len(places) :]
        keep_ref, send_ref, dots_ref, total_ref = refs
    else:
        key_refs, refs = refs[: len(places)], refs[len(places) :]
        dots_ref, columns_ref, total_ref = refs
    rows, own_rows = total_ref.shape[0], total_ref.shape[0] // row_parts
    index_heads, index_width = column_ref.shape[0], flat_ref.shape[1]
    head_count, own_keys = exps[0].shape[1], key_refs[0].shape[0]
    index_scale = float(index_heads * index_width) ** (-0.5)
    ikeys = jnp.concatenate([b[:own_keys, :] for b in blocks], axis=0)
    flat = flat_ref[...]
    dots = contract(flat, ikeys, (1, 1))
    for r in range(row_parts):
        lines = slice(0, own_rows)
        total_ref[r * own_rows : (r + 1) * own_rows, :] = near_ref[r, lines, :] + far_ref[r ^ 1, lines, :]
    shares = jnp.transpose(1.0 / total_ref[...])
    lane = lax.broadcasted_iota(jnp.int32, (index_heads, LANES), 1)
    columns = early_columns[...] if last else jnp.zeros((index_heads, LANES), f32)
    for t in range(rows):
        r, i = divmod(t, own_rows)
        share = shares[:, t : t + 1]
        at = own_rows + i
        index_total = near_ref[r, at : at + 1, :1] + far_ref[r ^ 1, at : at + 1, :1]
        target = jnp.concatenate(
            [
                jnp.sum(exps[n][t, :, p : p + own_keys] * share, axis=0, keepdims=True)
                for n, p in places
            ],
            axis=1,
        )
        index_exp = jnp.concatenate(
            [indexes[n][t : t + 1, p : p + own_keys] for n, p in places], axis=1
        )
        gradient = key_total * (index_exp / index_total - target / head_count)
        heads = dots[t * index_heads : (t + 1) * index_heads, :]
        column = index_scale * jnp.sum(gradient * jnp.maximum(heads, 0.0), axis=1, keepdims=True)
        columns = jnp.where(lane == t, columns + column, columns)
        weight = column_ref[:, t : t + 1]
        grad_dots = jnp.where(heads > 0, index_scale * gradient * weight, 0.0).astype(bf16)
        dots_ref[t * index_heads : (t + 1) * index_heads, :] = grad_dots
    grad_dots = dots_ref[...]
    key_grad = contract(grad_dots, flat, (0, 0))
    for k, key_ref in enumerate(key_refs):
        key_ref[...] = key_grad[k * own_keys : (k + 1) * own_keys, :].astype(key_ref.dtype)
    if not last:
        columns_ref[...] = columns
        return
    early_keys = jnp.concatenate([b[:own_keys, :] for b in early_blocks], axis=0)
    grad_query = contract(grad_dots, ikeys, (1, 0)) + contract(early_dots[...], early_keys, (1, 0))
    weights = jnp.transpose(jnp.concatenate([columns, jnp.zeros_like(columns)], axis=0)[:LANES])
    lines = own_rows * index_heads
    for r in range(row_parts):
        out, at = (keep_ref, r) if r < row_parts // 2 else (send_ref, r - row_parts // 2)
        out[at, :lines, :] = grad_query[r * lines : (r + 1) * lines, :]
        out[at, lines : lines + own_rows, :] = weights[r * own_rows : (r + 1) * own_rows, :]


def finish_kernel(parts, *refs):
    key_refs, (row_ref, row_got_ref, query_ref, weight_ref, key_out_ref) = refs[:parts], refs[parts:]
    lines = query_ref.shape[0]
    own_rows, index_heads = weight_ref.shape
    total = key_refs[0][...].astype(f32)
    for ref in key_refs[1:]:
        total = total + ref[...].astype(f32)
    key_out_ref[...] = total
    query_ref[...] = row_ref[:lines, :] + row_got_ref[:lines, :]
    tail = slice(lines, lines + own_rows)
    weight_ref[...] = (row_ref[tail, :] + row_got_ref[tail, :])[:, :index_heads]


def body(query_main, key_codes, key_scales, index_keys, index_query, index_weight, query_pos):
    own_rows, head_count, latent_width = query_main.shape
    index_heads, index_width = index_query.shape[1:]
    own_keys = key_codes.shape[0]
    count = lax.axis_size("ctx")
    row_parts = 4
    key_parts = count // row_parts
    key_total = own_keys * count
    rows = own_rows * row_parts
    lines = own_rows * index_heads
    tall = lines + 8
    struct = jax.ShapeDtypeStruct

    codes = key_codes.T
    groups = key_scales.shape[1]
    main_raw = jnp.transpose(query_main, (0, 2, 1))
    sources = (
        key_scales.T,
        index_keys,
        index_weight,
        query_pos,
        main_raw,
        index_query.reshape(lines, index_width),
        codes,
    )
    key_pack, index_own, main_own, codes_own = pl.pallas_call(
        pack_kernel,
        out_shape=(
            struct((own_keys + 16, own_keys), bf16),
            struct((lines + 16, index_width), bf16),
            struct(main_raw.shape, bf16),
            struct(codes.shape, bf16),
        ),
        in_specs=[pl.BlockSpec(memory_space=pltpu.HBM)] * len(sources),
        scratch_shapes=[
            pltpu.VMEM((groups, own_keys), jnp.int32),
            pltpu.VMEM((own_rows, index_heads), f32),
            pltpu.SMEM((own_rows,), jnp.int32),
            pltpu.SemaphoreType.DMA((len(sources),)),
        ],
        compiler_params=pltpu.CompilerParams(vmem_limit_bytes=8 << 20),
        name="pack",
    )(*(pltpu.with_memory_space_constraint(x, pltpu.HBM) for x in sources))
    codes = swap_gather(codes, row_parts, key_parts, count)
    codes[0] = codes_own
    blocks = [key_pack]
    for k in range(1, key_parts):
        blocks.append(swap(key_pack, row_parts * k, count))
    queries = swap_gather(main_raw, 1, row_parts, count)
    queries[0] = main_own
    iqueries = swap_gather(index_own, 1, row_parts, count)

    step = 4
    if key_parts <= step:
        pieces = [list(range(key_parts - 1)), [key_parts - 1]]
    else:
        pieces = [list(range(k, k + step)) for k in range(0, key_parts, step)]
    exps, indexes, sums, laid = [], [], None, None
    for n, piece in enumerate(pieces):
        wide = len(piece) * own_keys
        shapes = (
            struct((rows, head_count, wide), f32),
            struct((rows, wide), f32),
            struct((row_parts, 2 * own_rows, head_count), f32),
        )
        if n == 0:
            shapes += (
                struct((rows * head_count, latent_width), bf16),
                struct((rows * index_heads, index_width), bf16),
                struct((index_heads, rows), f32),
                struct((rows, LANES), f32),
            )
        out = kernel_call(
            functools.partial(score_kernel, tuple(piece), row_parts, groups, n == 0),
            shapes,
            (
                *(laid or (*queries, *iqueries)),
                *(codes[k] for k in piece),
                *(blocks[k] for k in piece),
            ),
            scratch=(pltpu.VMEM((rows, LANES), f32),) if n == 0 else (),
            flops=2 * rows * head_count * latent_width * wide,
        )
        laid = laid or out[3:]
        exps.append(out[0])
        indexes.append(out[1])
        sums = out[2] if sums is None else sums + out[2]

    bit = row_parts // 2
    while bit > 1:
        got = swap(sums, bit, count)
        sums = sums + jnp.stack([got[r ^ bit] for r in range(row_parts)])
        bit //= 2
    got = swap(sums, 1, count)

    place = {k: (n, p * own_keys) for n, piece in enumerate(pieces) for p, k in enumerate(piece)}
    teams = [list(range(key_parts))] if key_parts <= step else pieces
    found, keep, send = {}, None, None
    for ids in teams:
        early = None
        for part, mine in enumerate((ids[3:], ids[:3])):
            used = sorted({place[k][0] for k in mine})
            places = tuple((used.index(place[k][0]), place[k][1]) for k in mine)
            operands = (
                sums,
                got,
                *laid[1:3],
                *(exps[n] for n in used),
                *(indexes[n] for n in used),
                *(blocks[k] for k in mine),
            )
            shapes = tuple(
                struct((own_keys, index_width), bf16 if k % 2 else f32) for k in mine
            )
            more = struct((rows * index_heads, len(mine) * own_keys), bf16)
            scratch = (pltpu.VMEM((rows, head_count), f32),)
            if part == 0:
                shapes += (more, struct((index_heads, LANES), f32))
            else:
                operands += (*early, *(blocks[k] for k in ids[3:]))
                shapes += (struct((row_parts // 2, tall, index_width), f32),) * 2
                scratch = (pltpu.VMEM(more.shape, bf16), *scratch)
            out = kernel_call(
                functools.partial(grad_kernel, key_total, row_parts, places, len(ids[3:]) * part),
                shapes,
                operands,
                scratch=scratch,
                flops=6 * rows * index_heads * index_width * len(mine) * own_keys,
            )
            found.update(zip(mine, out))
            if part == 0:
                early = out[len(mine) :]
            else:
                keep = out[-2] if keep is None else keep + out[-2]
                send = out[-1] if send is None else send + out[-1]
    pick = lambda n: jnp.stack([found[k] for k in range(n, key_parts, 4)]) if key_parts > 4 else found[n]
    key_got = swap(pick(3), row_parts, count)
    near_got = swap(pick(1), row_parts, count)
    row_got = swap(send, row_parts // 2, count)
    key_sum = (pick(2) + key_got.astype(f32)).astype(bf16)
    key_got = swap(key_sum, 2 * row_parts, count)
    key_sums = (pick(0), near_got, key_got)
    bit = 4
    while bit < key_parts:
        key_sum = sum(x.astype(f32) for x in key_sums)
        key_got = swap(key_sum[1::2].astype(bf16), row_parts * bit, count)
        key_sums = (key_sum[0::2], key_got)
        bit *= 2
    if key_parts > 4:
        key_sums = tuple(x[0] for x in key_sums)
    row_sum = keep + row_got
    row_got = swap(row_sum[1], 1, count)
    grad_query, grad_weight, key_grad = kernel_call(
        functools.partial(finish_kernel, len(key_sums)),
        (
            struct((lines, index_width), f32),
            struct((own_rows, index_heads), f32),
            struct((own_keys, index_width), f32),
        ),
        (*key_sums, row_sum[0], row_got),
    )
    return grad_query.reshape(own_rows, index_heads, index_width), grad_weight, key_grad


def solution(mesh):
    placed = (
        P(("grp", "ctx"), None, None),
        P(("grp", "ctx"), None),
        P(("grp", "ctx"), None),
        P(("grp", "ctx"), None),
        P(("grp", "ctx"), None, None),
        P(("grp", "ctx"), None),
        P(("grp", "ctx")),
    )

    return jax.shard_map(
        body,
        mesh=mesh,
        in_specs=placed,
        out_specs=(P(("grp", "ctx"), None, None), P(("grp", "ctx"), None), P(("grp", "ctx"), None)),
        check_vma=False,
    )
```

```python
import functools

import jax
import jax.numpy as jnp
from jax import lax
from jax.experimental import pallas as pl
from jax.experimental.pallas import tpu as pltpu
from jax.sharding import PartitionSpec as P


ROPE = 64
LANES = 128

f32, bf16 = jnp.float32, jnp.bfloat16
main_scale = 192.0 ** (-0.5)


def kernel_call(kernel, shapes, operands, scratch=(), flops=0):
    nbytes = sum(x.size * x.dtype.itemsize for x in (*operands, *shapes))
    return pl.pallas_call(
        kernel,
        out_shape=tuple(shapes),
        scratch_shapes=list(scratch),
        compiler_params=pltpu.CompilerParams(vmem_limit_bytes=24 << 20),
        cost_estimate=pl.CostEstimate(flops=flops, bytes_accessed=nbytes, transcendentals=0),
    )(*operands)


def contract(left, right, dims):
    return lax.dot_general(left, right, ((dims[:1], dims[1:]), ((), ())), preferred_element_type=f32)


def swap(array, mask, count):
    return lax.ppermute(array, "ctx", [(i, i ^ mask) for i in range(count)])


def swap_gather(block, stride, parts, count):
    held = {0: block}
    bit = parts // 2
    while bit:
        for k, own in list(held.items()):
            held[k ^ bit] = swap(own, stride * bit, count)
        bit //= 2
    return [held[k] for k in range(parts)]


def pack_kernel(
    scales_hbm, keys_hbm, weight_hbm, pos_hbm, main_hbm, query_hbm, codes_hbm, out_ref, query_ref,
    main_ref, codes_ref, scales_ref, weight_ref, pos_ref, sems
):
    groups, own_keys = scales_hbm.shape
    key_count = keys_hbm.shape[0]
    lines = query_hbm.shape[0]
    pairs = (
        (scales_hbm, scales_ref),
        (weight_hbm, weight_ref),
        (pos_hbm, pos_ref),
        (keys_hbm, out_ref.at[pl.ds(0, key_count), :]),
        (query_hbm, query_ref.at[pl.ds(0, lines), :]),
        (main_hbm, main_ref),
        (codes_hbm, codes_ref),
    )
    copies = [pltpu.make_async_copy(a, b, sems.at[n]) for n, (a, b) in enumerate(pairs)]
    for copy in copies:
        copy.start()
    for copy in copies[:3]:
        copy.wait()
    factors = jnp.exp2(scales_ref[...].astype(f32))
    spare = out_ref.shape[0] - key_count - groups
    factors = jnp.concatenate([factors, jnp.zeros((spare, own_keys), f32)], axis=0)
    out_ref[key_count:, :] = factors.astype(bf16)
    own_rows, index_heads = weight_ref.shape
    rest = jnp.concatenate([weight_ref[...], jnp.zeros((own_rows, LANES - index_heads), f32)], axis=1)
    lane = lax.broadcasted_iota(jnp.int32, (1, LANES), 1)
    tail = []
    for part in range(3):
        piece = rest.astype(bf16).astype(f32)
        rest = rest - piece
        for i in range(own_rows):
            pos = jnp.full((1, LANES), pos_ref[i], jnp.int32)
            at = ((pos // LANES) * LANES, pos % LANES, jnp.zeros_like(pos))[part].astype(f32)
            tail.append(jnp.where(lane == index_heads, at, piece[i : i + 1, :]))
    tail.append(jnp.zeros((query_ref.shape[0] - lines - len(tail), LANES), f32))
    query_ref[lines:, :] = jnp.concatenate(tail, axis=0).astype(bf16)
    for copy in copies[3:]:
        copy.wait()


def latent_of(codes_ref, keys_ref, groups):
    latent_width, own_keys = codes_ref.shape
    group_width = (latent_width - ROPE) // groups
    factors = keys_ref[own_keys:, :].astype(f32)
    latent = [
        (codes_ref[g * group_width : (g + 1) * group_width, :].astype(f32) * factors[g : g + 1, :]).astype(bf16)
        for g in range(groups)
    ]
    return jnp.concatenate([*latent, codes_ref[groups * group_width :, :]], axis=0)


def score_kernel(offsets, row_parts, groups, first, *refs):
    parts = len(offsets)
    if first:
        queries, iqueries = refs[:row_parts], refs[row_parts : 2 * row_parts]
        refs = refs[2 * row_parts :]
        codes, blocks, refs = refs[:parts], refs[parts : 2 * parts], refs[2 * parts :]
        exp_ref, index_ref, sums_ref, main_ref, flat_ref, column_ref, pos_ref, side_ref = refs
        own_rows, head_count = queries[0].shape[0], queries[0].shape[2]
        lines = flat_ref.shape[0] // row_parts
        index_heads = lines // own_rows
        for r in range(row_parts):
            tail = iqueries[r][lines:, :].astype(f32)
            side = tail[:own_rows] + tail[own_rows : 2 * own_rows]
            side = side + tail[2 * own_rows : 3 * own_rows]
            side_ref[r * own_rows : (r + 1) * own_rows, :] = side
            flat_ref[r * lines : (r + 1) * lines, :] = iqueries[r][:lines, :]
            for i in range(own_rows):
                t = r * own_rows + i
                main_ref[t * head_count : (t + 1) * head_count, :] = jnp.transpose(queries[r][i])
        side = side_ref[...]
        columns = jnp.transpose(side)
        column_ref[...] = columns[:index_heads, :]
        pos_ref[...] = jnp.broadcast_to(side[:, index_heads : index_heads + 1], pos_ref.shape)
    else:
        main_ref, flat_ref, column_ref, pos_ref = refs[:4]
        codes, blocks = refs[4 : 4 + parts], refs[4 + parts : 4 + 2 * parts]
        exp_ref, index_ref, sums_ref = refs[4 + 2 * parts :]
    rows = pos_ref.shape[0]
    own_rows = rows // row_parts
    index_heads = column_ref.shape[0]
    index_width = flat_ref.shape[1]
    head_count = main_ref.shape[0] // rows
    own_keys = blocks[0].shape[1]
    index_scale = float(index_heads * index_width) ** (-0.5)
    me = lax.axis_index("ctx")
    iota = lax.broadcasted_iota(jnp.int32, (1, own_keys), 1)
    key_pos = [((me ^ (row_parts * k)) * own_keys + iota).astype(f32) for k in offsets]
    key_pos = jnp.concatenate(key_pos, axis=1)
    latent = jnp.concatenate([latent_of(c, b, groups) for c, b in zip(codes, blocks)], axis=1)
    ikeys = jnp.concatenate([b[:own_keys, :] for b in blocks], axis=0)
    dots = contract(flat_ref[...], ikeys, (1, 1))
    scores = contract(main_ref[...], latent, (1, 0))
    sums_ref[...] = jnp.zeros_like(sums_ref)
    for t in range(rows):
        r, i = divmod(t, own_rows)
        visible = key_pos <= pos_ref[t : t + 1, :1]
        heads = jnp.maximum(dots[t * index_heads : (t + 1) * index_heads, :], 0.0)
        score = jnp.sum(column_ref[:, t : t + 1] * heads, axis=0, keepdims=True)
        index_exp = jnp.where(visible, jnp.exp(index_scale * score), 0.0)
        index_ref[t : t + 1, :] = index_exp
        score = scores[t * head_count : (t + 1) * head_count, :] * main_scale
        main_exp = jnp.where(visible, jnp.exp(score), 0.0)
        exp_ref[t] = main_exp
        total = main_exp[:, :own_keys]
        for k in range(1, parts):
            total = total + main_exp[:, k * own_keys : (k + 1) * own_keys]
        sums_ref[r, i : i + 1, :] = jnp.sum(jnp.transpose(total), axis=0, keepdims=True)
        index_total = jnp.sum(index_exp, axis=1, keepdims=True)
        sums_ref[r, own_rows + i : own_rows + i + 1, :] = jnp.broadcast_to(
            index_total, (1, head_count)
        )


def grad_kernel(key_total, row_parts, places, early_count, *refs):
    count = 1 + max(n for n, _ in places)
    near_ref, far_ref, flat_ref, column_ref = refs[:4]
    exps, indexes = refs[4 : 4 + count], refs[4 + count : 4 + 2 * count]
    refs = refs[4 + 2 * count :]
    blocks, refs = refs[: len(places)], refs[len(places) :]
    last = early_count > 0
    if last:
        early_dots, early_columns = refs[:2]
        early_blocks, refs = refs[2 : 2 + early_count], refs[2 + early_count :]
        key_refs, refs = refs[: len(places)], refs[len(places) :]
        keep_ref, send_ref, dots_ref, total_ref = refs
    else:
        key_refs, refs = refs[: len(places)], refs[len(places) :]
        dots_ref, columns_ref, total_ref = refs
    rows, own_rows = total_ref.shape[0], total_ref.shape[0] // row_parts
    index_heads, index_width = column_ref.shape[0], flat_ref.shape[1]
    head_count, own_keys = exps[0].shape[1], key_refs[0].shape[0]
    index_scale = float(index_heads * index_width) ** (-0.5)
    ikeys = jnp.concatenate([b[:own_keys, :] for b in blocks], axis=0)
    flat = flat_ref[...]
    dots = contract(flat, ikeys, (1, 1))
    for r in range(row_parts):
        lines = slice(0, own_rows)
        total_ref[r * own_rows : (r + 1) * own_rows, :] = near_ref[r, lines, :] + far_ref[r ^ 1, lines, :]
    shares = jnp.transpose(1.0 / total_ref[...])
    lane = lax.broadcasted_iota(jnp.int32, (index_heads, LANES), 1)
    columns = early_columns[...] if last else jnp.zeros((index_heads, LANES), f32)
    for t in range(rows):
        r, i = divmod(t, own_rows)
        share = shares[:, t : t + 1]
        at = own_rows + i
        index_total = near_ref[r, at : at + 1, :1] + far_ref[r ^ 1, at : at + 1, :1]
        target = jnp.concatenate(
            [
                jnp.sum(exps[n][t, :, p : p + own_keys] * share, axis=0, keepdims=True)
                for n, p in places
            ],
            axis=1,
        )
        index_exp = jnp.concatenate(
            [indexes[n][t : t + 1, p : p + own_keys] for n, p in places], axis=1
        )
        gradient = key_total * (index_exp / index_total - target / head_count)
        heads = dots[t * index_heads : (t + 1) * index_heads, :]
        column = index_scale * jnp.sum(gradient * jnp.maximum(heads, 0.0), axis=1, keepdims=True)
        columns = jnp.where(lane == t, columns + column, columns)
        weight = column_ref[:, t : t + 1]
        grad_dots = jnp.where(heads > 0, index_scale * gradient * weight, 0.0).astype(bf16)
        dots_ref[t * index_heads : (t + 1) * index_heads, :] = grad_dots
    grad_dots = dots_ref[...]
    key_grad = contract(grad_dots, flat, (0, 0))
    for k, key_ref in enumerate(key_refs):
        key_ref[...] = key_grad[k * own_keys : (k + 1) * own_keys, :].astype(key_ref.dtype)
    if not last:
        columns_ref[...] = columns
        return
    early_keys = jnp.concatenate([b[:own_keys, :] for b in early_blocks], axis=0)
    grad_query = contract(grad_dots, ikeys, (1, 0)) + contract(early_dots[...], early_keys, (1, 0))
    weights = jnp.transpose(jnp.concatenate([columns, jnp.zeros_like(columns)], axis=0)[:LANES])
    lines = own_rows * index_heads
    weights = jnp.concatenate([weights, jnp.zeros((16, LANES), f32)], axis=0)
    for r in range(row_parts):
        out, at = (keep_ref, r) if r < row_parts // 2 else (send_ref, r - row_parts // 2)
        out[at, :lines, :] = grad_query[r * lines : (r + 1) * lines, :].astype(out.dtype)
        tail = weights[r * own_rows : r * own_rows + out.shape[1] - lines, :]
        out[at, lines:, :] = tail.astype(out.dtype)


def finish_kernel(parts, *refs):
    key_refs, (row_ref, row_got_ref, query_ref, weight_ref, key_out_ref) = refs[:parts], refs[parts:]
    lines = query_ref.shape[0]
    own_rows, index_heads = weight_ref.shape
    total = key_refs[0][...].astype(f32)
    for ref in key_refs[1:]:
        total = total + ref[...].astype(f32)
    key_out_ref[...] = total
    query_ref[...] = row_ref[:lines, :] + row_got_ref[:lines, :]
    tail = slice(lines, lines + own_rows)
    weight_ref[...] = (row_ref[tail, :] + row_got_ref[tail, :])[:, :index_heads]


def body(query_main, key_codes, key_scales, index_keys, index_query, index_weight, query_pos):
    own_rows, head_count, latent_width = query_main.shape
    index_heads, index_width = index_query.shape[1:]
    own_keys = key_codes.shape[0]
    count = lax.axis_size("ctx")
    row_parts = 4
    key_parts = count // row_parts
    key_total = own_keys * count
    rows = own_rows * row_parts
    lines = own_rows * index_heads
    tall = lines + 16
    struct = jax.ShapeDtypeStruct

    codes = key_codes.T
    groups = key_scales.shape[1]
    main_raw = jnp.transpose(query_main, (0, 2, 1))
    sources = (
        key_scales.T,
        index_keys,
        index_weight,
        query_pos,
        main_raw,
        index_query.reshape(lines, index_width),
        codes,
    )
    key_pack, index_own, main_own, codes_own = pl.pallas_call(
        pack_kernel,
        out_shape=(
            struct((own_keys + 16, own_keys), bf16),
            struct((lines + 16, index_width), bf16),
            struct(main_raw.shape, bf16),
            struct(codes.shape, bf16),
        ),
        in_specs=[pl.BlockSpec(memory_space=pltpu.HBM)] * len(sources),
        scratch_shapes=[
            pltpu.VMEM((groups, own_keys), jnp.int32),
            pltpu.VMEM((own_rows, index_heads), f32),
            pltpu.SMEM((own_rows,), jnp.int32),
            pltpu.SemaphoreType.DMA((len(sources),)),
        ],
        compiler_params=pltpu.CompilerParams(vmem_limit_bytes=8 << 20),
        name="pack",
    )(*(pltpu.with_memory_space_constraint(x, pltpu.HBM) for x in sources))
    codes = swap_gather(codes, row_parts, key_parts, count)
    codes[0] = codes_own
    blocks = swap_gather(key_pack, row_parts, key_parts, count)
    queries = swap_gather(main_raw, 1, row_parts, count)
    queries[0] = main_own
    iqueries = swap_gather(index_own, 1, row_parts, count)

    step = 4
    if key_parts <= step:
        pieces = [list(range(key_parts - 1)), [key_parts - 1]]
    else:
        pieces = [list(range(k, k + step)) for k in range(0, key_parts, step)]
    exps, indexes, sums, laid = [], [], None, None
    for n, piece in enumerate(pieces):
        wide = len(piece) * own_keys
        shapes = (
            struct((rows, head_count, wide), f32),
            struct((rows, wide), f32),
            struct((row_parts, 2 * own_rows, head_count), f32),
        )
        if n == 0:
            shapes += (
                struct((rows * head_count, latent_width), bf16),
                struct((rows * index_heads, index_width), bf16),
                struct((index_heads, rows), f32),
                struct((rows, LANES), f32),
            )
        out = kernel_call(
            functools.partial(score_kernel, tuple(piece), row_parts, groups, n == 0),
            shapes,
            (
                *(laid or (*queries, *iqueries)),
                *(codes[k] for k in piece),
                *(blocks[k] for k in piece),
            ),
            scratch=(pltpu.VMEM((rows, LANES), f32),) if n == 0 else (),
            flops=2 * rows * head_count * latent_width * wide,
        )
        laid = laid or out[3:]
        exps.append(out[0])
        indexes.append(out[1])
        sums = out[2] if sums is None else sums + out[2]

    bit = row_parts // 2
    while bit > 1:
        got = swap(sums, bit, count)
        sums = sums + jnp.stack([got[r ^ bit] for r in range(row_parts)])
        bit //= 2
    got = swap(sums, 1, count)

    place = {k: (n, p * own_keys) for n, piece in enumerate(pieces) for p, k in enumerate(piece)}
    teams = [list(range(key_parts))] if key_parts <= step else pieces
    found, keep, send = {}, None, None
    for ids in teams:
        early = None
        for part, mine in enumerate((ids[3:], ids[:3])):
            used = sorted({place[k][0] for k in mine})
            places = tuple((used.index(place[k][0]), place[k][1]) for k in mine)
            operands = (
                sums,
                got,
                *laid[1:3],
                *(exps[n] for n in used),
                *(indexes[n] for n in used),
                *(blocks[k] for k in mine),
            )
            shapes = tuple(
                struct((own_keys, index_width), bf16 if k % 2 else f32) for k in mine
            )
            more = struct((rows * index_heads, len(mine) * own_keys), bf16)
            scratch = (pltpu.VMEM((rows, head_count), f32),)
            if part == 0:
                shapes += (more, struct((index_heads, LANES), f32))
            else:
                operands += (*early, *(blocks[k] for k in ids[3:]))
                shapes += tuple(
                    struct((row_parts // 2, tall, index_width), kind) for kind in (f32, bf16)
                )
                scratch = (pltpu.VMEM(more.shape, bf16), *scratch)
            out = kernel_call(
                functools.partial(grad_kernel, key_total, row_parts, places, len(ids[3:]) * part),
                shapes,
                operands,
                scratch=scratch,
                flops=6 * rows * index_heads * index_width * len(mine) * own_keys,
            )
            found.update(zip(mine, out))
            if part == 0:
                early = out[len(mine) :]
            else:
                keep = out[-2] if keep is None else keep + out[-2]
                send = out[-1] if send is None else send + out[-1]
    pick = lambda n: jnp.stack([found[k] for k in range(n, key_parts, 4)]) if key_parts > 4 else found[n]
    key_got = swap(pick(3), row_parts, count)
    near_got = swap(pick(1), row_parts, count)
    row_got = swap(send, row_parts // 2, count)
    key_sum = (pick(2) + key_got.astype(f32)).astype(bf16)
    key_got = swap(key_sum, 2 * row_parts, count)
    key_sums = (pick(0), near_got, key_got)
    bit = 4
    while bit < key_parts:
        key_sum = sum(x.astype(f32) for x in key_sums)
        key_got = swap(key_sum[1::2].astype(bf16), row_parts * bit, count)
        key_sums = (key_sum[0::2], key_got)
        bit *= 2
    if key_parts > 4:
        key_sums = tuple(x[0] for x in key_sums)
    row_sum = keep + row_got.astype(f32)
    row_got = swap(row_sum[1], 1, count)
    grad_query, grad_weight, key_grad = kernel_call(
        functools.partial(finish_kernel, len(key_sums)),
        (
            struct((lines, index_width), f32),
            struct((own_rows, index_heads), f32),
            struct((own_keys, index_width), f32),
        ),
        (*key_sums, row_sum[0], row_got),
    )
    return grad_query.reshape(own_rows, index_heads, index_width), grad_weight, key_grad


def solution(mesh):
    placed = (
        P(("grp", "ctx"), None, None),
        P(("grp", "ctx"), None),
        P(("grp", "ctx"), None),
        P(("grp", "ctx"), None),
        P(("grp", "ctx"), None, None),
        P(("grp", "ctx"), None),
        P(("grp", "ctx")),
    )

    return jax.shard_map(
        body,
        mesh=mesh,
        in_specs=placed,
        out_specs=(P(("grp", "ctx"), None, None), P(("grp", "ctx"), None), P(("grp", "ctx"), None)),
        check_vma=False,
    )
```

```python
import functools

import jax
import jax.numpy as jnp
from jax import lax
from jax.experimental import pallas as pl
from jax.experimental.pallas import tpu as pltpu
from jax.sharding import PartitionSpec as P


ROPE = 64
LANES = 128

f32, bf16 = jnp.float32, jnp.bfloat16
main_scale = 192.0 ** (-0.5)


def kernel_call(kernel, shapes, operands, scratch=(), flops=0):
    nbytes = sum(x.size * x.dtype.itemsize for x in (*operands, *shapes))
    return pl.pallas_call(
        kernel,
        out_shape=tuple(shapes),
        scratch_shapes=list(scratch),
        compiler_params=pltpu.CompilerParams(vmem_limit_bytes=24 << 20),
        cost_estimate=pl.CostEstimate(flops=flops, bytes_accessed=nbytes, transcendentals=0),
    )(*operands)


def contract(left, right, dims):
    return lax.dot_general(left, right, ((dims[:1], dims[1:]), ((), ())), preferred_element_type=f32)


def swap(array, mask, count):
    return lax.ppermute(array, "ctx", [(i, i ^ mask) for i in range(count)])


def swap_gather(block, stride, parts, count):
    held = {0: block}
    bit = parts // 2
    while bit:
        for k, own in list(held.items()):
            held[k ^ bit] = swap(own, stride * bit, count)
        bit //= 2
    return [held[k] for k in range(parts)]


def pack_kernel(
    scales_hbm, keys_hbm, weight_hbm, pos_hbm, main_hbm, query_hbm, codes_hbm, out_ref, query_ref,
    main_ref, codes_ref, scales_ref, weight_ref, pos_ref, sems
):
    groups, own_keys = scales_hbm.shape
    key_count = keys_hbm.shape[0]
    lines = query_hbm.shape[0]
    pairs = (
        (scales_hbm, scales_ref),
        (weight_hbm, weight_ref),
        (pos_hbm, pos_ref),
        (keys_hbm, out_ref.at[pl.ds(0, key_count), :]),
        (query_hbm, query_ref.at[pl.ds(0, lines), :]),
        (main_hbm, main_ref),
        (codes_hbm, codes_ref),
    )
    copies = [pltpu.make_async_copy(a, b, sems.at[n]) for n, (a, b) in enumerate(pairs)]
    for copy in copies:
        copy.start()
    for copy in copies[:3]:
        copy.wait()
    factors = jnp.exp2(scales_ref[...].astype(f32))
    spare = out_ref.shape[0] - key_count - groups
    factors = jnp.concatenate([factors, jnp.zeros((spare, own_keys), f32)], axis=0)
    out_ref[key_count:, :] = factors.astype(bf16)
    own_rows, index_heads = weight_ref.shape
    rest = jnp.concatenate([weight_ref[...], jnp.zeros((own_rows, LANES - index_heads), f32)], axis=1)
    lane = lax.broadcasted_iota(jnp.int32, (1, LANES), 1)
    tail = []
    for part in range(3):
        piece = rest.astype(bf16).astype(f32)
        rest = rest - piece
        for i in range(own_rows):
            pos = jnp.full((1, LANES), pos_ref[i], jnp.int32)
            at = ((pos // LANES) * LANES, pos % LANES, jnp.zeros_like(pos))[part].astype(f32)
            tail.append(jnp.where(lane == index_heads, at, piece[i : i + 1, :]))
    tail.append(jnp.zeros((query_ref.shape[0] - lines - len(tail), LANES), f32))
    query_ref[lines:, :] = jnp.concatenate(tail, axis=0).astype(bf16)
    for copy in copies[3:]:
        copy.wait()


def latent_of(codes_ref, keys_ref, groups):
    latent_width, own_keys = codes_ref.shape
    group_width = (latent_width - ROPE) // groups
    factors = keys_ref[own_keys:, :].astype(f32)
    latent = [
        (codes_ref[g * group_width : (g + 1) * group_width, :].astype(f32) * factors[g : g + 1, :]).astype(bf16)
        for g in range(groups)
    ]
    return jnp.concatenate([*latent, codes_ref[groups * group_width :, :]], axis=0)


def score_kernel(offsets, row_parts, groups, first, *refs):
    parts = len(offsets)
    if first:
        queries, iqueries = refs[:row_parts], refs[row_parts : 2 * row_parts]
        refs = refs[2 * row_parts :]
        codes, blocks, refs = refs[:parts], refs[parts : 2 * parts], refs[2 * parts :]
        exp_ref, index_ref, sums_ref, main_ref, flat_ref, column_ref, pos_ref, side_ref = refs
        own_rows, head_count = queries[0].shape[0], queries[0].shape[2]
        lines = flat_ref.shape[0] // row_parts
        index_heads = lines // own_rows
        for r in range(row_parts):
            tail = iqueries[r][lines:, :].astype(f32)
            side = tail[:own_rows] + tail[own_rows : 2 * own_rows]
            side = side + tail[2 * own_rows : 3 * own_rows]
            side_ref[r * own_rows : (r + 1) * own_rows, :] = side
            flat_ref[r * lines : (r + 1) * lines, :] = iqueries[r][:lines, :]
            for i in range(own_rows):
                t = r * own_rows + i
                main_ref[t * head_count : (t + 1) * head_count, :] = jnp.transpose(queries[r][i])
        side = side_ref[...]
        columns = jnp.transpose(side)
        column_ref[...] = columns[:index_heads, :]
        pos_ref[...] = jnp.broadcast_to(side[:, index_heads : index_heads + 1], pos_ref.shape)
    else:
        main_ref, flat_ref, column_ref, pos_ref = refs[:4]
        codes, blocks = refs[4 : 4 + parts], refs[4 + parts : 4 + 2 * parts]
        exp_ref, index_ref, sums_ref = refs[4 + 2 * parts :]
    rows = pos_ref.shape[0]
    own_rows = rows // row_parts
    index_heads = column_ref.shape[0]
    index_width = flat_ref.shape[1]
    head_count = main_ref.shape[0] // rows
    own_keys = blocks[0].shape[1]
    index_scale = float(index_heads * index_width) ** (-0.5)
    me = lax.axis_index("ctx")
    iota = lax.broadcasted_iota(jnp.int32, (1, own_keys), 1)
    key_pos = [((me ^ (row_parts * k)) * own_keys + iota).astype(f32) for k in offsets]
    key_pos = jnp.concatenate(key_pos, axis=1)
    latent = jnp.concatenate([latent_of(c, b, groups) for c, b in zip(codes, blocks)], axis=1)
    ikeys = jnp.concatenate([b[:own_keys, :] for b in blocks], axis=0)
    dots = contract(flat_ref[...], ikeys, (1, 1))
    scores = contract(main_ref[...], latent, (1, 0))
    sums_ref[...] = jnp.zeros_like(sums_ref)
    for t in range(rows):
        r, i = divmod(t, own_rows)
        visible = key_pos <= pos_ref[t : t + 1, :1]
        heads = jnp.maximum(dots[t * index_heads : (t + 1) * index_heads, :], 0.0)
        score = jnp.sum(column_ref[:, t : t + 1] * heads, axis=0, keepdims=True)
        index_exp = jnp.where(visible, jnp.exp(index_scale * score), 0.0)
        index_ref[t : t + 1, :] = index_exp
        score = scores[t * head_count : (t + 1) * head_count, :] * main_scale
        main_exp = jnp.where(visible, jnp.exp(score), 0.0)
        exp_ref[t] = main_exp
        total = main_exp[:, :own_keys]
        for k in range(1, parts):
            total = total + main_exp[:, k * own_keys : (k + 1) * own_keys]
        sums_ref[r, i : i + 1, :] = jnp.sum(jnp.transpose(total), axis=0, keepdims=True)
        index_total = jnp.sum(index_exp, axis=1, keepdims=True)
        sums_ref[r, own_rows + i : own_rows + i + 1, :] = jnp.broadcast_to(
            index_total, (1, head_count)
        )


def prepare_kernel(flat_ref, column_ref, *refs):
    blocks, (heads_ref, masked_ref) = refs[:-2], refs[-2:]
    index_heads, rows = column_ref.shape
    own_keys = heads_ref.shape[1] // len(blocks)
    index_scale = float(index_heads * flat_ref.shape[1]) ** (-0.5)
    ikeys = jnp.concatenate([b[:own_keys, :] for b in blocks], axis=0)
    dots = contract(flat_ref[...], ikeys, (1, 1))
    heads_ref[...] = jnp.maximum(dots, 0.0)
    for t in range(rows):
        lines = slice(t * index_heads, (t + 1) * index_heads)
        weight = index_scale * column_ref[:, t : t + 1]
        masked_ref[lines, :] = jnp.where(dots[lines, :] > 0, weight, 0.0)


def gradient_of(key_total, row_parts, places, near_ref, far_ref, total_ref, exps, indexes, own_keys):
    rows, head_count = total_ref.shape
    own_rows = rows // row_parts
    for r in range(row_parts):
        lines = slice(0, own_rows)
        total_ref[r * own_rows : (r + 1) * own_rows, :] = near_ref[r, lines, :] + far_ref[r ^ 1, lines, :]
    shares = jnp.transpose(1.0 / total_ref[...])
    gradients = []
    for t in range(rows):
        r, i = divmod(t, own_rows)
        share = shares[:, t : t + 1]
        at = own_rows + i
        index_total = near_ref[r, at : at + 1, :1] + far_ref[r ^ 1, at : at + 1, :1]
        target = jnp.concatenate(
            [
                jnp.sum(exps[n][t, :, p : p + own_keys] * share, axis=0, keepdims=True)
                for n, p in places
            ],
            axis=1,
        )
        index_exp = jnp.concatenate(
            [indexes[n][t : t + 1, p : p + own_keys] for n, p in places], axis=1
        )
        gradients.append(key_total * (index_exp / index_total - target / head_count))
    return gradients


def first_grad_kernel(key_total, row_parts, places, *refs):
    count = 1 + max(n for n, _ in places)
    near_ref, far_ref, flat_ref, masked_ref = refs[:4]
    exps, indexes = refs[4 : 4 + count], refs[4 + count : 4 + 2 * count]
    key_ref, dots_ref, gradient_ref, total_ref = refs[4 + 2 * count :]
    own_keys = key_ref.shape[1]
    gradients = gradient_of(
        key_total, row_parts, places, near_ref, far_ref, total_ref, exps, indexes, own_keys
    )
    index_heads = flat_ref.shape[0] // len(gradients)
    for t, gradient in enumerate(gradients):
        lines = slice(t * index_heads, (t + 1) * index_heads)
        gradient_ref[t : t + 1, :] = gradient
        dots_ref[lines, :] = (gradient * masked_ref[lines, :]).astype(bf16)
    key_grad = contract(dots_ref[...], flat_ref[...], (0, 0))
    for k in range(len(places)):
        key_ref[k] = key_grad[k * own_keys : (k + 1) * own_keys, :].astype(key_ref.dtype)


def grad_kernel(key_total, row_parts, places, *refs):
    count = 1 + max(n for n, _ in places)
    near_ref, far_ref, flat_ref, column_ref = refs[:4]
    exps, indexes = refs[4 : 4 + count], refs[4 + count : 4 + 2 * count]
    refs = refs[4 + 2 * count :]
    blocks, refs = refs[: len(places)], refs[len(places) :]
    early_dots, early_gradient, early_heads = refs[:3]
    early_blocks, refs = refs[3 : 3 + len(places)], refs[3 + len(places) :]
    key_ref, keep_ref, send_ref, dots_ref, total_ref = refs
    own_rows = total_ref.shape[0] // row_parts
    index_heads, index_width = column_ref.shape[0], flat_ref.shape[1]
    own_keys = key_ref.shape[1]
    index_scale = float(index_heads * index_width) ** (-0.5)
    ikeys = jnp.concatenate([b[:own_keys, :] for b in blocks], axis=0)
    flat = flat_ref[...]
    dots = contract(flat, ikeys, (1, 1))
    gradients = gradient_of(
        key_total, row_parts, places, near_ref, far_ref, total_ref, exps, indexes, own_keys
    )
    lane = lax.broadcasted_iota(jnp.int32, (index_heads, LANES), 1)
    columns = jnp.zeros((index_heads, LANES), f32)
    for t, gradient in enumerate(gradients):
        lines = slice(t * index_heads, (t + 1) * index_heads)
        heads = dots[lines, :]
        terms = gradient * jnp.maximum(heads, 0.0)
        terms = terms + early_gradient[t : t + 1, :] * early_heads[lines, :]
        column = index_scale * jnp.sum(terms, axis=1, keepdims=True)
        columns = jnp.where(lane == t, column, columns)
        weight = column_ref[:, t : t + 1]
        grad_dots = jnp.where(heads > 0, index_scale * gradient * weight, 0.0).astype(bf16)
        dots_ref[lines, :] = grad_dots
    grad_dots = dots_ref[...]
    key_grad = contract(grad_dots, flat, (0, 0))
    for k in range(len(blocks)):
        key_ref[k] = key_grad[k * own_keys : (k + 1) * own_keys, :].astype(key_ref.dtype)
    early_keys = jnp.concatenate([b[:own_keys, :] for b in early_blocks], axis=0)
    grad_query = contract(grad_dots, ikeys, (1, 0)) + contract(early_dots[...], early_keys, (1, 0))
    weights = jnp.transpose(jnp.concatenate([columns, jnp.zeros_like(columns)], axis=0)[:LANES])
    lines = own_rows * index_heads
    for r in range(row_parts):
        out, at = (keep_ref, r) if r < row_parts // 2 else (send_ref, r - row_parts // 2)
        out[at, :lines, :] = grad_query[r * lines : (r + 1) * lines, :]
        out[at, lines : lines + own_rows, :] = weights[r * own_rows : (r + 1) * own_rows, :]


def finish_kernel(key_ref, key_got_ref, row_ref, row_got_ref, query_ref, weight_ref, key_out_ref):
    lines = query_ref.shape[0]
    own_rows, index_heads = weight_ref.shape
    key_out_ref[...] = key_ref[...] + key_got_ref[...].astype(f32)
    query_ref[...] = row_ref[:lines, :] + row_got_ref[:lines, :]
    tail = slice(lines, lines + own_rows)
    weight_ref[...] = (row_ref[tail, :] + row_got_ref[tail, :])[:, :index_heads]


def body(query_main, key_codes, key_scales, index_keys, index_query, index_weight, query_pos):
    own_rows, head_count, latent_width = query_main.shape
    index_heads, index_width = index_query.shape[1:]
    own_keys = key_codes.shape[0]
    count = lax.axis_size("ctx")
    row_parts = 4
    key_parts = count // row_parts
    key_total = own_keys * count
    rows = own_rows * row_parts
    lines = own_rows * index_heads
    tall = lines + 8
    struct = jax.ShapeDtypeStruct

    codes = key_codes.T
    groups = key_scales.shape[1]
    main_raw = jnp.transpose(query_main, (0, 2, 1))
    sources = (
        key_scales.T,
        index_keys,
        index_weight,
        query_pos,
        main_raw,
        index_query.reshape(lines, index_width),
        codes,
    )
    key_pack, index_own, main_own, codes_own = pl.pallas_call(
        pack_kernel,
        out_shape=(
            struct((own_keys + 16, own_keys), bf16),
            struct((lines + 16, index_width), bf16),
            struct(main_raw.shape, bf16),
            struct(codes.shape, bf16),
        ),
        in_specs=[pl.BlockSpec(memory_space=pltpu.HBM)] * len(sources),
        scratch_shapes=[
            pltpu.VMEM((groups, own_keys), jnp.int32),
            pltpu.VMEM((own_rows, index_heads), f32),
            pltpu.SMEM((own_rows,), jnp.int32),
            pltpu.SemaphoreType.DMA((len(sources),)),
        ],
        compiler_params=pltpu.CompilerParams(vmem_limit_bytes=8 << 20),
        name="pack",
    )(*(pltpu.with_memory_space_constraint(x, pltpu.HBM) for x in sources))
    codes = swap_gather(codes, row_parts, key_parts, count)
    codes[0] = codes_own
    blocks = swap_gather(key_pack, row_parts, key_parts, count)
    queries = swap_gather(main_raw, 1, row_parts, count)
    queries[0] = main_own
    iqueries = swap_gather(index_own, 1, row_parts, count)

    step = 4
    if key_parts <= step:
        pieces = [list(range(key_parts - 1)), [key_parts - 1]]
    else:
        pieces = [list(range(k, k + step)) for k in range(0, key_parts, step)]
    exps, indexes, sums, laid = [], [], None, None
    for n, piece in enumerate(pieces):
        wide = len(piece) * own_keys
        shapes = (
            struct((rows, head_count, wide), f32),
            struct((rows, wide), f32),
            struct((row_parts, 2 * own_rows, head_count), f32),
        )
        if n == 0:
            shapes += (
                struct((rows * head_count, latent_width), bf16),
                struct((rows * index_heads, index_width), bf16),
                struct((index_heads, rows), f32),
                struct((rows, LANES), f32),
            )
        out = kernel_call(
            functools.partial(score_kernel, tuple(piece), row_parts, groups, n == 0),
            shapes,
            (
                *(laid or (*queries, *iqueries)),
                *(codes[k] for k in piece),
                *(blocks[k] for k in piece),
            ),
            scratch=(pltpu.VMEM((rows, LANES), f32),) if n == 0 else (),
            flops=2 * rows * head_count * latent_width * wide,
        )
        laid = laid or out[3:]
        exps.append(out[0])
        indexes.append(out[1])
        sums = out[2] if sums is None else sums + out[2]

    bit = row_parts // 2
    while bit > 1:
        got = swap(sums, bit, count)
        sums = sums + jnp.stack([got[r ^ bit] for r in range(row_parts)])
        bit //= 2
    got = swap(sums, 1, count)

    place = {k: (n, p * own_keys) for n, piece in enumerate(pieces) for p, k in enumerate(piece)}
    teams = [list(range(key_parts))] if key_parts <= step else pieces
    even, odd, keep, send = [], [], None, None
    for ids in teams:
        half = len(ids) // 2
        more = struct((rows * index_heads, half * own_keys), bf16)
        wide = struct(more.shape, f32)
        grads_flops = 4 * rows * index_heads * index_width * half * own_keys
        heads, masked = kernel_call(
            prepare_kernel,
            (wide, wide),
            (*laid[1:3], *(blocks[k] for k in ids[1::2])),
            flops=grads_flops,
        )
        early = None
        for part in (1, 0):
            mine = ids[part::2]
            used = sorted({place[k][0] for k in mine})
            places = tuple((used.index(place[k][0]), place[k][1]) for k in mine)
            stored = (*(exps[n] for n in used), *(indexes[n] for n in used))
            shapes = (struct((half, own_keys, index_width), bf16 if part else f32),)
            scratch = (pltpu.VMEM((rows, head_count), f32),)
            if part:
                kernel = first_grad_kernel
                operands = (sums, got, laid[1], masked, *stored)
                shapes += (more, struct((rows, half * own_keys), f32))
            else:
                kernel = grad_kernel
                operands = (sums, got, *laid[1:3], *stored, *(blocks[k] for k in mine))
                operands += (*early, heads, *(blocks[k] for k in ids[1::2]))
                shapes += (struct((row_parts // 2, tall, index_width), f32),) * 2
                scratch = (pltpu.VMEM(more.shape, bf16), *scratch)
            out = kernel_call(
                functools.partial(kernel, key_total, row_parts, places),
                shapes,
                operands,
                scratch=scratch,
                flops=grads_flops,
            )
            if part:
                odd.append(out[0])
                early = out[1:]
            else:
                even.append(out[0])
                keep = out[1] if keep is None else keep + out[1]
                send = out[2] if send is None else send + out[2]
    key_sum = even[0] if len(even) == 1 else jnp.concatenate(even)
    key_send = odd[0] if len(odd) == 1 else jnp.concatenate(odd)

    key_got = swap(key_send, row_parts, count)
    row_got = swap(send, row_parts // 2, count)
    bit = 2
    while bit < key_parts:
        key_sum = key_sum + key_got.astype(f32)
        key_got = swap(key_sum[1::2].astype(bf16), row_parts * bit, count)
        key_sum = key_sum[0::2]
        bit *= 2
    row_sum = keep + row_got
    row_got = swap(row_sum[1], 1, count)
    grad_query, grad_weight, key_grad = kernel_call(
        finish_kernel,
        (
            struct((lines, index_width), f32),
            struct((own_rows, index_heads), f32),
            struct((own_keys, index_width), f32),
        ),
        (key_sum[0], key_got[0], row_sum[0], row_got),
    )
    return grad_query.reshape(own_rows, index_heads, index_width), grad_weight, key_grad


def solution(mesh):
    placed = (
        P(("grp", "ctx"), None, None),
        P(("grp", "ctx"), None),
        P(("grp", "ctx"), None),
        P(("grp", "ctx"), None),
        P(("grp", "ctx"), None, None),
        P(("grp", "ctx"), None),
        P(("grp", "ctx")),
    )

    return jax.shard_map(
        body,
        mesh=mesh,
        in_specs=placed,
        out_specs=(P(("grp", "ctx"), None, None), P(("grp", "ctx"), None), P(("grp", "ctx"), None)),
        check_vma=False,
    )
```

```python
import functools

import jax
import jax.numpy as jnp
from jax import lax
from jax.experimental import pallas as pl
from jax.experimental.pallas import tpu as pltpu
from jax.sharding import PartitionSpec as P


ROPE = 64
LANES = 128

f32, bf16 = jnp.float32, jnp.bfloat16
main_scale = 192.0 ** (-0.5)


def kernel_call(kernel, shapes, operands, scratch=(), flops=0):
    nbytes = sum(x.size * x.dtype.itemsize for x in (*operands, *shapes))
    return pl.pallas_call(
        kernel,
        out_shape=tuple(shapes),
        scratch_shapes=list(scratch),
        compiler_params=pltpu.CompilerParams(vmem_limit_bytes=24 << 20),
        cost_estimate=pl.CostEstimate(flops=flops, bytes_accessed=nbytes, transcendentals=0),
    )(*operands)


def contract(left, right, dims):
    return lax.dot_general(left, right, ((dims[:1], dims[1:]), ((), ())), preferred_element_type=f32)


def swap(array, mask, count):
    return lax.ppermute(array, "ctx", [(i, i ^ mask) for i in range(count)])


def swap_gather(block, stride, parts, count):
    held = {0: block}
    bit = parts // 2
    while bit:
        for k, own in list(held.items()):
            held[k ^ bit] = swap(own, stride * bit, count)
        bit //= 2
    return [held[k] for k in range(parts)]


def pack_kernel(
    scales_hbm, keys_hbm, weight_hbm, pos_hbm, main_hbm, query_hbm, codes_hbm, out_ref, query_ref,
    main_ref, codes_ref, scales_ref, weight_ref, pos_ref, sems
):
    groups, own_keys = scales_hbm.shape
    key_count = keys_hbm.shape[0]
    lines = query_hbm.shape[0]
    pairs = (
        (scales_hbm, scales_ref),
        (weight_hbm, weight_ref),
        (pos_hbm, pos_ref),
        (keys_hbm, out_ref.at[pl.ds(0, key_count), :]),
        (query_hbm, query_ref.at[pl.ds(0, lines), :]),
        (main_hbm, main_ref),
        (codes_hbm, codes_ref),
    )
    copies = [pltpu.make_async_copy(a, b, sems.at[n]) for n, (a, b) in enumerate(pairs)]
    for copy in copies:
        copy.start()
    for copy in copies[:3]:
        copy.wait()
    factors = jnp.exp2(scales_ref[...].astype(f32))
    spare = out_ref.shape[0] - key_count - groups
    factors = jnp.concatenate([factors, jnp.zeros((spare, own_keys), f32)], axis=0)
    out_ref[key_count:, :] = factors.astype(bf16)
    own_rows, index_heads = weight_ref.shape
    rest = jnp.concatenate([weight_ref[...], jnp.zeros((own_rows, LANES - index_heads), f32)], axis=1)
    lane = lax.broadcasted_iota(jnp.int32, (1, LANES), 1)
    tail = []
    for part in range(3):
        piece = rest.astype(bf16).astype(f32)
        rest = rest - piece
        for i in range(own_rows):
            pos = jnp.full((1, LANES), pos_ref[i], jnp.int32)
            at = ((pos // LANES) * LANES, pos % LANES, jnp.zeros_like(pos))[part].astype(f32)
            tail.append(jnp.where(lane == index_heads, at, piece[i : i + 1, :]))
    tail.append(jnp.zeros((query_ref.shape[0] - lines - len(tail), LANES), f32))
    query_ref[lines:, :] = jnp.concatenate(tail, axis=0).astype(bf16)
    for copy in copies[3:]:
        copy.wait()


def latent_of(codes_ref, keys_ref, groups):
    latent_width, own_keys = codes_ref.shape
    group_width = (latent_width - ROPE) // groups
    factors = keys_ref[own_keys:, :].astype(f32)
    latent = [
        (codes_ref[g * group_width : (g + 1) * group_width, :].astype(f32) * factors[g : g + 1, :]).astype(bf16)
        for g in range(groups)
    ]
    return jnp.concatenate([*latent, codes_ref[groups * group_width :, :]], axis=0)


def score_kernel(offsets, row_parts, groups, first, *refs):
    parts = len(offsets)
    if first:
        queries, iqueries = refs[:row_parts], refs[row_parts : 2 * row_parts]
        refs = refs[2 * row_parts :]
        codes, blocks, refs = refs[:parts], refs[parts : 2 * parts], refs[2 * parts :]
        exp_ref, index_ref, sums_ref, main_ref, flat_ref, column_ref, pos_ref, side_ref = refs
        own_rows, head_count = queries[0].shape[0], queries[0].shape[2]
        lines = flat_ref.shape[0] // row_parts
        index_heads = lines // own_rows
        for r in range(row_parts):
            tail = iqueries[r][lines:, :].astype(f32)
            side = tail[:own_rows] + tail[own_rows : 2 * own_rows]
            side = side + tail[2 * own_rows : 3 * own_rows]
            side_ref[r * own_rows : (r + 1) * own_rows, :] = side
            flat_ref[r * lines : (r + 1) * lines, :] = iqueries[r][:lines, :]
            for i in range(own_rows):
                t = r * own_rows + i
                main_ref[t * head_count : (t + 1) * head_count, :] = jnp.transpose(queries[r][i])
        side = side_ref[...]
        columns = jnp.transpose(side)
        column_ref[...] = columns[:index_heads, :]
        pos_ref[...] = jnp.broadcast_to(side[:, index_heads : index_heads + 1], pos_ref.shape)
    else:
        main_ref, flat_ref, column_ref, pos_ref = refs[:4]
        codes, blocks = refs[4 : 4 + parts], refs[4 + parts : 4 + 2 * parts]
        exp_ref, index_ref, sums_ref = refs[4 + 2 * parts :]
    rows = pos_ref.shape[0]
    own_rows = rows // row_parts
    index_heads = column_ref.shape[0]
    index_width = flat_ref.shape[1]
    head_count = main_ref.shape[0] // rows
    own_keys = blocks[0].shape[1]
    index_scale = float(index_heads * index_width) ** (-0.5)
    me = lax.axis_index("ctx")
    iota = lax.broadcasted_iota(jnp.int32, (1, own_keys), 1)
    key_pos = [((me ^ (row_parts * k)) * own_keys + iota).astype(f32) for k in offsets]
    key_pos = jnp.concatenate(key_pos, axis=1)
    latent = jnp.concatenate([latent_of(c, b, groups) for c, b in zip(codes, blocks)], axis=1)
    ikeys = jnp.concatenate([b[:own_keys, :] for b in blocks], axis=0)
    dots = contract(flat_ref[...], ikeys, (1, 1))
    scores = contract(main_ref[...], latent, (1, 0))
    sums_ref[...] = jnp.zeros_like(sums_ref)
    for t in range(rows):
        r, i = divmod(t, own_rows)
        visible = key_pos <= pos_ref[t : t + 1, :1]
        heads = jnp.maximum(dots[t * index_heads : (t + 1) * index_heads, :], 0.0)
        score = jnp.sum(column_ref[:, t : t + 1] * heads, axis=0, keepdims=True)
        index_exp = jnp.where(visible, jnp.exp(index_scale * score), 0.0)
        index_ref[t : t + 1, :] = index_exp
        score = scores[t * head_count : (t + 1) * head_count, :] * main_scale
        main_exp = jnp.where(visible, jnp.exp(score), 0.0)
        exp_ref[t] = main_exp
        total = main_exp[:, :own_keys]
        for k in range(1, parts):
            total = total + main_exp[:, k * own_keys : (k + 1) * own_keys]
        sums_ref[r, i : i + 1, :] = jnp.sum(jnp.transpose(total), axis=0, keepdims=True)
        index_total = jnp.sum(index_exp, axis=1, keepdims=True)
        sums_ref[r, own_rows + i : own_rows + i + 1, :] = jnp.broadcast_to(
            index_total, (1, head_count)
        )


def prepare_kernel(flat_ref, column_ref, *refs):
    blocks, (heads_ref, masked_ref) = refs[:-2], refs[-2:]
    index_heads, rows = column_ref.shape
    own_keys = heads_ref.shape[1] // len(blocks)
    index_scale = float(index_heads * flat_ref.shape[1]) ** (-0.5)
    ikeys = jnp.concatenate([b[:own_keys, :] for b in blocks], axis=0)
    dots = contract(flat_ref[...], ikeys, (1, 1))
    heads_ref[...] = jnp.maximum(dots, 0.0)
    for t in range(rows):
        lines = slice(t * index_heads, (t + 1) * index_heads)
        weight = index_scale * column_ref[:, t : t + 1]
        masked_ref[lines, :] = jnp.where(dots[lines, :] > 0, weight, 0.0)


def gradient_of(key_total, row_parts, places, sums, total_ref, exps, indexes, own_keys):
    rows, head_count = total_ref.shape
    own_rows = rows // row_parts
    for r in range(row_parts):
        lines = slice(0, own_rows)
        total_ref[r * own_rows : (r + 1) * own_rows, :] = sum(
            s[r ^ m, lines, :] for m, s in enumerate(sums)
        )
    shares = jnp.transpose(1.0 / total_ref[...])
    gradients = []
    for t in range(rows):
        r, i = divmod(t, own_rows)
        share = shares[:, t : t + 1]
        at = own_rows + i
        index_total = sum(s[r ^ m, at : at + 1, :1] for m, s in enumerate(sums))
        target = jnp.concatenate(
            [
                jnp.sum(exps[n][t, :, p : p + own_keys] * share, axis=0, keepdims=True)
                for n, p in places
            ],
            axis=1,
        )
        index_exp = jnp.concatenate(
            [indexes[n][t : t + 1, p : p + own_keys] for n, p in places], axis=1
        )
        gradients.append(key_total * (index_exp / index_total - target / head_count))
    return gradients


def first_grad_kernel(key_total, row_parts, places, *refs):
    count = 1 + max(n for n, _ in places)
    sums, refs = refs[:row_parts], refs[row_parts - 2 :]
    flat_ref, masked_ref = refs[2:4]
    exps, indexes = refs[4 : 4 + count], refs[4 + count : 4 + 2 * count]
    key_ref, dots_ref, gradient_ref, total_ref = refs[4 + 2 * count :]
    own_keys = key_ref.shape[1]
    gradients = gradient_of(
        key_total, row_parts, places, sums, total_ref, exps, indexes, own_keys
    )
    index_heads = flat_ref.shape[0] // len(gradients)
    for t, gradient in enumerate(gradients):
        lines = slice(t * index_heads, (t + 1) * index_heads)
        gradient_ref[t : t + 1, :] = gradient
        dots_ref[lines, :] = (gradient * masked_ref[lines, :]).astype(bf16)
    key_grad = contract(dots_ref[...], flat_ref[...], (0, 0))
    for k in range(len(places)):
        key_ref[k] = key_grad[k * own_keys : (k + 1) * own_keys, :].astype(key_ref.dtype)


def grad_kernel(key_total, row_parts, places, *refs):
    count = 1 + max(n for n, _ in places)
    sums, refs = refs[:row_parts], refs[row_parts - 2 :]
    flat_ref, column_ref = refs[2:4]
    exps, indexes = refs[4 : 4 + count], refs[4 + count : 4 + 2 * count]
    refs = refs[4 + 2 * count :]
    blocks, refs = refs[: len(places)], refs[len(places) :]
    early_dots, early_gradient, early_heads = refs[:3]
    early_blocks, refs = refs[3 : 3 + len(places)], refs[3 + len(places) :]
    key_ref, keep_ref, send_ref, dots_ref, total_ref = refs
    own_rows = total_ref.shape[0] // row_parts
    index_heads, index_width = column_ref.shape[0], flat_ref.shape[1]
    own_keys = key_ref.shape[1]
    index_scale = float(index_heads * index_width) ** (-0.5)
    ikeys = jnp.concatenate([b[:own_keys, :] for b in blocks], axis=0)
    flat = flat_ref[...]
    dots = contract(flat, ikeys, (1, 1))
    gradients = gradient_of(
        key_total, row_parts, places, sums, total_ref, exps, indexes, own_keys
    )
    lane = lax.broadcasted_iota(jnp.int32, (index_heads, LANES), 1)
    columns = jnp.zeros((index_heads, LANES), f32)
    for t, gradient in enumerate(gradients):
        lines = slice(t * index_heads, (t + 1) * index_heads)
        heads = dots[lines, :]
        terms = gradient * jnp.maximum(heads, 0.0)
        terms = terms + early_gradient[t : t + 1, :] * early_heads[lines, :]
        column = index_scale * jnp.sum(terms, axis=1, keepdims=True)
        columns = jnp.where(lane == t, column, columns)
        weight = column_ref[:, t : t + 1]
        grad_dots = jnp.where(heads > 0, index_scale * gradient * weight, 0.0).astype(bf16)
        dots_ref[lines, :] = grad_dots
    grad_dots = dots_ref[...]
    key_grad = contract(grad_dots, flat, (0, 0))
    for k in range(len(blocks)):
        key_ref[k] = key_grad[k * own_keys : (k + 1) * own_keys, :].astype(key_ref.dtype)
    early_keys = jnp.concatenate([b[:own_keys, :] for b in early_blocks], axis=0)
    grad_query = contract(grad_dots, ikeys, (1, 0)) + contract(early_dots[...], early_keys, (1, 0))
    weights = jnp.transpose(jnp.concatenate([columns, jnp.zeros_like(columns)], axis=0)[:LANES])
    lines = own_rows * index_heads
    for r in range(row_parts):
        out, at = (keep_ref, r) if r < row_parts // 2 else (send_ref, r - row_parts // 2)
        out[at, :lines, :] = grad_query[r * lines : (r + 1) * lines, :]
        out[at, lines : lines + own_rows, :] = weights[r * own_rows : (r + 1) * own_rows, :]


def finish_kernel(key_ref, key_got_ref, row_ref, row_got_ref, query_ref, weight_ref, key_out_ref):
    lines = query_ref.shape[0]
    own_rows, index_heads = weight_ref.shape
    key_out_ref[...] = key_ref[...] + key_got_ref[...].astype(f32)
    query_ref[...] = row_ref[:lines, :] + row_got_ref[:lines, :]
    tail = slice(lines, lines + own_rows)
    weight_ref[...] = (row_ref[tail, :] + row_got_ref[tail, :])[:, :index_heads]


def body(query_main, key_codes, key_scales, index_keys, index_query, index_weight, query_pos):
    own_rows, head_count, latent_width = query_main.shape
    index_heads, index_width = index_query.shape[1:]
    own_keys = key_codes.shape[0]
    count = lax.axis_size("ctx")
    row_parts = 4
    key_parts = count // row_parts
    key_total = own_keys * count
    rows = own_rows * row_parts
    lines = own_rows * index_heads
    tall = lines + 8
    struct = jax.ShapeDtypeStruct

    codes = key_codes.T
    groups = key_scales.shape[1]
    main_raw = jnp.transpose(query_main, (0, 2, 1))
    sources = (
        key_scales.T,
        index_keys,
        index_weight,
        query_pos,
        main_raw,
        index_query.reshape(lines, index_width),
        codes,
    )
    key_pack, index_own, main_own, codes_own = pl.pallas_call(
        pack_kernel,
        out_shape=(
            struct((own_keys + 16, own_keys), bf16),
            struct((lines + 16, index_width), bf16),
            struct(main_raw.shape, bf16),
            struct(codes.shape, bf16),
        ),
        in_specs=[pl.BlockSpec(memory_space=pltpu.HBM)] * len(sources),
        scratch_shapes=[
            pltpu.VMEM((groups, own_keys), jnp.int32),
            pltpu.VMEM((own_rows, index_heads), f32),
            pltpu.SMEM((own_rows,), jnp.int32),
            pltpu.SemaphoreType.DMA((len(sources),)),
        ],
        compiler_params=pltpu.CompilerParams(vmem_limit_bytes=8 << 20),
        name="pack",
    )(*(pltpu.with_memory_space_constraint(x, pltpu.HBM) for x in sources))
    codes = swap_gather(codes, row_parts, key_parts, count)
    codes[0] = codes_own
    blocks = swap_gather(key_pack, row_parts, key_parts, count)
    queries = swap_gather(main_raw, 1, row_parts, count)
    queries[0] = main_own
    iqueries = swap_gather(index_own, 1, row_parts, count)

    step = 4
    if key_parts <= step:
        pieces = [list(range(key_parts - 1)), [key_parts - 1]]
    else:
        pieces = [list(range(k, k + step)) for k in range(0, key_parts, step)]
    exps, indexes, sums, laid = [], [], None, None
    for n, piece in enumerate(pieces):
        wide = len(piece) * own_keys
        shapes = (
            struct((rows, head_count, wide), f32),
            struct((rows, wide), f32),
            struct((row_parts, 2 * own_rows, head_count), f32),
        )
        if n == 0:
            shapes += (
                struct((rows * head_count, latent_width), bf16),
                struct((rows * index_heads, index_width), bf16),
                struct((index_heads, rows), f32),
                struct((rows, LANES), f32),
            )
        out = kernel_call(
            functools.partial(score_kernel, tuple(piece), row_parts, groups, n == 0),
            shapes,
            (
                *(laid or (*queries, *iqueries)),
                *(codes[k] for k in piece),
                *(blocks[k] for k in piece),
            ),
            scratch=(pltpu.VMEM((rows, LANES), f32),) if n == 0 else (),
            flops=2 * rows * head_count * latent_width * wide,
        )
        laid = laid or out[3:]
        exps.append(out[0])
        indexes.append(out[1])
        sums = out[2] if sums is None else sums + out[2]

    sums = [sums]
    for mask in (2, 3, 1):
        sums.append(swap(sums[0], mask, count))
    sums = [sums[0], sums[3], sums[1], sums[2]]

    place = {k: (n, p * own_keys) for n, piece in enumerate(pieces) for p, k in enumerate(piece)}
    teams = [list(range(key_parts))] if key_parts <= step else pieces
    even, odd, keep, send = [], [], None, None
    for ids in teams:
        half = len(ids) // 2
        more = struct((rows * index_heads, half * own_keys), bf16)
        wide = struct(more.shape, f32)
        grads_flops = 4 * rows * index_heads * index_width * half * own_keys
        heads, masked = kernel_call(
            prepare_kernel,
            (wide, wide),
            (*laid[1:3], *(blocks[k] for k in ids[1::2])),
            flops=grads_flops,
        )
        early = None
        for part in (1, 0):
            mine = ids[part::2]
            used = sorted({place[k][0] for k in mine})
            places = tuple((used.index(place[k][0]), place[k][1]) for k in mine)
            stored = (*(exps[n] for n in used), *(indexes[n] for n in used))
            shapes = (struct((half, own_keys, index_width), bf16 if part else f32),)
            scratch = (pltpu.VMEM((rows, head_count), f32),)
            if part:
                kernel = first_grad_kernel
                operands = (*sums, laid[1], masked, *stored)
                shapes += (more, struct((rows, half * own_keys), f32))
            else:
                kernel = grad_kernel
                operands = (*sums, *laid[1:3], *stored, *(blocks[k] for k in mine))
                operands += (*early, heads, *(blocks[k] for k in ids[1::2]))
                shapes += (struct((row_parts // 2, tall, index_width), f32),) * 2
                scratch = (pltpu.VMEM(more.shape, bf16), *scratch)
            out = kernel_call(
                functools.partial(kernel, key_total, row_parts, places),
                shapes,
                operands,
                scratch=scratch,
                flops=grads_flops,
            )
            if part:
                odd.append(out[0])
                early = out[1:]
            else:
                even.append(out[0])
                keep = out[1] if keep is None else keep + out[1]
                send = out[2] if send is None else send + out[2]
    key_sum = even[0] if len(even) == 1 else jnp.concatenate(even)
    key_send = odd[0] if len(odd) == 1 else jnp.concatenate(odd)

    key_got = swap(key_send, row_parts, count)
    row_got = swap(send, row_parts // 2, count)
    bit = 2
    while bit < key_parts:
        key_sum = key_sum + key_got.astype(f32)
        key_got = swap(key_sum[1::2].astype(bf16), row_parts * bit, count)
        key_sum = key_sum[0::2]
        bit *= 2
    row_sum = keep + row_got
    row_got = swap(row_sum[1], 1, count)
    grad_query, grad_weight, key_grad = kernel_call(
        finish_kernel,
        (
            struct((lines, index_width), f32),
            struct((own_rows, index_heads), f32),
            struct((own_keys, index_width), f32),
        ),
        (key_sum[0], key_got[0], row_sum[0], row_got),
    )
    return grad_query.reshape(own_rows, index_heads, index_width), grad_weight, key_grad


def solution(mesh):
    placed = (
        P(("grp", "ctx"), None, None),
        P(("grp", "ctx"), None),
        P(("grp", "ctx"), None),
        P(("grp", "ctx"), None),
        P(("grp", "ctx"), None, None),
        P(("grp", "ctx"), None),
        P(("grp", "ctx")),
    )

    return jax.shard_map(
        body,
        mesh=mesh,
        in_specs=placed,
        out_specs=(P(("grp", "ctx"), None, None), P(("grp", "ctx"), None), P(("grp", "ctx"), None)),
        check_vma=False,
    )
```

```python
import functools

import jax
import jax.numpy as jnp
from jax import lax
from jax.experimental import pallas as pl
from jax.experimental.pallas import tpu as pltpu
from jax.sharding import PartitionSpec as P


ROPE = 64
LANES = 128

f32, bf16 = jnp.float32, jnp.bfloat16
main_scale = 192.0 ** (-0.5)


def kernel_call(kernel, shapes, operands, scratch=(), flops=0):
    nbytes = sum(x.size * x.dtype.itemsize for x in (*operands, *shapes))
    return pl.pallas_call(
        kernel,
        out_shape=tuple(shapes),
        scratch_shapes=list(scratch),
        compiler_params=pltpu.CompilerParams(vmem_limit_bytes=24 << 20),
        cost_estimate=pl.CostEstimate(flops=flops, bytes_accessed=nbytes, transcendentals=0),
    )(*operands)


def contract(left, right, dims):
    return lax.dot_general(left, right, ((dims[:1], dims[1:]), ((), ())), preferred_element_type=f32)


def swap(array, mask, count):
    return lax.ppermute(array, "ctx", [(i, i ^ mask) for i in range(count)])


def swap_gather(block, stride, parts, count):
    held = {0: block}
    bit = parts // 2
    while bit:
        for k, own in list(held.items()):
            held[k ^ bit] = swap(own, stride * bit, count)
        bit //= 2
    return [held[k] for k in range(parts)]


def pack_kernel(
    scales_hbm, keys_hbm, weight_hbm, pos_hbm, main_hbm, query_hbm, codes_hbm, out_ref, query_ref,
    main_ref, codes_ref, scales_ref, weight_ref, pos_ref, sems
):
    groups, own_keys = scales_hbm.shape
    key_count = keys_hbm.shape[0]
    lines = query_hbm.shape[0]
    pairs = (
        (scales_hbm, scales_ref),
        (weight_hbm, weight_ref),
        (pos_hbm, pos_ref),
        (keys_hbm, out_ref.at[pl.ds(0, key_count), :]),
        (query_hbm, query_ref.at[pl.ds(0, lines), :]),
        (main_hbm, main_ref),
        (codes_hbm, codes_ref),
    )
    copies = [pltpu.make_async_copy(a, b, sems.at[n]) for n, (a, b) in enumerate(pairs)]
    for copy in copies:
        copy.start()
    for copy in copies[:3]:
        copy.wait()
    factors = jnp.exp2(scales_ref[...].astype(f32))
    spare = out_ref.shape[0] - key_count - groups
    factors = jnp.concatenate([factors, jnp.zeros((spare, own_keys), f32)], axis=0)
    out_ref[key_count:, :] = factors.astype(bf16)
    own_rows, index_heads = weight_ref.shape
    rest = jnp.concatenate([weight_ref[...], jnp.zeros((own_rows, LANES - index_heads), f32)], axis=1)
    lane = lax.broadcasted_iota(jnp.int32, (1, LANES), 1)
    tail = []
    for part in range(3):
        piece = rest.astype(bf16).astype(f32)
        rest = rest - piece
        for i in range(own_rows):
            pos = jnp.full((1, LANES), pos_ref[i], jnp.int32)
            at = ((pos // LANES) * LANES, pos % LANES, jnp.zeros_like(pos))[part].astype(f32)
            tail.append(jnp.where(lane == index_heads, at, piece[i : i + 1, :]))
    tail.append(jnp.zeros((query_ref.shape[0] - lines - len(tail), LANES), f32))
    query_ref[lines:, :] = jnp.concatenate(tail, axis=0).astype(bf16)
    for copy in copies[3:]:
        copy.wait()


def latent_of(codes_ref, keys_ref, groups):
    latent_width, own_keys = codes_ref.shape
    group_width = (latent_width - ROPE) // groups
    factors = keys_ref[own_keys:, :].astype(f32)
    latent = [
        (codes_ref[g * group_width : (g + 1) * group_width, :].astype(f32) * factors[g : g + 1, :]).astype(bf16)
        for g in range(groups)
    ]
    return jnp.concatenate([*latent, codes_ref[groups * group_width :, :]], axis=0)


def lay_kernel(*refs):
    queries, main_ref = refs[:-1], refs[-1]
    own_rows, _, head_count = queries[0].shape
    for r, query in enumerate(queries):
        for i in range(own_rows):
            t = r * own_rows + i
            main_ref[t * head_count : (t + 1) * head_count, :] = jnp.transpose(query[i])


def score_kernel(offsets, row_parts, groups, first, *refs):
    parts = len(offsets)
    if first:
        early_ref, query, iqueries = refs[0], refs[1], refs[2 : 2 + row_parts]
        refs = refs[2 + row_parts :]
        codes, blocks, refs = refs[:parts], refs[parts : 2 * parts], refs[2 * parts :]
        exp_ref, index_ref, sums_ref, main_ref, flat_ref, column_ref, pos_ref, side_ref = refs
        own_rows, head_count = query.shape[0], query.shape[2]
        lines = flat_ref.shape[0] // row_parts
        index_heads = lines // own_rows
        for r in range(row_parts):
            tail = iqueries[r][lines:, :].astype(f32)
            side = tail[:own_rows] + tail[own_rows : 2 * own_rows]
            side = side + tail[2 * own_rows : 3 * own_rows]
            side_ref[r * own_rows : (r + 1) * own_rows, :] = side
            flat_ref[r * lines : (r + 1) * lines, :] = iqueries[r][:lines, :]
        for i in range(own_rows):
            main_ref[i * head_count : (i + 1) * head_count, :] = jnp.transpose(query[i])
        side = side_ref[...]
        columns = jnp.transpose(side)
        column_ref[...] = columns[:index_heads, :]
        pos_ref[...] = jnp.broadcast_to(side[:, index_heads : index_heads + 1], pos_ref.shape)
    else:
        early_ref, main_ref, flat_ref, column_ref, pos_ref = refs[:5]
        codes, blocks = refs[5 : 5 + parts], refs[5 + parts : 5 + 2 * parts]
        exp_ref, index_ref, sums_ref = refs[5 + 2 * parts :]
    rows = pos_ref.shape[0]
    own_rows = rows // row_parts
    index_heads = column_ref.shape[0]
    index_width = flat_ref.shape[1]
    early_rows = early_ref.shape[0]
    head_count = (early_rows + main_ref.shape[0]) // rows
    own_keys = blocks[0].shape[1]
    index_scale = float(index_heads * index_width) ** (-0.5)
    me = lax.axis_index("ctx")
    iota = lax.broadcasted_iota(jnp.int32, (1, own_keys), 1)
    key_pos = [((me ^ (row_parts * k)) * own_keys + iota).astype(f32) for k in offsets]
    key_pos = jnp.concatenate(key_pos, axis=1)
    latent = jnp.concatenate([latent_of(c, b, groups) for c, b in zip(codes, blocks)], axis=1)
    ikeys = jnp.concatenate([b[:own_keys, :] for b in blocks], axis=0)
    dots = contract(flat_ref[...], ikeys, (1, 1))
    scores = jnp.concatenate(
        [contract(early_ref[...], latent, (1, 0)), contract(main_ref[...], latent, (1, 0))], axis=0
    )
    sums_ref[...] = jnp.zeros_like(sums_ref)
    for t in range(rows):
        r, i = divmod(t, own_rows)
        visible = key_pos <= pos_ref[t : t + 1, :1]
        heads = jnp.maximum(dots[t * index_heads : (t + 1) * index_heads, :], 0.0)
        score = jnp.sum(column_ref[:, t : t + 1] * heads, axis=0, keepdims=True)
        index_exp = jnp.where(visible, jnp.exp(index_scale * score), 0.0)
        index_ref[t : t + 1, :] = index_exp
        score = scores[t * head_count : (t + 1) * head_count, :] * main_scale
        main_exp = jnp.where(visible, jnp.exp(score), 0.0)
        exp_ref[t] = main_exp
        total = main_exp[:, :own_keys]
        for k in range(1, parts):
            total = total + main_exp[:, k * own_keys : (k + 1) * own_keys]
        sums_ref[r, i : i + 1, :] = jnp.sum(jnp.transpose(total), axis=0, keepdims=True)
        index_total = jnp.sum(index_exp, axis=1, keepdims=True)
        sums_ref[r, own_rows + i : own_rows + i + 1, :] = jnp.broadcast_to(
            index_total, (1, head_count)
        )


def prepare_kernel(flat_ref, column_ref, *refs):
    blocks, (heads_ref, masked_ref) = refs[:-2], refs[-2:]
    index_heads, rows = column_ref.shape
    own_keys = heads_ref.shape[1] // len(blocks)
    index_scale = float(index_heads * flat_ref.shape[1]) ** (-0.5)
    ikeys = jnp.concatenate([b[:own_keys, :] for b in blocks], axis=0)
    dots = contract(flat_ref[...], ikeys, (1, 1))
    heads_ref[...] = jnp.maximum(dots, 0.0)
    for t in range(rows):
        lines = slice(t * index_heads, (t + 1) * index_heads)
        weight = index_scale * column_ref[:, t : t + 1]
        masked_ref[lines, :] = jnp.where(dots[lines, :] > 0, weight, 0.0)


def gradient_of(key_total, row_parts, places, sums, total_ref, exps, indexes, own_keys):
    rows, head_count = total_ref.shape
    own_rows = rows // row_parts
    for r in range(row_parts):
        lines = slice(0, own_rows)
        total_ref[r * own_rows : (r + 1) * own_rows, :] = sum(
            s[r ^ m, lines, :] for m, s in enumerate(sums)
        )
    shares = jnp.transpose(1.0 / total_ref[...])
    gradients = []
    for t in range(rows):
        r, i = divmod(t, own_rows)
        share = shares[:, t : t + 1]
        at = own_rows + i
        index_total = sum(s[r ^ m, at : at + 1, :1] for m, s in enumerate(sums))
        target = jnp.concatenate(
            [
                jnp.sum(exps[n][t, :, p : p + own_keys] * share, axis=0, keepdims=True)
                for n, p in places
            ],
            axis=1,
        )
        index_exp = jnp.concatenate(
            [indexes[n][t : t + 1, p : p + own_keys] for n, p in places], axis=1
        )
        gradients.append(key_total * (index_exp / index_total - target / head_count))
    return gradients


def first_grad_kernel(key_total, row_parts, places, *refs):
    count = 1 + max(n for n, _ in places)
    sums, refs = refs[:row_parts], refs[row_parts - 2 :]
    flat_ref, masked_ref = refs[2:4]
    exps, indexes = refs[4 : 4 + count], refs[4 + count : 4 + 2 * count]
    *key_refs, dots_ref, gradient_ref, total_ref = refs[4 + 2 * count :]
    own_keys = key_refs[0].shape[0]
    gradients = gradient_of(
        key_total, row_parts, places, sums, total_ref, exps, indexes, own_keys
    )
    index_heads = flat_ref.shape[0] // len(gradients)
    for t, gradient in enumerate(gradients):
        lines = slice(t * index_heads, (t + 1) * index_heads)
        gradient_ref[t : t + 1, :] = gradient
        dots_ref[lines, :] = (gradient * masked_ref[lines, :]).astype(bf16)
    key_grad = contract(dots_ref[...], flat_ref[...], (0, 0))
    for k, key_ref in enumerate(key_refs):
        key_ref[...] = key_grad[k * own_keys : (k + 1) * own_keys, :].astype(key_ref.dtype)


def grad_kernel(key_total, row_parts, places, *refs):
    count = 1 + max(n for n, _ in places)
    sums, refs = refs[:row_parts], refs[row_parts - 2 :]
    flat_ref, column_ref = refs[2:4]
    exps, indexes = refs[4 : 4 + count], refs[4 + count : 4 + 2 * count]
    refs = refs[4 + 2 * count :]
    blocks, refs = refs[: len(places)], refs[len(places) :]
    early_dots, early_gradient, early_heads = refs[:3]
    early_blocks, refs = refs[3 : 3 + len(places)], refs[3 + len(places) :]
    *key_refs, keep_ref, send_ref, dots_ref, total_ref = refs
    own_rows = total_ref.shape[0] // row_parts
    index_heads, index_width = column_ref.shape[0], flat_ref.shape[1]
    own_keys = key_refs[0].shape[0]
    index_scale = float(index_heads * index_width) ** (-0.5)
    ikeys = jnp.concatenate([b[:own_keys, :] for b in blocks], axis=0)
    flat = flat_ref[...]
    dots = contract(flat, ikeys, (1, 1))
    gradients = gradient_of(
        key_total, row_parts, places, sums, total_ref, exps, indexes, own_keys
    )
    lane = lax.broadcasted_iota(jnp.int32, (index_heads, LANES), 1)
    columns = jnp.zeros((index_heads, LANES), f32)
    for t, gradient in enumerate(gradients):
        lines = slice(t * index_heads, (t + 1) * index_heads)
        heads = dots[lines, :]
        terms = gradient * jnp.maximum(heads, 0.0)
        terms = terms + early_gradient[t : t + 1, :] * early_heads[lines, :]
        column = index_scale * jnp.sum(terms, axis=1, keepdims=True)
        columns = jnp.where(lane == t, column, columns)
        weight = column_ref[:, t : t + 1]
        grad_dots = jnp.where(heads > 0, index_scale * gradient * weight, 0.0).astype(bf16)
        dots_ref[lines, :] = grad_dots
    grad_dots = dots_ref[...]
    key_grad = contract(grad_dots, flat, (0, 0))
    for k, key_ref in enumerate(key_refs):
        key_ref[...] = key_grad[k * own_keys : (k + 1) * own_keys, :].astype(key_ref.dtype)
    early_keys = jnp.concatenate([b[:own_keys, :] for b in early_blocks], axis=0)
    grad_query = contract(grad_dots, ikeys, (1, 0)) + contract(early_dots[...], early_keys, (1, 0))
    weights = jnp.transpose(jnp.concatenate([columns, jnp.zeros_like(columns)], axis=0)[:LANES])
    lines = own_rows * index_heads
    for r in range(row_parts):
        out, at = (keep_ref, r) if r < row_parts // 2 else (send_ref, r - row_parts // 2)
        out[at, :lines, :] = grad_query[r * lines : (r + 1) * lines, :]
        out[at, lines : lines + own_rows, :] = weights[r * own_rows : (r + 1) * own_rows, :]


def finish_kernel(parts, *refs):
    key_refs, (row_ref, row_got_ref, query_ref, weight_ref, key_out_ref) = refs[:parts], refs[parts:]
    lines = query_ref.shape[0]
    own_rows, index_heads = weight_ref.shape
    key_out_ref[...] = sum(ref[...].astype(f32) for ref in key_refs)
    query_ref[...] = row_ref[:lines, :] + row_got_ref[:lines, :]
    tail = slice(lines, lines + own_rows)
    weight_ref[...] = (row_ref[tail, :] + row_got_ref[tail, :])[:, :index_heads]


def body(query_main, key_codes, key_scales, index_keys, index_query, index_weight, query_pos):
    own_rows, head_count, latent_width = query_main.shape
    index_heads, index_width = index_query.shape[1:]
    own_keys = key_codes.shape[0]
    count = lax.axis_size("ctx")
    row_parts = 4
    key_parts = count // row_parts
    key_total = own_keys * count
    rows = own_rows * row_parts
    lines = own_rows * index_heads
    tall = lines + 8
    struct = jax.ShapeDtypeStruct

    codes = key_codes.T
    groups = key_scales.shape[1]
    main_raw = jnp.transpose(query_main, (0, 2, 1))
    sources = (
        key_scales.T,
        index_keys,
        index_weight,
        query_pos,
        main_raw,
        index_query.reshape(lines, index_width),
        codes,
    )
    key_pack, index_own, main_own, codes_own = pl.pallas_call(
        pack_kernel,
        out_shape=(
            struct((own_keys + 16, own_keys), bf16),
            struct((lines + 16, index_width), bf16),
            struct(main_raw.shape, bf16),
            struct(codes.shape, bf16),
        ),
        in_specs=[pl.BlockSpec(memory_space=pltpu.HBM)] * len(sources),
        scratch_shapes=[
            pltpu.VMEM((groups, own_keys), jnp.int32),
            pltpu.VMEM((own_rows, index_heads), f32),
            pltpu.SMEM((own_rows,), jnp.int32),
            pltpu.SemaphoreType.DMA((len(sources),)),
        ],
        compiler_params=pltpu.CompilerParams(vmem_limit_bytes=8 << 20),
        name="pack",
    )(*(pltpu.with_memory_space_constraint(x, pltpu.HBM) for x in sources))
    codes = swap_gather(codes, row_parts, key_parts, count)
    codes[0] = codes_own
    blocks = swap_gather(key_pack, row_parts, key_parts, count)
    queries = swap_gather(main_raw, 1, row_parts, count)
    queries[0] = main_own
    iqueries = swap_gather(index_own, 1, row_parts, count)

    step = 4
    if key_parts <= step:
        pieces = [list(range(key_parts - 1)), [key_parts - 1]]
    else:
        pieces = [list(range(k, k + step)) for k in range(0, key_parts, step)]
    (main_early,) = kernel_call(
        lay_kernel, (struct(((rows - own_rows) * head_count, latent_width), bf16),), queries[:-1]
    )
    exps, indexes, sums, laid = [], [], None, None
    for n, piece in enumerate(pieces):
        wide = len(piece) * own_keys
        shapes = (
            struct((rows, head_count, wide), f32),
            struct((rows, wide), f32),
            struct((row_parts, 2 * own_rows, head_count), f32),
        )
        if n == 0:
            shapes += (
                struct((own_rows * head_count, latent_width), bf16),
                struct((rows * index_heads, index_width), bf16),
                struct((index_heads, rows), f32),
                struct((rows, LANES), f32),
            )
        out = kernel_call(
            functools.partial(score_kernel, tuple(piece), row_parts, groups, n == 0),
            shapes,
            (
                *(laid or (main_early, queries[-1], *iqueries)),
                *(codes[k] for k in piece),
                *(blocks[k] for k in piece),
            ),
            scratch=(pltpu.VMEM((rows, LANES), f32),) if n == 0 else (),
            flops=2 * rows * head_count * latent_width * wide,
        )
        laid = laid or (main_early, *out[3:])
        exps.append(out[0])
        indexes.append(out[1])
        sums = out[2] if sums is None else sums + out[2]

    sums = [sums]
    for mask in (2, 3, 1):
        sums.append(swap(sums[0], mask, count))
    sums = [sums[0], sums[3], sums[1], sums[2]]

    place = {k: (n, p * own_keys) for n, piece in enumerate(pieces) for p, k in enumerate(piece)}
    teams = [list(range(key_parts))] if key_parts <= step else pieces
    found, keep, send = {}, None, None
    for ids in teams:
        half = len(ids) // 2
        more = struct((rows * index_heads, half * own_keys), bf16)
        wide = struct(more.shape, f32)
        grads_flops = 4 * rows * index_heads * index_width * half * own_keys
        heads, masked = kernel_call(
            prepare_kernel,
            (wide, wide),
            (*laid[2:4], *(blocks[k] for k in ids[1::2])),
            flops=grads_flops,
        )
        early = None
        for part in (1, 0):
            mine = ids[part::2]
            used = sorted({place[k][0] for k in mine})
            places = tuple((used.index(place[k][0]), place[k][1]) for k in mine)
            stored = (*(exps[n] for n in used), *(indexes[n] for n in used))
            shapes = (struct((own_keys, index_width), bf16 if part else f32),) * half
            scratch = (pltpu.VMEM((rows, head_count), f32),)
            if part:
                kernel = first_grad_kernel
                operands = (*sums, laid[2], masked, *stored)
                shapes += (more, struct((rows, half * own_keys), f32))
            else:
                kernel = grad_kernel
                operands = (*sums, *laid[2:4], *stored, *(blocks[k] for k in mine))
                operands += (*early, heads, *(blocks[k] for k in ids[1::2]))
                shapes += (struct((row_parts // 2, tall, index_width), f32),) * 2
                scratch = (pltpu.VMEM(more.shape, bf16), *scratch)
            out = kernel_call(
                functools.partial(kernel, key_total, row_parts, places),
                shapes,
                operands,
                scratch=scratch,
                flops=grads_flops,
            )
            found.update(zip(mine, out))
            if part:
                early = out[half:]
            else:
                keep = out[-2] if keep is None else keep + out[-2]
                send = out[-1] if send is None else send + out[-1]

    def pick(n):
        return found[n] if len(teams) == 1 else jnp.stack([found[k] for k in range(n, key_parts, 4)])

    key_got = swap(pick(3), row_parts, count)
    near_got = swap(pick(1), row_parts, count)
    row_got = swap(send, row_parts // 2, count)
    key_sum = (pick(2) + key_got.astype(f32)).astype(bf16)
    key_got = swap(key_sum, 2 * row_parts, count)
    key_sums = (pick(0), near_got, key_got)
    bit = 4
    while bit < key_parts:
        key_sum = sum(x.astype(f32) for x in key_sums)
        key_got = swap(key_sum[1::2].astype(bf16), row_parts * bit, count)
        key_sums = (key_sum[0::2], key_got)
        bit *= 2
    if len(teams) > 1:
        key_sums = tuple(x[0] for x in key_sums)
    row_sum = keep + row_got
    row_got = swap(row_sum[1], 1, count)
    grad_query, grad_weight, key_grad = kernel_call(
        functools.partial(finish_kernel, len(key_sums)),
        (
            struct((lines, index_width), f32),
            struct((own_rows, index_heads), f32),
            struct((own_keys, index_width), f32),
        ),
        (*key_sums, row_sum[0], row_got),
    )
    return grad_query.reshape(own_rows, index_heads, index_width), grad_weight, key_grad


def solution(mesh):
    placed = (
        P(("grp", "ctx"), None, None),
        P(("grp", "ctx"), None),
        P(("grp", "ctx"), None),
        P(("grp", "ctx"), None),
        P(("grp", "ctx"), None, None),
        P(("grp", "ctx"), None),
        P(("grp", "ctx")),
    )

    return jax.shard_map(
        body,
        mesh=mesh,
        in_specs=placed,
        out_specs=(P(("grp", "ctx"), None, None), P(("grp", "ctx"), None), P(("grp", "ctx"), None)),
        check_vma=False,
    )
```

```python
import functools

import jax
import jax.numpy as jnp
from jax import lax
from jax.experimental import pallas as pl
from jax.experimental.pallas import tpu as pltpu
from jax.sharding import PartitionSpec as P


ROPE = 64
LANES = 128

f32, bf16 = jnp.float32, jnp.bfloat16
main_scale = 192.0 ** (-0.5)


def kernel_call(kernel, shapes, operands, scratch=(), flops=0):
    nbytes = sum(x.size * x.dtype.itemsize for x in (*operands, *shapes))
    return pl.pallas_call(
        kernel,
        out_shape=tuple(shapes),
        scratch_shapes=list(scratch),
        compiler_params=pltpu.CompilerParams(vmem_limit_bytes=24 << 20),
        cost_estimate=pl.CostEstimate(flops=flops, bytes_accessed=nbytes, transcendentals=0),
    )(*operands)


def contract(left, right, dims):
    return lax.dot_general(left, right, ((dims[:1], dims[1:]), ((), ())), preferred_element_type=f32)


def swap(array, mask, count):
    return lax.ppermute(array, "ctx", [(i, i ^ mask) for i in range(count)])


def swap_gather(block, stride, parts, count):
    held = {0: block}
    bit = parts // 2
    while bit:
        for k, own in list(held.items()):
            held[k ^ bit] = swap(own, stride * bit, count)
        bit //= 2
    return [held[k] for k in range(parts)]


def pack_kernel(
    scales_hbm, keys_hbm, weight_hbm, pos_hbm, main_hbm, query_hbm, codes_hbm, out_ref, query_ref,
    main_ref, codes_ref, scales_ref, weight_ref, pos_ref, sems
):
    groups, own_keys = scales_hbm.shape
    key_count = keys_hbm.shape[0]
    lines = query_hbm.shape[0]
    pairs = (
        (scales_hbm, scales_ref),
        (weight_hbm, weight_ref),
        (pos_hbm, pos_ref),
        (keys_hbm, out_ref.at[pl.ds(0, key_count), :]),
        (query_hbm, query_ref.at[pl.ds(0, lines), :]),
        (main_hbm, main_ref),
        (codes_hbm, codes_ref),
    )
    copies = [pltpu.make_async_copy(a, b, sems.at[n]) for n, (a, b) in enumerate(pairs)]
    for copy in copies:
        copy.start()
    for copy in copies[:3]:
        copy.wait()
    factors = jnp.exp2(scales_ref[...].astype(f32))
    spare = out_ref.shape[0] - key_count - groups
    factors = jnp.concatenate([factors, jnp.zeros((spare, own_keys), f32)], axis=0)
    out_ref[key_count:, :] = factors.astype(bf16)
    own_rows, index_heads = weight_ref.shape
    rest = jnp.concatenate([weight_ref[...], jnp.zeros((own_rows, LANES - index_heads), f32)], axis=1)
    lane = lax.broadcasted_iota(jnp.int32, (1, LANES), 1)
    tail = []
    for part in range(3):
        piece = rest.astype(bf16).astype(f32)
        rest = rest - piece
        for i in range(own_rows):
            pos = jnp.full((1, LANES), pos_ref[i], jnp.int32)
            at = ((pos // LANES) * LANES, pos % LANES, jnp.zeros_like(pos))[part].astype(f32)
            tail.append(jnp.where(lane == index_heads, at, piece[i : i + 1, :]))
    tail.append(jnp.zeros((query_ref.shape[0] - lines - len(tail), LANES), f32))
    query_ref[lines:, :] = jnp.concatenate(tail, axis=0).astype(bf16)
    for copy in copies[3:]:
        copy.wait()


def latent_of(codes_ref, keys_ref, groups):
    latent_width, own_keys = codes_ref.shape
    group_width = (latent_width - ROPE) // groups
    factors = keys_ref[own_keys:, :].astype(f32)
    latent = [
        (codes_ref[g * group_width : (g + 1) * group_width, :].astype(f32) * factors[g : g + 1, :]).astype(bf16)
        for g in range(groups)
    ]
    return jnp.concatenate([*latent, codes_ref[groups * group_width :, :]], axis=0)


def score_kernel(offsets, row_parts, groups, first, *refs):
    parts = len(offsets)
    if first:
        queries, iqueries = refs[:row_parts], refs[row_parts : 2 * row_parts]
        refs = refs[2 * row_parts :]
        codes, blocks, refs = refs[:parts], refs[parts : 2 * parts], refs[2 * parts :]
        exp_ref, index_ref, sums_ref, main_ref, flat_ref, column_ref, pos_ref, side_ref = refs
        own_rows, head_count = queries[0].shape[0], queries[0].shape[2]
        lines = flat_ref.shape[0] // row_parts
        index_heads = lines // own_rows
        for r in range(row_parts):
            tail = iqueries[r][lines:, :].astype(f32)
            side = tail[:own_rows] + tail[own_rows : 2 * own_rows]
            side = side + tail[2 * own_rows : 3 * own_rows]
            side_ref[r * own_rows : (r + 1) * own_rows, :] = side
            flat_ref[r * lines : (r + 1) * lines, :] = iqueries[r][:lines, :]
            for i in range(own_rows):
                t = r * own_rows + i
                main_ref[t * head_count : (t + 1) * head_count, :] = jnp.transpose(queries[r][i])
        side = side_ref[...]
        columns = jnp.transpose(side)
        column_ref[...] = columns[:index_heads, :]
        pos_ref[...] = jnp.broadcast_to(side[:, index_heads : index_heads + 1], pos_ref.shape)
    else:
        main_ref, flat_ref, column_ref, pos_ref = refs[:4]
        codes, blocks = refs[4 : 4 + parts], refs[4 + parts : 4 + 2 * parts]
        exp_ref, index_ref, sums_ref = refs[4 + 2 * parts :]
    rows = pos_ref.shape[0]
    own_rows = rows // row_parts
    index_heads = column_ref.shape[0]
    index_width = flat_ref.shape[1]
    head_count = main_ref.shape[0] // rows
    own_keys = blocks[0].shape[1]
    index_scale = float(index_heads * index_width) ** (-0.5)
    me = lax.axis_index("ctx")
    iota = lax.broadcasted_iota(jnp.int32, (1, own_keys), 1)
    key_pos = [((me ^ (row_parts * k)) * own_keys + iota).astype(f32) for k in offsets]
    key_pos = jnp.concatenate(key_pos, axis=1)
    latent = jnp.concatenate([latent_of(c, b, groups) for c, b in zip(codes, blocks)], axis=1)
    ikeys = jnp.concatenate([b[:own_keys, :] for b in blocks], axis=0)
    dots = contract(flat_ref[...], ikeys, (1, 1))
    scores = contract(main_ref[...], latent, (1, 0))
    sums_ref[...] = jnp.zeros_like(sums_ref)
    for t in range(rows):
        r, i = divmod(t, own_rows)
        visible = key_pos <= pos_ref[t : t + 1, :1]
        heads = jnp.maximum(dots[t * index_heads : (t + 1) * index_heads, :], 0.0)
        score = jnp.sum(column_ref[:, t : t + 1] * heads, axis=0, keepdims=True)
        index_exp = jnp.where(visible, jnp.exp(index_scale * score), 0.0)
        index_ref[t : t + 1, :] = index_exp
        score = scores[t * head_count : (t + 1) * head_count, :] * main_scale
        main_exp = jnp.where(visible, jnp.exp(score), 0.0)
        exp_ref[t] = main_exp
        total = main_exp[:, :own_keys]
        for k in range(1, parts):
            total = total + main_exp[:, k * own_keys : (k + 1) * own_keys]
        sums_ref[r, i : i + 1, :] = jnp.sum(jnp.transpose(total), axis=0, keepdims=True)
        index_total = jnp.sum(index_exp, axis=1, keepdims=True)
        sums_ref[r, own_rows + i : own_rows + i + 1, :] = jnp.broadcast_to(
            index_total, (1, head_count)
        )


def prepare_kernel(flat_ref, column_ref, *refs):
    blocks, (heads_ref, masked_ref) = refs[:-2], refs[-2:]
    index_heads, rows = column_ref.shape
    own_keys = heads_ref.shape[1] // len(blocks)
    index_scale = float(index_heads * flat_ref.shape[1]) ** (-0.5)
    ikeys = jnp.concatenate([b[:own_keys, :] for b in blocks], axis=0)
    dots = contract(flat_ref[...], ikeys, (1, 1))
    heads_ref[...] = jnp.maximum(dots, 0.0)
    for t in range(rows):
        lines = slice(t * index_heads, (t + 1) * index_heads)
        weight = index_scale * column_ref[:, t : t + 1]
        masked_ref[lines, :] = jnp.where(dots[lines, :] > 0, weight, 0.0)


def gradient_of(key_total, row_parts, places, sums, total_ref, exps, indexes, own_keys):
    rows, head_count = total_ref.shape
    own_rows = rows // row_parts
    for r in range(row_parts):
        lines = slice(0, own_rows)
        total_ref[r * own_rows : (r + 1) * own_rows, :] = sum(
            s[r ^ m, lines, :] for m, s in enumerate(sums)
        )
    shares = jnp.transpose(1.0 / total_ref[...])
    gradients = []
    for t in range(rows):
        r, i = divmod(t, own_rows)
        share = shares[:, t : t + 1]
        at = own_rows + i
        index_total = sum(s[r ^ m, at : at + 1, :1] for m, s in enumerate(sums))
        target = jnp.concatenate(
            [
                jnp.sum(exps[n][t, :, p : p + own_keys] * share, axis=0, keepdims=True)
                for n, p in places
            ],
            axis=1,
        )
        index_exp = jnp.concatenate(
            [indexes[n][t : t + 1, p : p + own_keys] for n, p in places], axis=1
        )
        gradients.append(key_total * (index_exp / index_total - target / head_count))
    return gradients


def first_grad_kernel(key_total, row_parts, places, *refs):
    count = 1 + max(n for n, _ in places)
    sums, refs = refs[:row_parts], refs[row_parts - 2 :]
    flat_ref, masked_ref = refs[2:4]
    exps, indexes = refs[4 : 4 + count], refs[4 + count : 4 + 2 * count]
    *key_refs, dots_ref, gradient_ref, total_ref = refs[4 + 2 * count :]
    own_keys = key_refs[0].shape[0]
    gradients = gradient_of(
        key_total, row_parts, places, sums, total_ref, exps, indexes, own_keys
    )
    index_heads = flat_ref.shape[0] // len(gradients)
    for t, gradient in enumerate(gradients):
        lines = slice(t * index_heads, (t + 1) * index_heads)
        gradient_ref[t : t + 1, :] = gradient
        dots_ref[lines, :] = (gradient * masked_ref[lines, :]).astype(bf16)
    key_grad = contract(dots_ref[...], flat_ref[...], (0, 0))
    for k, key_ref in enumerate(key_refs):
        key_ref[...] = key_grad[k * own_keys : (k + 1) * own_keys, :].astype(key_ref.dtype)


def grad_kernel(key_total, row_parts, places, *refs):
    count = 1 + max(n for n, _ in places)
    sums, refs = refs[:row_parts], refs[row_parts - 2 :]
    flat_ref, column_ref = refs[2:4]
    exps, indexes = refs[4 : 4 + count], refs[4 + count : 4 + 2 * count]
    refs = refs[4 + 2 * count :]
    blocks, refs = refs[: len(places)], refs[len(places) :]
    early_dots, early_gradient, early_heads = refs[:3]
    early_blocks, refs = refs[3 : 3 + len(places)], refs[3 + len(places) :]
    *key_refs, keep_ref, send_ref, dots_ref, total_ref = refs
    own_rows = total_ref.shape[0] // row_parts
    index_heads, index_width = column_ref.shape[0], flat_ref.shape[1]
    own_keys = key_refs[0].shape[0]
    index_scale = float(index_heads * index_width) ** (-0.5)
    ikeys = jnp.concatenate([b[:own_keys, :] for b in blocks], axis=0)
    flat = flat_ref[...]
    dots = contract(flat, ikeys, (1, 1))
    gradients = gradient_of(
        key_total, row_parts, places, sums, total_ref, exps, indexes, own_keys
    )
    lane = lax.broadcasted_iota(jnp.int32, (index_heads, LANES), 1)
    columns = jnp.zeros((index_heads, LANES), f32)
    for t, gradient in enumerate(gradients):
        lines = slice(t * index_heads, (t + 1) * index_heads)
        heads = dots[lines, :]
        terms = gradient * jnp.maximum(heads, 0.0)
        terms = terms + early_gradient[t : t + 1, :] * early_heads[lines, :]
        column = index_scale * jnp.sum(terms, axis=1, keepdims=True)
        columns = jnp.where(lane == t, column, columns)
        weight = column_ref[:, t : t + 1]
        grad_dots = jnp.where(heads > 0, index_scale * gradient * weight, 0.0).astype(bf16)
        dots_ref[lines, :] = grad_dots
    grad_dots = dots_ref[...]
    key_grad = contract(grad_dots, flat, (0, 0))
    for k, key_ref in enumerate(key_refs):
        key_ref[...] = key_grad[k * own_keys : (k + 1) * own_keys, :].astype(key_ref.dtype)
    early_keys = jnp.concatenate([b[:own_keys, :] for b in early_blocks], axis=0)
    grad_query = contract(grad_dots, ikeys, (1, 0)) + contract(early_dots[...], early_keys, (1, 0))
    weights = jnp.transpose(jnp.concatenate([columns, jnp.zeros_like(columns)], axis=0)[:LANES])
    lines = own_rows * index_heads
    for r in range(row_parts):
        out, at = (keep_ref, r) if r < row_parts // 2 else (send_ref, r - row_parts // 2)
        out[at, :lines, :] = grad_query[r * lines : (r + 1) * lines, :]
        out[at, lines : lines + own_rows, :] = weights[r * own_rows : (r + 1) * own_rows, :]


def finish_kernel(parts, *refs):
    key_refs, (row_ref, row_got_ref, query_ref, weight_ref, key_out_ref) = refs[:parts], refs[parts:]
    lines = query_ref.shape[0]
    own_rows, index_heads = weight_ref.shape
    key_out_ref[...] = sum(ref[...].astype(f32) for ref in key_refs)
    query_ref[...] = row_ref[:lines, :] + row_got_ref[:lines, :]
    tail = slice(lines, lines + own_rows)
    weight_ref[...] = (row_ref[tail, :] + row_got_ref[tail, :])[:, :index_heads]


def body(query_main, key_codes, key_scales, index_keys, index_query, index_weight, query_pos):
    own_rows, head_count, latent_width = query_main.shape
    index_heads, index_width = index_query.shape[1:]
    own_keys = key_codes.shape[0]
    count = lax.axis_size("ctx")
    row_parts = 4
    key_parts = count // row_parts
    key_total = own_keys * count
    rows = own_rows * row_parts
    lines = own_rows * index_heads
    tall = lines + 8
    struct = jax.ShapeDtypeStruct

    codes = key_codes.T
    groups = key_scales.shape[1]
    main_raw = jnp.transpose(query_main, (0, 2, 1))
    sources = (
        key_scales.T,
        index_keys,
        index_weight,
        query_pos,
        main_raw,
        index_query.reshape(lines, index_width),
        codes,
    )
    key_pack, index_own, main_own, codes_own = pl.pallas_call(
        pack_kernel,
        out_shape=(
            struct((own_keys + 16, own_keys), bf16),
            struct((lines + 16, index_width), bf16),
            struct(main_raw.shape, bf16),
            struct(codes.shape, bf16),
        ),
        in_specs=[pl.BlockSpec(memory_space=pltpu.HBM)] * len(sources),
        scratch_shapes=[
            pltpu.VMEM((groups, own_keys), jnp.int32),
            pltpu.VMEM((own_rows, index_heads), f32),
            pltpu.SMEM((own_rows,), jnp.int32),
            pltpu.SemaphoreType.DMA((len(sources),)),
        ],
        compiler_params=pltpu.CompilerParams(vmem_limit_bytes=8 << 20),
        name="pack",
    )(*(pltpu.with_memory_space_constraint(x, pltpu.HBM) for x in sources))
    codes = swap_gather(codes, row_parts, key_parts, count)
    codes[0] = codes_own
    blocks = swap_gather(key_pack, row_parts, key_parts, count)
    queries = swap_gather(main_raw, 1, row_parts, count)
    queries[0] = main_own
    iqueries = swap_gather(index_own, 1, row_parts, count)

    step = 4
    if key_parts <= step:
        pieces = [list(range(key_parts - 1)), [key_parts - 1]]
    else:
        pieces = [list(range(k, k + step)) for k in range(0, key_parts, step)]
    exps, indexes, sums, laid = [], [], None, None
    for n, piece in enumerate(pieces):
        wide = len(piece) * own_keys
        shapes = (
            struct((rows, head_count, wide), f32),
            struct((rows, wide), f32),
            struct((row_parts, 2 * own_rows, head_count), f32),
        )
        if n == 0:
            shapes += (
                struct((rows * head_count, latent_width), bf16),
                struct((rows * index_heads, index_width), bf16),
                struct((index_heads, rows), f32),
                struct((rows, LANES), f32),
            )
        out = kernel_call(
            functools.partial(score_kernel, tuple(piece), row_parts, groups, n == 0),
            shapes,
            (
                *(laid or (*queries, *iqueries)),
                *(codes[k] for k in piece),
                *(blocks[k] for k in piece),
            ),
            scratch=(pltpu.VMEM((rows, LANES), f32),) if n == 0 else (),
            flops=2 * rows * head_count * latent_width * wide,
        )
        laid = laid or out[3:]
        exps.append(out[0])
        indexes.append(out[1])
        sums = out[2] if sums is None else sums + out[2]

    sums = [sums]
    for mask in (2, 3, 1):
        sums.append(swap(sums[0], mask, count))
    sums = [sums[0], sums[3], sums[1], sums[2]]

    place = {k: (n, p * own_keys) for n, piece in enumerate(pieces) for p, k in enumerate(piece)}
    teams = [list(range(key_parts))] if key_parts <= step else pieces
    found, keep, send = {}, None, None
    for ids in teams:
        half = len(ids) // 2
        more = struct((rows * index_heads, half * own_keys), bf16)
        wide = struct(more.shape, f32)
        grads_flops = 4 * rows * index_heads * index_width * half * own_keys
        heads, masked = kernel_call(
            prepare_kernel,
            (wide, wide),
            (*laid[1:3], *(blocks[k] for k in ids[1::2])),
            flops=grads_flops,
        )
        early = None
        for part in (1, 0):
            mine = ids[part::2]
            used = sorted({place[k][0] for k in mine})
            places = tuple((used.index(place[k][0]), place[k][1]) for k in mine)
            stored = (*(exps[n] for n in used), *(indexes[n] for n in used))
            shapes = (struct((own_keys, index_width), bf16 if part else f32),) * half
            scratch = (pltpu.VMEM((rows, head_count), f32),)
            if part:
                kernel = first_grad_kernel
                operands = (*sums, laid[1], masked, *stored)
                shapes += (more, struct((rows, half * own_keys), f32))
            else:
                kernel = grad_kernel
                operands = (*sums, *laid[1:3], *stored, *(blocks[k] for k in mine))
                operands += (*early, heads, *(blocks[k] for k in ids[1::2]))
                shapes += (struct((row_parts // 2, tall, index_width), f32),) * 2
                scratch = (pltpu.VMEM(more.shape, bf16), *scratch)
            out = kernel_call(
                functools.partial(kernel, key_total, row_parts, places),
                shapes,
                operands,
                scratch=scratch,
                flops=grads_flops,
            )
            found.update(zip(mine, out))
            if part:
                early = out[half:]
            else:
                keep = out[-2] if keep is None else keep + out[-2]
                send = out[-1] if send is None else send + out[-1]

    def pick(n):
        return found[n] if len(teams) == 1 else jnp.stack([found[k] for k in range(n, key_parts, 4)])

    key_got = swap(pick(3), row_parts, count)
    near_got = swap(pick(1), row_parts, count)
    row_got = swap(send, row_parts // 2, count)
    key_sum = (pick(2) + key_got.astype(f32)).astype(bf16)
    key_got = swap(key_sum, 2 * row_parts, count)
    key_sums = (pick(0), near_got, key_got)
    bit = 4
    while bit < key_parts:
        key_sum = sum(x.astype(f32) for x in key_sums)
        key_got = swap(key_sum[1::2].astype(bf16), row_parts * bit, count)
        key_sums = (key_sum[0::2], key_got)
        bit *= 2
    if len(teams) > 1:
        key_sums = tuple(x[0] for x in key_sums)
    row_sum = keep + row_got
    row_got = swap(row_sum[1], 1, count)
    grad_query, grad_weight, key_grad = kernel_call(
        functools.partial(finish_kernel, len(key_sums)),
        (
            struct((lines, index_width), f32),
            struct((own_rows, index_heads), f32),
            struct((own_keys, index_width), f32),
        ),
        (*key_sums, row_sum[0], row_got),
    )
    return grad_query.reshape(own_rows, index_heads, index_width), grad_weight, key_grad


def solution(mesh):
    placed = (
        P(("grp", "ctx"), None, None),
        P(("grp", "ctx"), None),
        P(("grp", "ctx"), None),
        P(("grp", "ctx"), None),
        P(("grp", "ctx"), None, None),
        P(("grp", "ctx"), None),
        P(("grp", "ctx")),
    )

    return jax.shard_map(
        body,
        mesh=mesh,
        in_specs=placed,
        out_specs=(P(("grp", "ctx"), None, None), P(("grp", "ctx"), None), P(("grp", "ctx"), None)),
        check_vma=False,
    )
```
